32 devices in a mesh: ctx: 16 (over z, y, core), head: 2 (over x).
Axes of the slice: x: 2, y: 2, z: 4, core: 2. Of those that a mesh axis runs over, the one named last changes fastest.
Arguments:
- queries: bfloat16 [4096, 512], P('ctx', 'head'), may hold values from -5 to 5
- keys: bfloat16 [4096, 512], P('ctx', 'head'), may hold values from -5 to 5
- values: bfloat16 [4096, 32, 128], P('ctx', 'head'), may hold values from -16 to 16
- win_q: bfloat16 [4096, 32, 128], P('ctx', 'head'), may hold values from -5 to 5
- win_k: bfloat16 [4096, 32, 128], P('ctx', 'head'), may hold values from -5 to 5
- gain: bfloat16 [32, 128], P('head'), may hold values from 0.25 to 1.75
Outputs:
- normed_out: bfloat16 [4096, 32, 128], P('ctx', 'head')
The draws below stay inside these ranges and needn't reach their ends.
All inputs are finite; a program needn't handle non-finite values.
Results may differ from the reference program's by a relative error of at most 0.00065.
The reference program's roundings to bfloat16 on the way (of `weights`) count: a program that leaves them out, or rounds other values in their place, can miss the bound.
Values may be sent and summed in bfloat16 or wider, within the bound.
No kernel may reach another device: no remote copies, remote signals or barrier semaphores. Data moves between devices by JAX's collectives and lax.ppermute only.
A program may use at most 192 MiB of HBM per device.

```python
import math
import jax
import jax.numpy as jnp
from jax import lax

HEADS = 32
DV = 128
DK = 16
FEAT = 273
WINDOW = 64
TOKENS = 4096


def window_pair(key):
    base_q = jnp.clip(jax.random.normal(jax.random.fold_in(key, 11), (TOKENS, HEADS, DV), jnp.float32), -5.0, 5.0)
    base_k = jnp.clip(jax.random.normal(jax.random.fold_in(key, 12), (TOKENS, HEADS, DV), jnp.float32), -5.0, 5.0)
    return (base_q, base_k)


def draw_win_q(key, part):
    return window_pair(key)[0].astype(jnp.bfloat16)


def draw_win_k(key, part):
    return window_pair(key)[1].astype(jnp.bfloat16)


def draw_values(key, part):
    noise = jnp.clip(jax.random.normal(jax.random.fold_in(key, 21), (TOKENS, HEADS, DV), jnp.float32), -5.0, 5.0)
    top_log = 1.4
    level = jax.random.uniform(jax.random.fold_in(key, 22), (HEADS, DV), jnp.float32, -1.5, 1.5)
    jitter = jax.random.uniform(jax.random.fold_in(key, 23), (HEADS,), jnp.float32, 0.0, 1.0)
    head_scale = jnp.exp(top_log * (jnp.arange(HEADS).astype(jnp.float32) + jitter) / HEADS)
    ramp = 0.5 + jnp.arange(TOKENS).astype(jnp.float32) / TOKENS
    drawn = (noise + level[None, :, :] * ramp[:, None, None]) * head_scale[None, :, None]
    return jnp.clip(drawn, -16.0, 16.0).astype(jnp.bfloat16)


def block_scale(key, shape, shards, least, largest):
    def one(axis_at, blocks):
        draws = jax.random.uniform(jax.random.fold_in(jax.random.fold_in(key, 6), axis_at), (blocks,), jnp.float32, least / len(shards), largest / len(shards))
        return jnp.repeat(jnp.exp(draws), shape[axis_at] // blocks).reshape((-1,) + (1,) * (len(shape) - axis_at - 1))

    level = one(*shards[0])
    for cut in shards[1:]:
        level = level * one(*cut)
    return level


def gaussian(rng, shape, scale, bound, split=(), dtype=jnp.bfloat16):
    factor_of = block_scale(rng, shape, split, -0.22, 0.18) if split else 1.0
    result = jax.random.normal(rng, shape, jnp.float32) * scale * factor_of
    return jnp.minimum(jnp.maximum(result, -bound), bound).astype(dtype)


def setup_inputs(seed: int = 0) -> dict:
    arg_keys = jax.random.split(jax.random.key(seed), 7)
    queries = gaussian(arg_keys[0], (TOKENS, HEADS * DK), 1.0, 5.0, ((0, 16), (1, 2)))
    keys = gaussian(arg_keys[1], (TOKENS, HEADS * DK), 1.0, 5.0, ((0, 16), (1, 2)))
    values = draw_values(jax.random.fold_in(arg_keys[6], 71), 0)
    win_q = draw_win_q(jax.random.fold_in(arg_keys[6], 71), 0)
    win_k = draw_win_k(jax.random.fold_in(arg_keys[6], 71), 0)
    gain = jnp.clip(1.0 + 0.15 * jax.random.normal(arg_keys[5], (HEADS, DV), jnp.float32), 0.25, 1.75).astype(jnp.bfloat16)
    return dict(queries=queries, keys=keys, values=values, win_q=win_q, win_k=win_k, gain=gain)


exact_precision = lax.Precision.HIGHEST
norm_epsilon = 1e-06

def features(inputs):
    dim_k = inputs.shape[-1]
    outer_part = (inputs[..., :, None] * inputs[..., None, :]).reshape(inputs.shape[:-1] + (dim_k * dim_k,))
    ones_part = jnp.ones(inputs.shape[:-1] + (1,), jnp.float32)
    return jnp.concatenate([ones_part, inputs * dim_k ** (-0.25), outer_part / math.sqrt(2.0 * dim_k)], axis=-1)

def linear_head(operands):
    query_rows, key_rows, value_rows = operands
    span_rows = 64
    piece_count = TOKENS // span_rows
    query_features = features(query_rows.astype(jnp.float32)).reshape(piece_count, span_rows, FEAT)
    key_features = features(key_rows.astype(jnp.float32)).reshape(piece_count, span_rows, FEAT)
    vals_all = value_rows.astype(jnp.float32).reshape(piece_count, span_rows, DV)
    lower_triangle = jnp.tril(jnp.ones((span_rows, span_rows), jnp.float32))

    def advance(carry, inputs):
        state, totals = carry
        query_part, key_part, value_part = inputs
        kernel = jnp.dot(query_part, key_part.T, precision=exact_precision) * lower_triangle
        numer = jnp.dot(kernel, value_part, precision=exact_precision) + jnp.dot(query_part, state, precision=exact_precision)
        denom = lax.optimization_barrier(jnp.sum(kernel, axis=1)) + jnp.dot(query_part, totals, precision=exact_precision)
        state = state + jnp.dot(key_part.T, value_part, precision=exact_precision)
        totals = totals + lax.optimization_barrier(jnp.sum(key_part, axis=0))
        return ((state, totals), numer / denom[:, None])
    start_carry = (jnp.zeros((FEAT, DV), jnp.float32), jnp.zeros((FEAT,), jnp.float32))
    final_carry, results = lax.scan(advance, start_carry, (query_features, key_features, vals_all))
    return results.reshape(TOKENS, DV)

def reference(queries, keys, values, win_q, win_k, gain):
    query_heads = queries.reshape(TOKENS, HEADS, DK).transpose(1, 0, 2)
    key_heads = keys.reshape(TOKENS, HEADS, DK).transpose(1, 0, 2)
    value_heads = values.transpose(1, 0, 2)
    linear = lax.map(linear_head, (query_heads, key_heads, value_heads)).transpose(1, 0, 2)
    ext_keys = jnp.concatenate([jnp.zeros((WINDOW, HEADS, DV), jnp.bfloat16), win_k], axis=0)
    ext_vals = jnp.concatenate([jnp.zeros((WINDOW, HEADS, DV), jnp.bfloat16), values], axis=0)
    query_span = 64
    row_idx = jnp.arange(query_span)[:, None]
    col_idx = jnp.arange(query_span + WINDOW)[None, :]

    def one_span(first_row):
        query_part = lax.dynamic_slice_in_dim(win_q, first_row, query_span, 0).astype(jnp.float32)
        key_part = lax.dynamic_slice_in_dim(ext_keys, first_row, query_span + WINDOW, 0).astype(jnp.float32)
        value_part = lax.dynamic_slice_in_dim(ext_vals, first_row, query_span + WINDOW, 0).astype(jnp.float32)
        scores = jnp.einsum('qhd,khd->hqk', query_part, key_part, precision=exact_precision) / math.sqrt(DV)
        valid = (col_idx > row_idx) & (col_idx <= row_idx + WINDOW) & (first_row + col_idx - WINDOW >= 0)
        scores = jnp.where(valid[None], scores, jnp.float32(-1e+30))
        peak = lax.optimization_barrier(jnp.max(scores, axis=-1, keepdims=True))
        expo = jnp.exp(scores - peak)
        weights = (expo / lax.optimization_barrier(jnp.sum(expo, axis=-1, keepdims=True))).astype(jnp.bfloat16)
        weights = lax.optimization_barrier(weights).astype(jnp.float32)
        return jnp.einsum('hqk,khd->qhd', weights, value_part, precision=exact_precision)
    starts_list = (jnp.arange(TOKENS // query_span) * query_span).astype(jnp.int32)
    window = lax.map(one_span, starts_list).reshape(TOKENS, HEADS, DV)
    mixed = linear + window
    mean_square = lax.optimization_barrier(jnp.mean(mixed * mixed, axis=(1, 2)))
    scaled = mixed * lax.rsqrt(mean_square + norm_epsilon)[:, None, None] * gain.astype(jnp.float32)[None]
    return scaled.astype(jnp.bfloat16)
```

```python
import functools
import math

import jax
import jax.numpy as jnp
import numpy as np
from jax import lax
from jax.experimental import pallas as pl
from jax.experimental.pallas import tpu as pltpu
from jax.sharding import PartitionSpec as P

HEADS = 32
DV = 128
DK = 16
WINDOW = 64
NORM_EPS = 1e-06

ROWS = 160
TOTAL_ROW = 33
WIDE = 40

F32 = jnp.float32
BF16 = jnp.bfloat16
NN = (((1,), (0,)), ((), ()))
NT = (((1,), (1,)), ((), ()))


def pair_tables():
    first = np.zeros((DK, ROWS), np.float32)
    second = np.zeros((DK, ROWS), np.float32)
    add = np.zeros((8, ROWS), np.float32)
    for i in range(DK):
        first[i, i] = 1.0 / 32.0
        second[i, i] = 1.0
        first[i, DK + i] = 0.25
        add[1, DK + i] = 1.0
        for d in range(1, 8):
            row = WIDE + DK * (d - 1) + i
            first[i, row] = 1.0 / 16.0
            second[(i + d) % DK, row] = 1.0
    for i in range(8):
        first[i, 152 + i] = 1.0 / 16.0
        second[i + 8, 152 + i] = 1.0
    add[0, 2 * DK] = 1.0
    add[1, 2 * DK] = 1.0
    return first, second, add


def dot(a, b, dims=NN):
    return lax.dot_general(a, b, dims, preferred_element_type=F32)


def split(x):
    high = x.astype(BF16)
    return high, (x - high.astype(F32)).astype(BF16)


def quarter(place_ref, r):
    low, mid = place_ref[0], place_ref[1]
    half = jnp.where(r >= 2, 1 - low, low)
    part = jnp.where(r % 2 == 1, 1 - mid, mid)
    return half * 2 + part


def state_kernel(place_ref, kt_ref, v_ref, out_ref):
    heads, toks = v_ref.shape[1], v_ref.shape[2]
    ones = jnp.where(lax.broadcasted_iota(jnp.int32, (8, toks), 0) == 0, 1.0, 0.0)
    ones = ones.astype(F32)
    all_ones = jnp.ones((8, toks), BF16)
    for j in range(heads):
        x = kt_ref[0, j * DK : (j + 1) * DK, :].astype(F32)
        parts = [x * x, x, ones]
        for d in range(1, 8):
            parts.append(x * pltpu.roll(x, DK - d, 0))
        parts.append(x[:8] * x[8:])
        high, low = split(jnp.concatenate(parts, axis=0))
        v = v_ref[0, j]
        out_ref[0, j] = dot(high, v) + dot(low, v)
        total = dot(all_ones, high, NT) + dot(all_ones, low, NT)
        out_ref[0, j, TOTAL_ROW : TOTAL_ROW + 1, :] = total[:1, :128]
        out_ref[0, j, TOTAL_ROW + 1 : TOTAL_ROW + 2, : ROWS - 128] = total[:1, 128:]


def states(place, keys_t, values_h):
    quarters, heads, toks, dim = values_h.shape
    return pl.pallas_call(
        state_kernel,
        out_shape=jax.ShapeDtypeStruct((quarters, heads, ROWS, dim), F32),
        grid_spec=pltpu.PrefetchScalarGridSpec(
            num_scalar_prefetch=1,
            grid=(quarters,),
            in_specs=[
                pl.BlockSpec((1, heads * DK, toks), lambda r, p: (quarter(p, r), 0, 0)),
                pl.BlockSpec((1, heads, toks, dim), lambda r, p: (quarter(p, r), 0, 0, 0)),
            ],
            out_specs=pl.BlockSpec((1, heads, ROWS, dim), lambda r, p: (r, 0, 0, 0)),
        ),
        name="states",
    )(place, keys_t, values_h)


def local_kernel(first_ref, q_ref, k_ref, v_ref, wq_ref, wk_ref, rk_ref, rv_ref,
                 num_ref, den_ref, win_ref):
    heads, toks, dim = v_ref.shape[1], v_ref.shape[2], v_ref.shape[3]
    half = toks // 2
    first = first_ref[0]
    row = lax.broadcasted_iota(jnp.int32, (half, half), 0)
    col = lax.broadcasted_iota(jnp.int32, (half, half), 1)
    tri = col <= row
    wrow = lax.broadcasted_iota(jnp.int32, (WINDOW, 2 * WINDOW), 0)
    wcol = lax.broadcasted_iota(jnp.int32, (WINDOW, 2 * WINDOW), 1)
    band = (wcol > wrow) & (wcol <= wrow + WINDOW)
    edge = band & ((wcol >= WINDOW) | (first == 0))
    den_ref[...] = jnp.zeros_like(den_ref)
    for j in range(heads):
        q = q_ref[0, :, j * DK : (j + 1) * DK]
        k = k_ref[0, :, j * DK : (j + 1) * DK]
        v = v_ref[0, j]
        for b in range(2):
            lo = b * half
            s = dot(q[lo : lo + half], k[: lo + half], NT)
            kern = 1.0 + s * 0.25 + s * s * (1.0 / 32.0)
            if b == 0:
                kern = jnp.where(tri, kern, 0.0)
            else:
                kern = jnp.concatenate(
                    [kern[:, :half], jnp.where(tri, kern[:, half:], 0.0)], axis=1
                )
            high, low = split(kern)
            num_ref[0, j, lo : lo + half, :] = dot(high, v[: lo + half]) + dot(low, v[: lo + half])
            den_ref[0, lo : lo + half, j : j + 1] = jnp.sum(kern, axis=1, keepdims=True)
        for b in range(toks // WINDOW):
            lo = b * WINDOW
            if b == 0:
                kk = jnp.concatenate([rk_ref[0, j], wk_ref[0, j, :WINDOW]], axis=0)
                vv = jnp.concatenate([rv_ref[0, j], v[:WINDOW]], axis=0)
                valid = edge
            else:
                kk = wk_ref[0, j, lo - WINDOW : lo + WINDOW]
                vv = v[lo - WINDOW : lo + WINDOW]
                valid = band
            sc = dot(wq_ref[0, j, lo : lo + WINDOW], kk, NT) / math.sqrt(dim)
            sc = jnp.where(valid, sc, -1e30)
            expo = jnp.exp(sc - jnp.max(sc, axis=1, keepdims=True))
            weights = (expo / jnp.sum(expo, axis=1, keepdims=True)).astype(BF16)
            win_ref[0, j, lo : lo + WINDOW, :] = dot(weights, vv)


def local(first, q4, k4, values_h, wq_h, wk_h, rim_k, rim_v):
    quarters, heads, toks, dim = values_h.shape
    full = pl.BlockSpec((1, heads, toks, dim), lambda r, p: (r, 0, 0, 0))
    rim = pl.BlockSpec((1, heads, WINDOW, dim), lambda r, p: (r, 0, 0, 0))
    narrow = pl.BlockSpec((1, toks, heads * DK), lambda r, p: (r, 0, 0))
    return pl.pallas_call(
        local_kernel,
        out_shape=(
            jax.ShapeDtypeStruct((quarters, heads, toks, dim), F32),
            jax.ShapeDtypeStruct((quarters, toks, 128), F32),
            jax.ShapeDtypeStruct((quarters, heads, toks, dim), F32),
        ),
        grid_spec=pltpu.PrefetchScalarGridSpec(
            num_scalar_prefetch=1,
            grid=(quarters,),
            in_specs=[narrow, narrow, full, full, full, rim, rim],
            out_specs=(full, pl.BlockSpec((1, toks, 128), lambda r, p: (r, 0, 0)), full),
        ),
        name="local",
    )(first, q4, k4, values_h, wq_h, wk_h, rim_k, rim_v)


def final_kernel(place_ref, q_ref, prior_ref, num_ref, den_ref, win_ref, e1_ref, e2_ref, add_ref,
                 mixed_ref, sq_ref, acc_ref):
    heads, toks, dim = num_ref.shape[1], num_ref.shape[2], num_ref.shape[3]
    r = pl.program_id(0)
    squares = jnp.zeros((toks, dim), F32)
    for j in range(heads):
        q = q_ref[0, :, j * DK : (j + 1) * DK]
        phi = (dot(q, e1_ref[...]) + add_ref[0:1]) * (dot(q, e2_ref[...]) + add_ref[1:2])
        phi_high, phi_low = split(phi)
        prior = prior_ref[0, j]
        high, low = split(prior)
        both = dot(phi_high, jnp.concatenate([high, low], axis=1))
        numer = num_ref[0, j] + ((both[:, dim:] + dot(phi_low, high)) + both[:, :dim])
        t0 = prior[TOTAL_ROW : TOTAL_ROW + 1, :]
        t1 = prior[TOTAL_ROW + 1 : TOTAL_ROW + 2, : ROWS - 128]
        denom = den_ref[0, :, j : j + 1] + (
            jnp.sum(phi[:, :128] * t0, axis=1, keepdims=True)
            + jnp.sum(phi[:, 128:] * t1, axis=1, keepdims=True)
        )
        mixed = numer / denom + win_ref[0, j]
        mixed_ref[0, j] = mixed
        squares = squares + mixed * mixed

    @pl.when(r == 0)
    def _():
        acc_ref[...] = squares

    @pl.when(r > 0)
    def _():
        acc_ref[...] += squares

    @pl.when(r == pl.num_programs(0) - 1)
    def _():
        sq_ref[...] = lax.dot_general(
            jnp.ones((8, dim), F32), acc_ref[...], NT,
            precision=lax.Precision.HIGHEST, preferred_element_type=F32,
        )


def final(place, q4, prior, num, den, win):
    quarters, heads, toks, dim = num.shape
    first, second, add = pair_tables()
    own = pl.BlockSpec((1, heads, toks, dim), lambda r, p: (quarter(p, r), 0, 0, 0))
    table = pl.BlockSpec((DK, ROWS), lambda r, p: (0, 0))
    return pl.pallas_call(
        final_kernel,
        out_shape=(
            jax.ShapeDtypeStruct((quarters, heads, toks, dim), F32),
            jax.ShapeDtypeStruct((8, toks), F32),
        ),
        grid_spec=pltpu.PrefetchScalarGridSpec(
            num_scalar_prefetch=1,
            grid=(quarters,),
            in_specs=[
                pl.BlockSpec((1, toks, heads * DK), lambda r, p: (quarter(p, r), 0, 0)),
                pl.BlockSpec((1, heads, ROWS, dim), lambda r, p: (r, 0, 0, 0)),
                own,
                pl.BlockSpec((1, toks, 128), lambda r, p: (quarter(p, r), 0, 0)),
                own,
                table,
                table,
                pl.BlockSpec((8, ROWS), lambda r, p: (0, 0)),
            ],
            out_specs=(own, pl.BlockSpec((8, toks), lambda r, p: (0, 0))),
            scratch_shapes=[pltpu.VMEM((toks, dim), F32)],
        ),
        name="final",
    )(place, q4, prior, num, den, win, jnp.asarray(first, BF16), jnp.asarray(second, BF16),
      jnp.asarray(add, F32))


def norm_kernel(mixed_ref, sq_ref, gain_ref, out_ref, turn_ref):
    heads, toks, dim = mixed_ref.shape
    scale = lax.rsqrt(sq_ref[...] / (HEADS * DV) + NORM_EPS)
    column = jnp.transpose(scale, (1, 0))[:, :1]
    for h in range(heads):
        turn_ref[:, h, :] = mixed_ref[h] * column * gain_ref[h : h + 1, :].astype(F32)
    out_ref[...] = turn_ref[...].astype(BF16)


def norm(mixed, squares, gain):
    heads, toks, dim = mixed.shape
    block = 128
    return pl.pallas_call(
        norm_kernel,
        out_shape=jax.ShapeDtypeStruct((toks, heads, dim), BF16),
        grid=(toks // block,),
        in_specs=[
            pl.BlockSpec((heads, block, dim), lambda i: (0, i, 0)),
            pl.BlockSpec((8, block), lambda i: (0, i)),
            pl.BlockSpec((heads, dim), lambda i: (0, 0)),
        ],
        out_specs=pl.BlockSpec((block, heads, dim), lambda i: (i, 0, 0)),
        scratch_shapes=[pltpu.VMEM((block, heads, dim), F32)],
        name="norm",
    )(mixed, squares, gain)


def exclusive_scan(own, count, low, mid):
    def permute(x, pairs):
        return lax.ppermute(x, "ctx", pairs)

    core_swap = [(i, i ^ 1) for i in range(count)]
    pair_swap = [(i, i ^ 2) for i in range(count)]
    other_core = permute(own[2:], core_swap)
    chip = own[:2] + other_core
    other_chip = permute(chip[1], pair_swap)
    plane = chip[0] + other_chip
    groups = count // 4
    before = jnp.zeros_like(plane)
    inclusive = plane
    step = 1
    while step < groups:
        got = permute(inclusive, [(i, i + 4 * step) for i in range(count - 4 * step)])
        before = got if step == 1 else before + got
        inclusive = inclusive + got
        step *= 2
    mine = before + jnp.where(mid == 1, other_chip, 0.0)
    send = before + jnp.where(mid == 0, chip[0], 0.0)
    half = jnp.stack([mine, permute(send, pair_swap)])
    send = half + jnp.where(low == 0, own[:2], 0.0)
    mine = half + jnp.where(low == 1, other_core, 0.0)
    return jnp.concatenate([mine, permute(send, core_swap)], axis=0)


def on_device(queries, keys, values, win_q, win_k, gain):
    toks, heads, dim = values.shape
    count = lax.axis_size("ctx")
    where = lax.axis_index("ctx")
    low, mid = where % 2, (where // 2) % 2
    place = jnp.stack([low, mid]).astype(jnp.int32)
    part = heads // 4

    rim_pairs = [(i, i + 1) for i in range(count - 1)]
    rim_k = lax.ppermute(win_k[toks - WINDOW :], "ctx", rim_pairs)
    rim_v = lax.ppermute(values[toks - WINDOW :], "ctx", rim_pairs)

    def by_head(x):
        return jnp.transpose(x, (1, 0, 2)).reshape(4, part, x.shape[0], dim)

    values_h = by_head(values)
    own = states(place, keys.T.reshape(4, part * DK, toks), values_h)
    prior = exclusive_scan(own, count, low, mid)

    q4 = jnp.transpose(queries.reshape(toks, 4, part * DK), (1, 0, 2))
    k4 = jnp.transpose(keys.reshape(toks, 4, part * DK), (1, 0, 2))
    first = (where == 0).astype(jnp.int32)[None]
    num, den, win = local(
        first, q4, k4, values_h, by_head(win_q), by_head(win_k), by_head(rim_k), by_head(rim_v)
    )
    mixed, squares = final(place, q4, prior, num, den, win)
    squares = lax.psum(squares[:1], "head")
    squares = jnp.broadcast_to(squares, (8, toks))
    return norm(mixed.reshape(heads, toks, dim), squares, gain)


def solution(mesh):
    return jax.shard_map(
        on_device,
        mesh=mesh,
        in_specs=(
            P("ctx", "head"),
            P("ctx", "head"),
            P("ctx", "head", None),
            P("ctx", "head", None),
            P("ctx", "head", None),
            P("head", None),
        ),
        out_specs=P("ctx", "head", None),
        check_vma=False,
    )
```

```python
import functools
import math

import jax
import jax.numpy as jnp
import numpy as np
from jax import lax
from jax.experimental import pallas as pl
from jax.experimental.pallas import tpu as pltpu
from jax.sharding import PartitionSpec as P

HEADS = 32
DV = 128
DK = 16
WINDOW = 64
NORM_EPS = 1e-06

ROWS = 160
TOTAL_ROW = 33
WIDE = 40
SENT = ROWS + WIDE

F32 = jnp.float32
BF16 = jnp.bfloat16
NN = (((1,), (0,)), ((), ()))
NT = (((1,), (1,)), ((), ()))


def pair_tables(heads):
    first = np.zeros((DK, ROWS), np.float32)
    second = np.zeros((DK, ROWS), np.float32)
    add = np.zeros((8, ROWS), np.float32)
    for i in range(DK):
        first[i, i] = 1.0 / 32.0
        second[i, i] = 1.0
        first[i, DK + i] = 0.25
        add[1, DK + i] = 1.0
        for d in range(1, 8):
            row = WIDE + DK * (d - 1) + i
            first[i, row] = 1.0 / 16.0
            second[(i + d) % DK, row] = 1.0
    for i in range(8):
        first[i, 152 + i] = 1.0 / 16.0
        second[i + 8, 152 + i] = 1.0
    add[0, 2 * DK] = 1.0
    add[1, 2 * DK] = 1.0
    both = []
    for one in (first, second):
        table = np.zeros((heads, heads * DK, ROWS), np.float32)
        for j in range(heads):
            table[j, j * DK : (j + 1) * DK] = one
        both.append(jnp.asarray(table, BF16))
    return both[0], both[1], jnp.asarray(add, F32)


def dot(a, b, dims=NN):
    return lax.dot_general(a, b, dims, preferred_element_type=F32)


def split(x):
    high = x.astype(BF16)
    return high, (x - high.astype(F32)).astype(BF16)


def pack(ref, x):
    high = x.astype(BF16)
    ref[:ROWS] = high
    ref[ROWS:] = (x[:WIDE] - high[:WIDE].astype(F32)).astype(BF16)


def unpack(got):
    wide = got[:WIDE].astype(F32) + got[ROWS:].astype(F32)
    return jnp.concatenate([wide, got[WIDE:ROWS].astype(F32)], axis=0)


def in_vmem(shape, dtype):
    return pltpu.VMEM(shape, dtype)


VMEM_SPEC = pl.BlockSpec(memory_space=pltpu.VMEM)
SMEM_SPEC = pl.BlockSpec(memory_space=pltpu.SMEM)


def call(body, name, outs, *operands, scalars=0, scratch=(), vmem=48 << 20):
    held = [
        x if i < scalars else pltpu.with_memory_space_constraint(x, pltpu.VMEM)
        for i, x in enumerate(operands)
    ]
    many = isinstance(outs, tuple)
    return pl.pallas_call(
        body,
        out_shape=outs,
        in_specs=[SMEM_SPEC] * scalars + [VMEM_SPEC] * (len(operands) - scalars),
        out_specs=tuple(VMEM_SPEC for _ in outs) if many else VMEM_SPEC,
        scratch_shapes=list(scratch),
        compiler_params=pltpu.CompilerParams(vmem_limit_bytes=vmem),
        name=name,
    )(*held)


def one_state(x, v):
    toks = x.shape[1]
    ones = jnp.where(lax.broadcasted_iota(jnp.int32, (8, toks), 0) == 0, 1.0, 0.0).astype(F32)
    parts = [x * x, x, ones]
    for d in range(1, 8):
        parts.append(x * pltpu.roll(x, DK - d, 0))
    parts.append(x[:8] * x[8:])
    high, low = split(jnp.concatenate(parts, axis=0))
    full = jnp.ones((8, toks), BF16)
    total = dot(full, high, NT) + dot(full, low, NT)
    return dot(high, v) + dot(low, v), total


def put_states(out_ref, place_ref, far, kt_ref, vh_ref):
    part = out_ref.shape[1]
    half = place_ref[0] if far == 0 else 1 - place_ref[0]

    def one(r, carry):
        mid = jnp.where(r == 1, 1 - place_ref[1], place_ref[1])
        base = (half * 2 + mid) * part
        for j in range(part):
            x = kt_ref[pl.ds(pl.multiple_of((base + j) * DK, DK), DK), :]
            state, total = one_state(x, vh_ref[base + j])
            out_ref[r, j] = state
            out_ref[r, j, TOTAL_ROW : TOTAL_ROW + 1, :] = total[:1, :128]
            out_ref[r, j, TOTAL_ROW + 1 : TOTAL_ROW + 2, : ROWS - 128] = total[:1, 128:]
        return carry

    lax.fori_loop(0, 2, one, 0)


def far_states_kernel(place_ref, keys_ref, v_ref, out_ref, vh_ref, kt_ref):
    vh_ref[...] = jnp.swapaxes(v_ref[...], 0, 1)
    kt_ref[...] = jnp.transpose(keys_ref[...].astype(F32), (1, 0))
    put_states(out_ref, place_ref, 1, kt_ref, vh_ref)


def near_states_kernel(place_ref, kt_ref, vh_ref, after_ref, out_ref):
    put_states(out_ref, place_ref, 0, kt_ref, vh_ref)


def chip_kernel(own_ref, other_ref, chip_ref, msg_ref):
    for j in range(own_ref.shape[1]):
        far = own_ref[1, j] + other_ref[1, j]
        chip_ref[1, j] = far
        pack(msg_ref.at[j], far)
        chip_ref[0, j] = own_ref[0, j] + other_ref[0, j]


def add_kernel(base_ref, got_ref, *rest):
    sum_ref, msg_ref = rest[-2:]
    for j in range(sum_ref.shape[0]):
        total = base_ref[j] + unpack(got_ref[j])
        sum_ref[j] = total
        pack(msg_ref.at[j], total)


def plane_kernel(chip_ref, got_ref, *rest):
    add_kernel(chip_ref.at[0], got_ref, *rest)


def before_kernel(rounds, place_ref, chip_ref, pair_ref, *rest):
    gots, (mine_ref, msg_ref) = rest[:rounds], rest[-2:]
    mid = place_ref[1]
    for j in range(mine_ref.shape[0]):
        before = unpack(gots[0][j])
        for got in gots[1:]:
            before = before + unpack(got[j])
        mine_ref[j] = before + jnp.where(mid == 1, unpack(pair_ref[j]), 0.0)
        pack(msg_ref.at[j], before + jnp.where(mid == 0, chip_ref[0, j], 0.0))


def half_kernel(place_ref, mine_ref, got_ref, own_ref, other_ref, prior_ref, send_ref):
    low = place_ref[0]
    for r in range(2):
        for j in range(mine_ref.shape[0]):
            half = mine_ref[j] if r == 0 else unpack(got_ref[j])
            send_ref[r, j] = half + jnp.where(low == 0, own_ref[r, j], 0.0)
            prior_ref[r, j] = half + jnp.where(low == 1, other_ref[r, j], 0.0)


def phi_kernel(q_ref, e1_ref, e2_ref, add_ref, after_ref, high_ref, low_ref, q4_ref):
    part = e1_ref.shape[0]
    width = part * DK
    for r in range(4):
        q4_ref[r] = q_ref[:, r * width : (r + 1) * width]

    def one(r, carry):
        q = q4_ref[r]
        for j in range(part):
            a = dot(q, e1_ref[j]) + add_ref[0:1]
            b = dot(q, e2_ref[j]) + add_ref[1:2]
            high, low = split(a * b)
            high_ref[r * part + j] = high
            low_ref[r * part + j] = low
        return carry

    lax.fori_loop(0, 4, one, 0)


def intra_kernel(q_ref, k_ref, vh_ref, after_ref, num_ref, den_ref, q4_ref, k4_ref):
    heads, toks, dim = vh_ref.shape
    part = heads // 4
    width = part * DK
    half = toks // 2
    for r in range(4):
        q4_ref[r] = q_ref[:, r * width : (r + 1) * width]
        k4_ref[r] = k_ref[:, r * width : (r + 1) * width]
    row = lax.broadcasted_iota(jnp.int32, (half, half), 0)
    col = lax.broadcasted_iota(jnp.int32, (half, half), 1)
    tri = col <= row
    lane = lax.broadcasted_iota(jnp.int32, (toks, width), 1) // DK

    def poly(s):
        return 1.0 + s * 0.25 + s * s * (1.0 / 32.0)

    def one(r, carry):
        q, k = q4_ref[r], k4_ref[r]
        tops, lows, rights = [], [], []
        for j in range(part):
            own = jnp.where(lane == j, q, jnp.zeros_like(q))
            tops.append(dot(own[:half], k[:half], NT))
            lows.append(dot(own[half:], k, NT))
        for j in range(part):
            v = vh_ref[r * part + j]
            top = jnp.where(tri, poly(tops[j]), 0.0)
            left = poly(lows[j][:, :half])
            right = jnp.where(tri, poly(lows[j][:, half:]), 0.0)
            high, low = split(top)
            num_ref[r * part + j, :half] = dot(high, v[:half]) + dot(low, v[:half])
            high, low = split(jnp.concatenate([left, right], axis=1))
            num_ref[r * part + j, half:] = dot(high, v) + dot(low, v)
            den_ref[r, :half, j : j + 1] = jnp.sum(top, axis=1, keepdims=True)
            den_ref[r, half:, j : j + 1] = jnp.sum(left + right, axis=1, keepdims=True)
        return carry

    lax.fori_loop(0, 4, one, 0)


def window_kernel(first_ref, wq_ref, wk_ref, vh_ref, rk_ref, rv_ref, after_ref,
                  win_ref, qh_ref, kh_ref, ve_ref):
    heads, toks, dim = vh_ref.shape
    part = heads // 4
    qh_ref[...] = jnp.swapaxes(wq_ref[...], 0, 1)
    kh_ref[:, :WINDOW] = jnp.swapaxes(rk_ref[...], 0, 1)
    kh_ref[:, WINDOW:] = jnp.swapaxes(wk_ref[...], 0, 1)
    ve_ref[:, :WINDOW] = jnp.swapaxes(rv_ref[...], 0, 1)
    ve_ref[:, WINDOW:] = vh_ref[...]
    row = lax.broadcasted_iota(jnp.int32, (WINDOW, 2 * WINDOW), 0)
    col = lax.broadcasted_iota(jnp.int32, (WINDOW, 2 * WINDOW), 1)
    band = (col > row) & (col <= row + WINDOW)
    edge = band & ((col >= WINDOW) | (first_ref[0] == 0))
    blocks = toks // WINDOW

    def one(r, carry):
        scores = []
        for j in range(part):
            head = r * part + j
            for b in range(blocks):
                lo = b * WINDOW
                sc = dot(qh_ref[head, lo : lo + WINDOW], kh_ref[head, lo : lo + 2 * WINDOW], NT)
                scores.append(jnp.where(edge if b == 0 else band, sc / math.sqrt(dim), -1e30))
        sc = jnp.concatenate(scores, axis=0)
        expo = jnp.exp(sc - jnp.max(sc, axis=1, keepdims=True))
        weights = (expo / jnp.sum(expo, axis=1, keepdims=True)).astype(BF16)
        for j in range(part):
            head = r * part + j
            for b in range(blocks):
                lo = b * WINDOW
                at = (j * blocks + b) * WINDOW
                win_ref[head, lo : lo + WINDOW] = dot(
                    weights[at : at + WINDOW], ve_ref[head, lo : lo + 2 * WINDOW]
                )
        return carry

    lax.fori_loop(0, 4, one, 0)


def final_kernel(far, place_ref, prior_ref, high_ref, low_ref, num_ref, den_ref, win_ref, *rest):
    mixed_ref, sq_ref = rest[-2:]
    part = prior_ref.shape[1]
    toks, dim = num_ref.shape[1:]
    half = place_ref[0] if far == 0 else 1 - place_ref[0]
    squares = jnp.zeros((toks, dim), F32)
    for a in range(2):
        r = jnp.where(place_ref[1] == a, 0, 1)
        for j in range(part):
            head = (half * 2 + a) * part + j
            prior = prior_ref[r, j]
            phi_high, phi_low = high_ref[head], low_ref[head]
            high, low = split(prior)
            both = dot(phi_high, jnp.concatenate([high, low], axis=1))
            numer = num_ref[head] + ((both[:, dim:] + dot(phi_low, high)) + both[:, :dim])
            t0 = prior[TOTAL_ROW : TOTAL_ROW + 1, :]
            t1 = prior[TOTAL_ROW + 1 : TOTAL_ROW + 2, : ROWS - 128]
            phi = phi_high.astype(F32) + phi_low.astype(F32)
            denom = den_ref[half * 2 + a, :, j : j + 1] + (
                jnp.sum(phi[:, :128] * t0, axis=1, keepdims=True)
                + jnp.sum(phi[:, 128:] * t1, axis=1, keepdims=True)
            )
            mixed = numer / denom + win_ref[head]
            mixed_ref[:, a * part + j, :] = mixed
            squares = squares + mixed * mixed
    total = lax.dot_general(
        jnp.ones((8, dim), F32), squares, NT,
        precision=lax.Precision.HIGHEST, preferred_element_type=F32,
    )
    sq_ref[...] = total if far == 0 else total + rest[0][...]


def norm_kernel(peers, place_ref, near_ref, far_ref, gain_ref, sq_ref, *rest):
    out_ref = rest[-1]
    half = near_ref.shape[1]
    total = sq_ref[...]
    for got in rest[:peers]:
        total = total + got[...]
    scale = lax.rsqrt(total / (HEADS * DV) + NORM_EPS)
    column = jnp.transpose(scale, (1, 0))[:, :1][:, :, None]
    gain = gain_ref[...].astype(F32)[None]

    def put(left_ref, right_ref):
        left = left_ref[...] * column * gain[:, :half]
        right = right_ref[...] * column * gain[:, half:]
        out_ref[...] = jnp.concatenate([left, right], axis=1).astype(BF16)

    @pl.when(place_ref[0] == 0)
    def _():
        put(near_ref, far_ref)

    @pl.when(place_ref[0] == 1)
    def _():
        put(far_ref, near_ref)


def on_device(queries, keys, values, win_q, win_k, gain):
    toks, heads, dim = values.shape
    count = lax.axis_size("ctx")
    peers = lax.axis_size("head") - 1
    where = lax.axis_index("ctx")
    place = jnp.stack([where & 1, (where >> 1) & 1]).astype(jnp.int32)
    first = (where == 0).astype(jnp.int32)[None]
    part = heads // 4
    core_swap = [(i, i ^ 1) for i in range(count)]
    pair_swap = [(i, i ^ 2) for i in range(count)]
    half_shape = in_vmem((2, part, ROWS, dim), F32)
    quarter_shape = in_vmem((part, ROWS, dim), F32)
    msg_shape = in_vmem((part, SENT, dim), BF16)
    head_wide = in_vmem((heads, toks, dim), F32)

    def permute(x, pairs):
        return lax.ppermute(x, "ctx", pairs)

    rim_pairs = [(i, i + 1) for i in range(count - 1)]
    rim_k = permute(win_k[toks - WINDOW :], rim_pairs)
    rim_v = permute(values[toks - WINDOW :], rim_pairs)

    far_own, values_h, keys_t = call(
        far_states_kernel, "far_states",
        (half_shape, in_vmem((heads, toks, dim), BF16), in_vmem((heads * DK, toks), F32)),
        place, keys, values, scalars=1,
    )
    other = permute(far_own, core_swap)
    own = call(near_states_kernel, "near_states", half_shape,
               place, keys_t, values_h, far_own, scalars=1)
    chip, msg = call(chip_kernel, "chip", (half_shape, msg_shape), own, other)
    pair = permute(msg, pair_swap)
    num, den = call(
        intra_kernel, "intra", (head_wide, in_vmem((4, toks, 128), F32)),
        queries, keys, values_h, msg,
        scratch=[pltpu.VMEM((4, toks, part * DK), BF16)] * 2,
    )
    inclusive, msg = call(plane_kernel, "plane", (quarter_shape, msg_shape), chip, pair, den)

    first_table, second_table, add_table = pair_tables(part)
    gots = []
    step = 1
    phi_high = phi_low = win = None
    while step < count // 4:
        got = permute(msg, [(i, i + 4 * step) for i in range(count - 4 * step)])
        gots.append(got)
        if step == 1:
            phi_high, phi_low = call(
                phi_kernel, "phi", (in_vmem((heads, toks, ROWS), BF16),) * 2,
                queries, first_table, second_table, add_table, msg,
                scratch=[pltpu.VMEM((4, toks, part * DK), BF16)],
            )
        if step == 2:
            win = call(
                window_kernel, "window", head_wide,
                first, win_q, win_k, values_h, rim_k, rim_v, msg, scalars=1,
                scratch=[
                    pltpu.VMEM((heads, toks, dim), BF16),
                    pltpu.VMEM((heads, toks + WINDOW, dim), BF16),
                    pltpu.VMEM((heads, toks + WINDOW, dim), BF16),
                ],
            )
        step *= 2
        if step < count // 4:
            inclusive, msg = call(
                add_kernel, "add", (quarter_shape, msg_shape), inclusive, got, phi_high
            )
    mine, msg = call(
        functools.partial(before_kernel, len(gots)), "before", (quarter_shape, msg_shape),
        place, chip, pair, *gots, win, scalars=1,
    )
    got = permute(msg, pair_swap)
    prior, send = call(half_kernel, "half", (half_shape, half_shape),
                       place, mine, got, own, other, scalars=1)
    far_prior = permute(send, core_swap)

    mixed_shape = in_vmem((toks, heads // 2, dim), F32)
    sq_shape = in_vmem((8, toks), F32)
    near, squares = call(
        functools.partial(final_kernel, 0), "near_final", (mixed_shape, sq_shape),
        place, prior, phi_high, phi_low, num, den, win, send, scalars=1,
    )
    far, squares = call(
        functools.partial(final_kernel, 1), "far_final", (mixed_shape, sq_shape),
        place, far_prior, phi_high, phi_low, num, den, win, squares, scalars=1,
    )
    others = [
        lax.ppermute(squares, "head", [(i, (i + k) % (peers + 1)) for i in range(peers + 1)])
        for k in range(1, peers + 1)
    ]
    return call(
        functools.partial(norm_kernel, peers), "norm",
        jax.ShapeDtypeStruct((toks, heads, dim), BF16),
        place, near, far, gain, squares, *others, scalars=1,
    )


def solution(mesh):
    return jax.shard_map(
        on_device,
        mesh=mesh,
        in_specs=(
            P("ctx", "head"),
            P("ctx", "head"),
            P("ctx", "head", None),
            P("ctx", "head", None),
            P("ctx", "head", None),
            P("head", None),
        ),
        out_specs=P("ctx", "head", None),
        check_vma=False,
    )
```

```python
import functools
import math

import jax
import jax.numpy as jnp
import numpy as np
from jax import lax
from jax.experimental import pallas as pl
from jax.experimental.pallas import tpu as pltpu
from jax.sharding import PartitionSpec as P

HEADS = 32
DV = 128
DK = 16
WINDOW = 64
NORM_EPS = 1e-06

ROWS = 160
TOTAL_ROW = 33
WIDE = 40
SENT = ROWS + WIDE

F32 = jnp.float32
BF16 = jnp.bfloat16
NN = (((1,), (0,)), ((), ()))
NT = (((1,), (1,)), ((), ()))


def pair_tables(heads):
    first = np.zeros((DK, ROWS), np.float32)
    second = np.zeros((DK, ROWS), np.float32)
    add = np.zeros((8, ROWS), np.float32)
    for i in range(DK):
        first[i, i] = 1.0 / 32.0
        second[i, i] = 1.0
        first[i, DK + i] = 0.25
        add[1, DK + i] = 1.0
        for d in range(1, 8):
            row = WIDE + DK * (d - 1) + i
            first[i, row] = 1.0 / 16.0
            second[(i + d) % DK, row] = 1.0
    for i in range(8):
        first[i, 152 + i] = 1.0 / 16.0
        second[i + 8, 152 + i] = 1.0
    add[0, 2 * DK] = 1.0
    add[1, 2 * DK] = 1.0
    both = []
    for one in (first, second):
        table = np.zeros((heads, heads * DK, ROWS), np.float32)
        for j in range(heads):
            table[j, j * DK : (j + 1) * DK] = one
        both.append(jnp.asarray(table, BF16))
    return both[0], both[1], jnp.asarray(add, F32)


def dot(a, b, dims=NN):
    return lax.dot_general(a, b, dims, preferred_element_type=F32)


def split(x):
    high = x.astype(BF16)
    return high, (x - high.astype(F32)).astype(BF16)


def pack(ref, x):
    high = x.astype(BF16)
    ref[:ROWS] = high
    ref[ROWS:] = (x[:WIDE] - high[:WIDE].astype(F32)).astype(BF16)


def unpack(got):
    wide = got[:WIDE].astype(F32) + got[ROWS:].astype(F32)
    return jnp.concatenate([wide, got[WIDE:ROWS].astype(F32)], axis=0)


VMEM_SPEC = pl.BlockSpec(memory_space=pltpu.VMEM)
SMEM_SPEC = pl.BlockSpec(memory_space=pltpu.SMEM)
VMEM_LIMIT = 12 << 20


def call(body, name, outs, *operands, scalars=0, scratch=(), raw=False, aliases=None):
    held = [
        x if i < scalars else pltpu.with_memory_space_constraint(x, pltpu.HBM if raw else pltpu.VMEM)
        for i, x in enumerate(operands)
    ]
    many = isinstance(outs, tuple)
    spec = pl.BlockSpec(memory_space=pltpu.HBM) if raw else VMEM_SPEC
    return pl.pallas_call(
        body,
        out_shape=outs,
        in_specs=[SMEM_SPEC] * scalars + [spec] * (len(operands) - scalars),
        out_specs=tuple(VMEM_SPEC for _ in outs) if many else VMEM_SPEC,
        scratch_shapes=list(scratch),
        input_output_aliases=aliases or {},
        compiler_params=pltpu.CompilerParams(vmem_limit_bytes=VMEM_LIMIT),
        name=name,
    )(*held)


def one_state(x, v):
    toks = x.shape[1]
    ones = jnp.where(lax.broadcasted_iota(jnp.int32, (8, toks), 0) == 0, 1.0, 0.0).astype(F32)
    parts = [x * x, x, ones]
    for d in range(1, 8):
        parts.append(x * pltpu.roll(x, DK - d, 0))
    parts.append(x[:8] * x[8:])
    high, low = split(jnp.concatenate(parts, axis=0))
    full = jnp.ones((8, toks), BF16)
    total = dot(full, high, NT) + dot(full, low, NT)
    return dot(high, v) + dot(low, v), total


def put_states(out_ref, place_ref, far, other, kt_ref, vh_ref):
    part = out_ref.shape[0]
    half = place_ref[0] if far == 0 else 1 - place_ref[0]
    mid = place_ref[1] if other == 0 else 1 - place_ref[1]
    base = (half * 2 + mid) * part
    for j in range(part):
        x = kt_ref[pl.ds(pl.multiple_of((base + j) * DK, DK), DK), :]
        state, total = one_state(x, vh_ref[base + j])
        out_ref[j] = state
        out_ref[j, TOTAL_ROW : TOTAL_ROW + 1, :] = total[:1, :128]
        out_ref[j, TOTAL_ROW + 1 : TOTAL_ROW + 2, : ROWS - 128] = total[:1, 128:]


def rim_kernel(wk_ref, v_ref, rim_ref, sems):
    rows = pl.ds(wk_ref.shape[0] - WINDOW, WINDOW)
    copies = [
        pltpu.make_async_copy(ref.at[rows], rim_ref.at[i], sems.at[i])
        for i, ref in enumerate((wk_ref, v_ref))
    ]
    for copy in copies:
        copy.start()
    for copy in copies:
        copy.wait()


def first_states_kernel(place_ref, keys_ref, v_ref, after_ref, out_ref, vh_ref, kt_ref):
    vh_ref[...] = jnp.swapaxes(v_ref[...], 0, 1)
    kt_ref[...] = jnp.transpose(keys_ref[...].astype(F32), (1, 0))
    put_states(out_ref, place_ref, 1, 1, kt_ref, vh_ref)


def states_kernel(far, other, place_ref, kt_ref, vh_ref, after_ref, out_ref):
    put_states(out_ref, place_ref, far, other, kt_ref, vh_ref)


def chip_kernel(own_ref, other_ref, msg_ref):
    for j in range(own_ref.shape[0]):
        pack(msg_ref.at[j], own_ref[j] + other_ref[j])


def plane_kernel(own_ref, other_ref, got_ref, after_ref, sum_ref, msg_ref):
    for j in range(sum_ref.shape[0]):
        total = own_ref[j] + other_ref[j] + unpack(got_ref[j])
        sum_ref[j] = total
        pack(msg_ref.at[j], total)


def add_kernel(base_ref, got_ref, *rest):
    sum_ref, msg_ref = rest[-2:]
    for j in range(sum_ref.shape[0]):
        total = base_ref[j] + unpack(got_ref[j])
        sum_ref[j] = total
        pack(msg_ref.at[j], total)


def add_two_kernel(base_ref, got_ref, early_ref, *rest):
    sum_ref, msg_ref = rest[-2:]
    for j in range(sum_ref.shape[0]):
        total = base_ref[j] + (unpack(got_ref[j]) + unpack(early_ref[j]))
        sum_ref[j] = total
        pack(msg_ref.at[j], total)


def before_kernel(count, place_ref, own_ref, other_ref, pair_ref, *rest):
    gots, (prior_ref, send_ref, msg_ref) = rest[:count], rest[-3:]
    low, mid = place_ref[0], place_ref[1]
    for j in range(prior_ref.shape[0]):
        before = unpack(gots[0][j])
        for got in gots[1:]:
            before = before + unpack(got[j])
        own, other = own_ref[j], other_ref[j]
        mine = before + jnp.where(mid == 1, unpack(pair_ref[j]), 0.0)
        pack(msg_ref.at[j], before + jnp.where(mid == 0, own + other, 0.0))
        send_ref[j] = mine + jnp.where(low == 0, own, 0.0)
        prior_ref[j] = mine + jnp.where(low == 1, other, 0.0)


def rest_kernel(place_ref, got_ref, own_ref, other_ref, after_ref, prior_ref, send_ref):
    low = place_ref[0]
    for j in range(prior_ref.shape[0]):
        mine = unpack(got_ref[j])
        send_ref[j] = mine + jnp.where(low == 0, own_ref[j], 0.0)
        prior_ref[j] = mine + jnp.where(low == 1, other_ref[j], 0.0)


def phi_kernel(q_ref, e1_ref, e2_ref, add_ref, gain_ref, after_ref,
               high_ref, low_ref, gain_out_ref, q4_ref):
    for h in range(gain_ref.shape[0]):
        gain_out_ref[h] = gain_ref[h : h + 1].astype(F32)
    part = e1_ref.shape[0]
    width = part * DK
    for r in range(4):
        q4_ref[r] = q_ref[:, r * width : (r + 1) * width]

    def one(r, carry):
        q = q4_ref[r]
        for j in range(part):
            a = dot(q, e1_ref[j]) + add_ref[0:1]
            b = dot(q, e2_ref[j]) + add_ref[1:2]
            high, low = split(a * b)
            high_ref[r * part + j] = high
            low_ref[r * part + j] = low
        return carry

    lax.fori_loop(0, 4, one, 0)


def intra_kernel(q_ref, k_ref, vh_ref, after_ref, num_ref, den_ref, q4_ref, k4_ref):
    heads, toks, dim = vh_ref.shape
    part = heads // 4
    width = part * DK
    half = toks // 2
    for r in range(4):
        q4_ref[r] = q_ref[:, r * width : (r + 1) * width]
        k4_ref[r] = k_ref[:, r * width : (r + 1) * width]
    row = lax.broadcasted_iota(jnp.int32, (half, half), 0)
    col = lax.broadcasted_iota(jnp.int32, (half, half), 1)
    tri = col <= row
    lane = lax.broadcasted_iota(jnp.int32, (toks, width), 1) // DK
    ones = jnp.ones((toks, dim), BF16)

    def poly(s):
        return 1.0 + s * 0.25 + s * s * (1.0 / 32.0)

    def one(r, carry):
        q, k = q4_ref[r], k4_ref[r]
        tops, lows, rights = [], [], []
        for j in range(part):
            own = jnp.where(lane == j, q, jnp.zeros_like(q))
            tops.append(dot(own[:half], k[:half], NT))
            lows.append(dot(own[half:], k, NT))
        for j in range(part):
            head = r * part + j
            v = jnp.concatenate([vh_ref[head], ones], axis=1)
            top = jnp.where(tri, poly(tops[j]), 0.0)
            left = poly(lows[j][:, :half])
            right = jnp.where(tri, poly(lows[j][:, half:]), 0.0)
            high, low = split(top)
            both = dot(high, v[:half]) + dot(low, v[:half])
            num_ref[head, :half] = both[:, :dim]
            den_ref[head, :half] = both[:, dim:]
            high, low = split(jnp.concatenate([left, right], axis=1))
            both = dot(high, v) + dot(low, v)
            num_ref[head, half:] = both[:, :dim]
            den_ref[head, half:] = both[:, dim:]
        return carry

    lax.fori_loop(0, 4, one, 0)


def window_kernel(place_ref, wq_ref, wk_ref, vh_ref, rim_ref, after_ref,
                  win_ref, qh_ref, kh_ref, ve_ref):
    heads, toks, dim = vh_ref.shape
    part = heads // 4
    qh_ref[...] = jnp.swapaxes(wq_ref[...], 0, 1)
    kh_ref[:, :WINDOW] = jnp.swapaxes(rim_ref[0], 0, 1)
    kh_ref[:, WINDOW:] = jnp.swapaxes(wk_ref[...], 0, 1)
    ve_ref[:, :WINDOW] = jnp.swapaxes(rim_ref[1], 0, 1)
    ve_ref[:, WINDOW:] = vh_ref[...]
    row = lax.broadcasted_iota(jnp.int32, (WINDOW, 2 * WINDOW), 0)
    col = lax.broadcasted_iota(jnp.int32, (WINDOW, 2 * WINDOW), 1)
    band = (col > row) & (col <= row + WINDOW)
    edge = band & ((col >= WINDOW) | (place_ref[2] > 0))
    blocks = toks // WINDOW

    def one(r, carry):
        scores = []
        for j in range(part):
            head = r * part + j
            for b in range(blocks):
                lo = b * WINDOW
                sc = dot(qh_ref[head, lo : lo + WINDOW], kh_ref[head, lo : lo + 2 * WINDOW], NT)
                scores.append(jnp.where(edge if b == 0 else band, sc / math.sqrt(dim), -1e30))
        sc = jnp.concatenate(scores, axis=0)
        expo = jnp.exp(sc - jnp.max(sc, axis=1, keepdims=True))
        weights = (expo / jnp.sum(expo, axis=1, keepdims=True)).astype(BF16)
        for j in range(part):
            head = r * part + j
            for b in range(blocks):
                lo = b * WINDOW
                at = (j * blocks + b) * WINDOW
                win_ref[head, lo : lo + WINDOW] = dot(
                    weights[at : at + WINDOW], ve_ref[head, lo : lo + 2 * WINDOW]
                )
        return carry

    lax.fori_loop(0, 4, one, 0)


def final_kernel(far, other, stage, place_ref, prior_ref, high_ref, low_ref, num_ref, den_ref,
                 win_ref, gain_ref, *rest):
    mixed_ref, sq_ref = rest[-2:]
    part = prior_ref.shape[0]
    toks, dim = num_ref.shape[1:]
    half = place_ref[0] if far == 0 else 1 - place_ref[0]
    mid = place_ref[1] if other == 0 else 1 - place_ref[1]
    base = (half * 2 + mid) * part
    squares = jnp.zeros((toks, dim), F32) if stage == 0 else rest[1][...]
    for j in range(part):
        head = base + j
        prior = prior_ref[j]
        phi_high, phi_low = high_ref[head], low_ref[head]
        high, low = split(prior)
        both = dot(phi_high, jnp.concatenate([high, low], axis=1))
        numer = num_ref[head] + ((both[:, dim:] + dot(phi_low, high)) + both[:, :dim])
        total = jnp.concatenate(
            [prior[TOTAL_ROW : TOTAL_ROW + 1], prior[TOTAL_ROW + 1 : TOTAL_ROW + 2, : ROWS - 128]],
            axis=1,
        )
        t_high, t_low = split(jnp.broadcast_to(total, (dim, ROWS)))
        both = dot(phi_high, jnp.concatenate([t_high, t_low], axis=0), NT)
        denom = den_ref[head] + ((both[:, dim:] + dot(phi_low, t_high, NT)) + both[:, :dim])
        mixed = numer / denom + win_ref[head]
        mixed_ref[head] = mixed * gain_ref[head]
        squares = squares + mixed * mixed
    if stage < 3:
        sq_ref[...] = squares
    else:
        sq_ref[...] = lax.dot_general(
            jnp.ones((8, dim), F32), squares, NT,
            precision=lax.Precision.HIGHEST, preferred_element_type=F32,
        )


def norm_kernel(peers, mixed_ref, sq_ref, *rest):
    out_ref = rest[-1]
    total = sq_ref[...]
    for got in rest[:peers]:
        total = total + got[...]
    scale = lax.rsqrt(total / (HEADS * DV) + NORM_EPS)
    column = jnp.transpose(scale, (1, 0))[:, :1]
    wide = jnp.broadcast_to(column, mixed_ref.shape[1:])
    out_ref[...] = jnp.swapaxes((mixed_ref[...] * wide[None]).astype(BF16), 0, 1)


def on_device(queries, keys, values, win_q, win_k, gain):
    toks, heads, dim = values.shape
    count = lax.axis_size("ctx")
    peers = lax.axis_size("head") - 1
    where = lax.axis_index("ctx")
    place = jnp.stack([where & 1, (where >> 1) & 1, where]).astype(jnp.int32)
    part = heads // 4
    core_swap = [(i, i ^ 1) for i in range(count)]
    pair_swap = [(i, i ^ 2) for i in range(count)]
    state_shape = pltpu.VMEM((part, ROWS, dim), F32)
    msg_shape = pltpu.VMEM((part, SENT, dim), BF16)
    head_wide = pltpu.VMEM((heads, toks, dim), F32)

    def permute(x, pairs):
        return lax.ppermute(x, "ctx", pairs)

    rim = call(
        rim_kernel, "rim", pltpu.VMEM((2, WINDOW, heads, dim), BF16), win_k, values,
        raw=True, scratch=[pltpu.SemaphoreType.DMA((2,))],
    )
    rim_prev = permute(rim, [(i, i + 1) for i in range(count - 1)])

    far1, values_h, keys_t = call(
        first_states_kernel, "far1",
        (state_shape, pltpu.VMEM((heads, toks, dim), BF16), pltpu.VMEM((heads * DK, toks), F32)),
        place, keys, values, rim, scalars=1,
    )
    other1 = permute(far1, core_swap)

    def states(name, far, other, after):
        return call(functools.partial(states_kernel, far, other), name, state_shape,
                    place, keys_t, values_h, after, scalars=1)

    far0 = states("far0", 1, 0, far1)
    other0 = permute(far0, core_swap)
    near1 = states("near1", 0, 1, far0)
    msg = call(chip_kernel, "chip", msg_shape, near1, other1)
    pair = permute(msg, pair_swap)
    near0 = states("near0", 0, 0, msg)
    num, den = call(
        intra_kernel, "intra", (head_wide, head_wide), queries, keys, values_h, near0,
        scratch=[pltpu.VMEM((4, toks, part * DK), BF16)] * 2,
    )
    inclusive, msg = call(
        plane_kernel, "plane", (state_shape, msg_shape), near0, other0, pair, den
    )

    first_table, second_table, add_table = pair_tables(part)
    groups = count // 4
    gots = []
    start = msg
    step = 1
    phi_high = phi_low = win = None
    early = {}
    while step < groups:
        if step == 1:
            got = [permute(msg, [(i, i + 4) for i in range(count - 4)])]
            far_step = 2
            while far_step < groups:
                early[far_step] = permute(start, [(i, i + 4 * far_step) for i in range(4)])
                far_step *= 2
            phi_high, phi_low, gain = call(
                phi_kernel, "phi",
                (pltpu.VMEM((heads, toks, ROWS), BF16),) * 2 + (pltpu.VMEM((heads, 1, dim), F32),),
                queries, first_table, second_table, add_table, gain, msg,
                scratch=[pltpu.VMEM((4, toks, part * DK), BF16)],
            )
        else:
            got = [permute(msg, [(i, i + 4 * step) for i in range(4, count - 4 * step)]), early[step]]
        if step == 2:
            win = call(
                window_kernel, "window", head_wide,
                place, win_q, win_k, values_h, rim_prev, msg, scalars=1,
                scratch=[
                    pltpu.VMEM((heads, toks, dim), BF16),
                    pltpu.VMEM((heads, toks + WINDOW, dim), BF16),
                    pltpu.VMEM((heads, toks + WINDOW, dim), BF16),
                ],
            )
        gots.extend(got)
        step *= 2
        if step < groups:
            body = add_kernel if len(got) == 1 else add_two_kernel
            inclusive, msg = call(body, "add", (state_shape, msg_shape), inclusive, *got, phi_high)
    prior, send, msg = call(
        functools.partial(before_kernel, len(gots)), "before",
        (state_shape, state_shape, msg_shape),
        place, near0, other0, pair, *gots, win, scalars=1,
    )
    got = permute(msg, pair_swap)
    far_prior = permute(send, core_swap)

    def final(name, far, other, stage, prior, *held):
        last = pltpu.VMEM((8, toks) if stage == 3 else (toks, dim), F32)
        return call(
            functools.partial(final_kernel, far, other, stage), name, (head_wide, last),
            place, prior, phi_high, phi_low, num, den, win, gain, *held, scalars=1,
            aliases={8: 0} if stage else None,
        )

    mixed, squares = final("final0", 0, 0, 0, prior, msg)
    mixed, squares = final("final1", 1, 0, 1, far_prior, mixed, squares)
    prior, send = call(rest_kernel, "rest", (state_shape, state_shape),
                       place, got, near1, other1, squares, scalars=1)
    far_prior = permute(send, core_swap)
    mixed, squares = final("final2", 0, 1, 2, prior, mixed, squares)
    mixed, squares = final("final3", 1, 1, 3, far_prior, mixed, squares)
    others = [
        lax.ppermute(squares, "head", [(i, (i + k) % (peers + 1)) for i in range(peers + 1)])
        for k in range(1, peers + 1)
    ]
    return call(
        functools.partial(norm_kernel, peers), "norm",
        jax.ShapeDtypeStruct((toks, heads, dim), BF16),
        mixed, squares, *others,
    )


def solution(mesh):
    return jax.shard_map(
        on_device,
        mesh=mesh,
        in_specs=(
            P("ctx", "head"),
            P("ctx", "head"),
            P("ctx", "head", None),
            P("ctx", "head", None),
            P("ctx", "head", None),
            P("head", None),
        ),
        out_specs=P("ctx", "head", None),
        check_vma=False,
    )
```

```python
import functools
import math

import jax
import jax.numpy as jnp
import numpy as np
from jax import lax
from jax.experimental import pallas as pl
from jax.experimental.pallas import tpu as pltpu
from jax.sharding import PartitionSpec as P

HEADS = 32
DV = 128
DK = 16
WINDOW = 64
NORM_EPS = 1e-06

ROWS = 160
TOTAL_ROW = 33
WIDE = 40
HALF_WIDE = 2 * DK
SENT = ROWS + HALF_WIDE
GROUP = 4

F32 = jnp.float32
BF16 = jnp.bfloat16
NN = (((1,), (0,)), ((), ()))
NT = (((1,), (1,)), ((), ()))


def pair_tables(heads):
    first = np.zeros((DK, ROWS), np.float32)
    second = np.zeros((DK, ROWS), np.float32)
    add = np.zeros((8, ROWS), np.float32)
    for i in range(DK):
        first[i, i] = 1.0 / 32.0
        second[i, i] = 1.0
        first[i, DK + i] = 0.25
        add[1, DK + i] = 1.0
        for d in range(1, 8):
            row = WIDE + DK * (d - 1) + i
            first[i, row] = 1.0 / 16.0
            second[(i + d) % DK, row] = 1.0
    for i in range(8):
        first[i, 152 + i] = 1.0 / 16.0
        second[i + 8, 152 + i] = 1.0
    add[0, 2 * DK] = 1.0
    add[1, 2 * DK] = 1.0
    both = []
    for one in (first, second):
        table = np.zeros((heads, heads * DK, ROWS), np.float32)
        for j in range(heads):
            table[j, j * DK : (j + 1) * DK] = one
        both.append(jnp.asarray(table, BF16))
    return both[0], both[1], jnp.asarray(add, F32)


def dot(a, b, dims=NN):
    return lax.dot_general(a, b, dims, preferred_element_type=F32)


def split(x):
    high = x.astype(BF16)
    return high, (x - high.astype(F32)).astype(BF16)


def full(pairs, count):
    sources = [i for i in range(count) if i not in {a for a, _ in pairs}]
    targets = [i for i in range(count) if i not in {b for _, b in pairs}]
    stay = sorted(set(sources) & set(targets))
    moved = zip([i for i in sources if i not in stay], [i for i in targets if i not in stay])
    return list(pairs) + [(i, i) for i in stay] + list(moved)


def plane_index():
    return lax.axis_index("ctx") >> 2


def arrived(got_refs, limits, j):
    total = None
    for ref, (least, most) in zip(got_refs, limits):
        here = plane_index()
        meant = (here >= least) & (here <= most)
        got = jnp.where(meant, unpack(ref[j]), 0.0)
        total = got if total is None else total + got
    return total


def core_bit():
    return lax.axis_index("ctx") & 1


def pair_bit():
    return (lax.axis_index("ctx") >> 1) & 1


def each(count, body):
    group = math.gcd(GROUP, count)

    def step(i, carry):
        for j in range(group):
            body(i * group + j)
        return carry

    if group == count:
        step(0, 0)
    else:
        lax.fori_loop(0, count // group, step, 0)


def pack(ref, x):
    high = x.astype(BF16).astype(F32)
    low = x[:WIDE] - high[:WIDE]
    mid = high[HALF_WIDE:WIDE] + pltpu.roll(low[HALF_WIDE:], 3, 0).astype(BF16).astype(F32)
    ref[...] = jnp.concatenate(
        [high[:HALF_WIDE], mid, high[WIDE:], low[:HALF_WIDE]], axis=0
    ).astype(BF16)


def unpack(got):
    got = got.astype(F32)
    mid = got[HALF_WIDE:WIDE]
    row = lax.broadcasted_iota(jnp.int32, mid.shape, 0)
    mid = jnp.where(row < 3, mid + pltpu.roll(mid, 5, 0), 0.0)
    return jnp.concatenate([got[:HALF_WIDE] + got[ROWS:], mid, got[WIDE:ROWS]], axis=0)


VMEM_SPEC = pl.BlockSpec(memory_space=pltpu.VMEM)
VMEM_LIMIT = 12 << 20
FLOPS_PER_US = 1_150_000_000
EXPECTED_US = {"phi": 1.8, "intra": 2.8, "window": 3.5, "chip": 0.1, "plane": 0.1, "open": 12.0, "pick": 0.1}


def call(body, name, outs, *operands, scratch=(), raw=False, aliases=None):
    held = [
        pltpu.with_memory_space_constraint(x, pltpu.HBM if raw else pltpu.VMEM)
        for x in operands
    ]
    many = isinstance(outs, tuple)
    spec = pl.BlockSpec(memory_space=pltpu.HBM) if raw else VMEM_SPEC
    return pl.pallas_call(
        body,
        out_shape=outs,
        in_specs=[spec] * len(operands),
        out_specs=tuple(VMEM_SPEC for _ in outs) if many else VMEM_SPEC,
        scratch_shapes=list(scratch),
        input_output_aliases=aliases or {},
        cost_estimate=pl.CostEstimate(
            flops=int(EXPECTED_US.get(name, 1.0) * FLOPS_PER_US), bytes_accessed=0, transcendentals=0
        ),
        compiler_params=pltpu.CompilerParams(vmem_limit_bytes=VMEM_LIMIT),
        name=name,
    )(*held)


def one_state(x, v):
    toks = x.shape[1]
    ones = jnp.where(lax.broadcasted_iota(jnp.int32, (8, toks), 0) == 0, 1.0, 0.0).astype(F32)
    parts = [x * x, x, ones]
    for d in range(1, 8):
        parts.append(x * pltpu.roll(x, DK - d, 0))
    parts.append(x[:8] * x[8:])
    high, low = split(jnp.concatenate(parts, axis=0))
    full = jnp.ones((8, toks), BF16)
    total = dot(full, high, NT) + dot(full, low, NT)
    return dot(high, v) + dot(low, v), total


def put_states(out_ref, far, other, kt_ref, vh_ref):
    part = out_ref.shape[0]
    base = first_head(far, other, part)

    def one(j):
        x = kt_ref[pl.ds(pl.multiple_of((base + j) * DK, DK), DK), :]
        state, total = one_state(x, vh_ref[base + j])
        out_ref[j] = state
        out_ref[j, TOTAL_ROW : TOTAL_ROW + 1, :] = total[:1, :128]
        out_ref[j, TOTAL_ROW + 1 : TOTAL_ROW + 2, : ROWS - 128] = total[:1, 128:]

    each(part, one)


def rim_kernel(wk_ref, v_ref, rim_ref, sems):
    rows = pl.ds(wk_ref.shape[0] - WINDOW, WINDOW)
    copies = [
        pltpu.make_async_copy(ref.at[rows], rim_ref.at[i], sems.at[i])
        for i, ref in enumerate((wk_ref, v_ref))
    ]
    for copy in copies:
        copy.start()
    for copy in copies:
        copy.wait()


def first_states_kernel(keys_ref, v_ref, after_ref, out_ref, vh_ref, kt_ref):
    vh_ref[...] = jnp.swapaxes(v_ref[...], 0, 1)
    kt_ref[...] = jnp.transpose(keys_ref[...].astype(F32), (1, 0))
    put_states(out_ref, 1, 1, kt_ref, vh_ref)


def states_kernel(far, other, kt_ref, vh_ref, after_ref, out_ref):
    put_states(out_ref, far, other, kt_ref, vh_ref)


def far_rim_kernel(kt_ref, vh_ref, rim_ref, after_ref, out_ref, rim_out_ref):
    rim_out_ref[...] = rim_ref[...]
    put_states(out_ref, 1, 0, kt_ref, vh_ref)


def chip_kernel(own_ref, other_ref, msg_ref):
    def one(j):
        pack(msg_ref.at[j], own_ref[j] + other_ref[j])

    each(own_ref.shape[0], one)


def open_kernel(got_ref, *rest):
    out_ref = rest[-1]

    def one(j):
        out_ref[j] = unpack(got_ref[j])

    each(got_ref.shape[0], one)


def plane_kernel(own_ref, other_ref, got_ref, *rest):
    total_ref, msg_ref = rest[-2:]

    def one(j):
        total = own_ref[j] + other_ref[j] + got_ref[j]
        total_ref[j] = total
        pack(msg_ref.at[j], total)

    each(own_ref.shape[0], one)


def round_kernel(limits, total_ref, *rest):
    gots, (next_ref, msg_ref) = rest[: len(limits)], rest[-2:]

    def one(j):
        total = total_ref[j] + arrived(gots, limits, j)
        next_ref[j] = total
        pack(msg_ref.at[j], total)

    each(total_ref.shape[0], one)


def before_kernel(limits, own_ref, other_ref, pair_ref, *rest):
    gots, (mine_ref, msg_ref) = rest[: len(limits)], rest[-2:]
    mid = pair_bit()

    def one(j):
        before = arrived(gots, limits, j)
        mine_ref[j] = before + jnp.where(mid == 1, pair_ref[j], 0.0)
        pack(msg_ref.at[j], before + jnp.where(mid == 0, own_ref[j] + other_ref[j], 0.0))

    each(own_ref.shape[0], one)


def pick_kernel(rim_ref, got_ref, after_ref, out_ref):
    last = lax.axis_index("ctx") % 4 == 3

    @pl.when(last)
    def _():
        out_ref[...] = got_ref[...]

    @pl.when(jnp.logical_not(last))
    def _():
        out_ref[...] = rim_ref[...]


def phi_kernel(q_ref, e1_ref, e2_ref, add_ref, gain_ref, after_ref,
               high_ref, low_ref, gain_out_ref, q4_ref):
    for h in range(gain_ref.shape[0]):
        gain_out_ref[h] = gain_ref[h : h + 1].astype(F32)
    part = e1_ref.shape[0]
    width = part * DK
    for r in range(4):
        q4_ref[r] = q_ref[:, r * width : (r + 1) * width]

    def one(r, carry):
        q = q4_ref[r]
        for j in range(part):
            a = dot(q, e1_ref[j]) + add_ref[0:1]
            b = dot(q, e2_ref[j]) + add_ref[1:2]
            high, low = split(a * b)
            high_ref[r * part + j] = high
            low_ref[r * part + j] = low
        return carry

    lax.fori_loop(0, 4, one, 0)


def intra_kernel(q_ref, k_ref, vh_ref, after_ref,
                 num_ref, den_ref, again_ref, token_ref, q4_ref, k4_ref):
    again_ref[...] = after_ref[...]
    token_ref[...] = jnp.zeros_like(token_ref)
    heads, toks, dim = vh_ref.shape
    part = heads // 4
    width = part * DK
    half = toks // 2
    for r in range(4):
        q4_ref[r] = q_ref[:, r * width : (r + 1) * width]
        k4_ref[r] = k_ref[:, r * width : (r + 1) * width]
    row = lax.broadcasted_iota(jnp.int32, (half, half), 0)
    col = lax.broadcasted_iota(jnp.int32, (half, half), 1)
    tri = col <= row
    lane = lax.broadcasted_iota(jnp.int32, (toks, width), 1) // DK
    ones = jnp.ones((toks, dim), BF16)

    def poly(s):
        return 1.0 + s * 0.25 + s * s * (1.0 / 32.0)

    def one(r, carry):
        q, k = q4_ref[r], k4_ref[r]
        tops, lows, rights = [], [], []
        for j in range(part):
            own = jnp.where(lane == j, q, jnp.zeros_like(q))
            tops.append(dot(own[:half], k[:half], NT))
            lows.append(dot(own[half:], k, NT))
        for j in range(part):
            head = r * part + j
            v = jnp.concatenate([vh_ref[head], ones], axis=1)
            top = jnp.where(tri, poly(tops[j]), 0.0)
            left = poly(lows[j][:, :half])
            right = jnp.where(tri, poly(lows[j][:, half:]), 0.0)
            high, low = split(top)
            both = dot(high, v[:half]) + dot(low, v[:half])
            num_ref[head, :half] = both[:, :dim]
            den_ref[head, :half] = both[:, dim:]
            high, low = split(jnp.concatenate([left, right], axis=1))
            both = dot(high, v) + dot(low, v)
            num_ref[head, half:] = both[:, :dim]
            den_ref[head, half:] = both[:, dim:]
        return carry

    lax.fori_loop(0, 4, one, 0)


def softmax_blocks(scores):
    sc = jnp.concatenate(scores, axis=0)
    expo = jnp.exp(sc - jnp.max(sc, axis=1, keepdims=True))
    return (expo / jnp.sum(expo, axis=1, keepdims=True)).astype(BF16)


def band_mask():
    row = lax.broadcasted_iota(jnp.int32, (WINDOW, 2 * WINDOW), 0)
    col = lax.broadcasted_iota(jnp.int32, (WINDOW, 2 * WINDOW), 1)
    return (col > row) & (col <= row + WINDOW), col


def window_kernel(wq_ref, wk_ref, vh_ref, after_ref,
                  win_ref, edge_q_ref, edge_k_ref, token_ref, qh_ref, kh_ref):
    heads, toks, dim = vh_ref.shape
    part = heads // 4
    token_ref[...] = jnp.zeros_like(token_ref)
    qh_ref[...] = jnp.swapaxes(wq_ref[...], 0, 1)
    kh_ref[...] = jnp.swapaxes(wk_ref[...], 0, 1)
    edge_q_ref[...] = qh_ref[:, :WINDOW]
    edge_k_ref[...] = kh_ref[:, :WINDOW]
    band, _ = band_mask()
    blocks = toks // WINDOW - 1

    def one(r, carry):
        scores = []
        for j in range(part):
            head = r * part + j
            for b in range(blocks):
                lo = b * WINDOW
                q = qh_ref[head, lo + WINDOW : lo + 2 * WINDOW]
                sc = dot(q, kh_ref[head, lo : lo + 2 * WINDOW], NT)
                scores.append(jnp.where(band, sc / math.sqrt(dim), -1e30))
        weights = softmax_blocks(scores)
        for j in range(part):
            head = r * part + j
            for b in range(blocks):
                lo = b * WINDOW
                at = (j * blocks + b) * WINDOW
                win_ref[head, lo : lo + WINDOW] = dot(
                    weights[at : at + WINDOW], vh_ref[head, lo : lo + 2 * WINDOW]
                )
        return carry

    lax.fori_loop(0, 4, one, 0)


def edge_kernel(q_ref, k_ref, vh_ref, rim_ref, after_ref, out_ref, rk_ref, rv_ref):
    heads, _, dim = vh_ref.shape
    part = heads // 4
    rk_ref[...] = jnp.swapaxes(rim_ref[0], 0, 1)
    rv_ref[...] = jnp.swapaxes(rim_ref[1], 0, 1)
    band, col = band_mask()
    valid = band & ((col >= WINDOW) | (lax.axis_index("ctx") > 0))

    def one(r, carry):
        scores = []
        for j in range(part):
            head = r * part + j
            k = jnp.concatenate([rk_ref[head], k_ref[head]], axis=0)
            sc = dot(q_ref[head], k, NT)
            scores.append(jnp.where(valid, sc / math.sqrt(dim), -1e30))
        weights = softmax_blocks(scores)
        for j in range(part):
            head = r * part + j
            v = jnp.concatenate([rv_ref[head], vh_ref[head, :WINDOW]], axis=0)
            out_ref[head] = dot(weights[j * WINDOW : (j + 1) * WINDOW], v)
        return carry

    lax.fori_loop(0, 4, one, 0)


def first_head(far, other, part):
    half = core_bit() if far == 0 else 1 - core_bit()
    mid = pair_bit() if other == 0 else 1 - pair_bit()
    return (half * 2 + mid) * part


def mix(first, base_ref, extra_ref, high_ref, low_ref, num_ref, den_ref, edge_ref, win_ref,
        gain_ref, mixed_ref, squares):
    part, dim = base_ref.shape[0], num_ref.shape[2]
    for j in range(part):
        head = first + j
        base = unpack(base_ref[j]) if base_ref.shape[1] == SENT else base_ref[j]
        prior = base + jnp.where(core_bit() == 1, extra_ref[j], 0.0)
        phi_high, phi_low = high_ref[head], low_ref[head]
        high, low = split(prior)
        both = dot(phi_high, jnp.concatenate([high, low], axis=1))
        numer = num_ref[head] + ((both[:, dim:] + dot(phi_low, high)) + both[:, :dim])
        total = jnp.concatenate(
            [prior[TOTAL_ROW : TOTAL_ROW + 1], prior[TOTAL_ROW + 1 : TOTAL_ROW + 2, : ROWS - 128]],
            axis=1,
        )
        t_high, t_low = split(jnp.broadcast_to(total, (dim, ROWS)))
        both = dot(phi_high, jnp.concatenate([t_high, t_low], axis=0), NT)
        denom = den_ref[head] + ((both[:, dim:] + dot(phi_low, t_high, NT)) + both[:, :dim])
        window = jnp.concatenate([edge_ref[head], win_ref[head]], axis=0)
        mixed = numer / denom + window
        mixed_ref[head] = mixed * gain_ref[head]
        squares = squares + mixed * mixed
    return squares


def first_final_kernel(mine_ref, other_ref, far_ref, extra_ref, *rest):
    held, (mixed_ref, sq_ref) = rest[:-2], rest[-2:]
    part = mine_ref.shape[0]
    squares = jnp.zeros(sq_ref.shape, F32)
    squares = mix(first_head(0, 0, part), mine_ref, other_ref, *held, mixed_ref, squares)
    squares = mix(first_head(1, 0, part), far_ref, extra_ref, *held, mixed_ref, squares)
    sq_ref[...] = squares


def next_final_kernel(far, base_ref, extra_ref, *rest):
    held, (squares_ref, mixed_ref, sq_ref) = rest[:7], rest[-3:]
    first = first_head(far, 1, base_ref.shape[0])
    squares = mix(first, base_ref, extra_ref, *held, mixed_ref, squares_ref[...])
    if far == 0:
        sq_ref[...] = squares
    else:
        sq_ref[...] = lax.dot_general(
            jnp.ones((8, squares.shape[1]), F32), squares, NT,
            precision=lax.Precision.HIGHEST, preferred_element_type=F32,
        )


def norm_kernel(peers, mixed_ref, sq_ref, *rest):
    out_ref = rest[-1]
    total = sq_ref[...]
    for got in rest[:peers]:
        total = total + got[...]
    scale = lax.rsqrt(total / (HEADS * DV) + NORM_EPS)
    column = jnp.transpose(scale, (1, 0))[:, :1]
    wide = jnp.broadcast_to(column, mixed_ref.shape[1:])
    out_ref[...] = jnp.swapaxes((mixed_ref[...] * wide[None]).astype(BF16), 0, 1)


def on_device(queries, keys, values, win_q, win_k, gain):
    toks, heads, dim = values.shape
    count = lax.axis_size("ctx")
    peers = lax.axis_size("head") - 1
    part = heads // 4
    core_swap = [(i, i ^ 1) for i in range(count)]
    pair_swap = [(i, i ^ 2) for i in range(count)]
    state_shape = pltpu.VMEM((part, ROWS, dim), F32)
    msg_shape = pltpu.VMEM((part, SENT, dim), BF16)
    head_wide = pltpu.VMEM((heads, toks, dim), F32)
    token_shape = pltpu.VMEM((8, 128), F32)

    def permute(x, pairs):
        return lax.ppermute(x, "ctx", pairs)

    rim = call(
        rim_kernel, "rim", pltpu.VMEM((2, WINDOW, heads, dim), BF16), win_k, values,
        raw=True, scratch=[pltpu.SemaphoreType.DMA((2,))],
    )
    far1, values_h, keys_t = call(
        first_states_kernel, "far1",
        (state_shape, pltpu.VMEM((heads, toks, dim), BF16), pltpu.VMEM((heads * DK, toks), F32)),
        keys, values, rim,
    )
    other1 = permute(far1, core_swap)

    def states(name, far, other, after):
        return call(functools.partial(states_kernel, far, other), name, state_shape,
                    keys_t, values_h, after)

    near1 = states("near1", 0, 1, far1)
    msg = call(chip_kernel, "chip", msg_shape, near1, other1)
    pair = call(open_kernel, "open", state_shape, permute(msg, pair_swap))
    far0, rim = call(
        far_rim_kernel, "far0", (state_shape, pltpu.VMEM(rim.shape, BF16)),
        keys_t, values_h, rim, msg,
    )
    rim_up = permute(rim, full([(i, i + 4) for i in range(3, count - 4, 4)], count))
    other0 = permute(far0, core_swap)
    near0 = states("near0", 0, 0, far0)
    first_table, second_table, add_table = pair_tables(part)
    phi_high, phi_low, gain = call(
        phi_kernel, "phi",
        (pltpu.VMEM((heads, toks, ROWS), BF16),) * 2 + (pltpu.VMEM((heads, 1, dim), F32),),
        queries, first_table, second_table, add_table, gain, near0,
        scratch=[pltpu.VMEM((4, toks, part * DK), BF16)],
    )
    total, msg = call(plane_kernel, "plane", (state_shape, msg_shape), near0, other0, pair, gain)
    groups = count // 4
    gots, limits, early = [], [], {}
    step = 1
    while step < groups:
        if step == 1:
            got = [permute(msg, full([(i, i + 4) for i in range(count - 4)], count))]
            limit = [(1, groups)]
            far_near1 = permute(near1, core_swap)
            num, den, again, token = call(
                intra_kernel, "intra", (head_wide, head_wide, msg_shape, token_shape),
                queries, keys, values_h, msg,
                scratch=[pltpu.VMEM((4, toks, part * DK), BF16)] * 2,
            )
            while 2 * step < groups:
                step *= 2
                early[step] = permute(
                    again, full([(i, i + 4 * step) for i in range(4)], count)
                )
            step = 1
        else:
            pairs = [(i, i + 4 * step) for i in range(4, count - 4 * step)]
            got = [permute(msg, full(pairs, count)), early[step]]
            limit = [(step + 1, groups), (step, step)]
        if step == 2:
            far_near0 = permute(near0, core_swap)
            rim = call(pick_kernel, "pick", pltpu.VMEM(rim.shape, BF16), rim, rim_up, msg)
            rim_prev = permute(rim, [(i, i - i % 4 + (i + 1) % 4) for i in range(count)])
            win, edge_q, edge_k, token = call(
                window_kernel, "window",
                (pltpu.VMEM((heads, toks - WINDOW, dim), F32),)
                + (pltpu.VMEM((heads, WINDOW, dim), BF16),) * 2 + (token_shape,),
                win_q, win_k, values_h, msg,
                scratch=[pltpu.VMEM((heads, toks, dim), BF16)] * 2,
            )
        gots.extend(got)
        limits.extend(limit)
        step *= 2
        if step < groups:
            total, msg = call(
                functools.partial(round_kernel, limit), "round", (state_shape, msg_shape),
                total, *got, token,
            )
    mine, msg = call(
        functools.partial(before_kernel, limits), "before", (state_shape, msg_shape),
        near0, other0, pair, *gots, token,
    )
    got = permute(msg, pair_swap)
    far_mine = permute(mine, core_swap)
    edge = call(edge_kernel, "edge", pltpu.VMEM((heads, WINDOW, dim), F32),
                edge_q, edge_k, values_h, rim_prev, msg,
                scratch=[pltpu.VMEM((heads, WINDOW, dim), BF16)] * 2)

    held = (phi_high, phi_low, num, den, edge, win, gain)
    square_shape = pltpu.VMEM((toks, dim), F32)
    mixed, squares = call(
        first_final_kernel, "final0", (head_wide, square_shape),
        mine, other0, far_mine, far_near0, *held,
    )
    mine = call(open_kernel, "open", state_shape, got, squares)
    got, mine, squares = lax.optimization_barrier((got, mine, squares))
    far_got = permute(got, core_swap)
    mixed, squares = call(
        functools.partial(next_final_kernel, 0), "final1", (head_wide, square_shape),
        mine, other1, *held, mixed, squares, aliases={9: 0},
    )
    mixed, squares = call(
        functools.partial(next_final_kernel, 1), "final2",
        (head_wide, pltpu.VMEM((8, toks), F32)),
        far_got, far_near1, *held, mixed, squares, aliases={9: 0},
    )
    others = [
        lax.ppermute(squares, "head", [(i, (i + k) % (peers + 1)) for i in range(peers + 1)])
        for k in range(1, peers + 1)
    ]
    return call(
        functools.partial(norm_kernel, peers), "norm",
        jax.ShapeDtypeStruct((toks, heads, dim), BF16),
        mixed, squares, *others,
    )


def solution(mesh):
    return jax.shard_map(
        on_device,
        mesh=mesh,
        in_specs=(
            P("ctx", "head"),
            P("ctx", "head"),
            P("ctx", "head", None),
            P("ctx", "head", None),
            P("ctx", "head", None),
            P("head", None),
        ),
        out_specs=P("ctx", "head", None),
        check_vma=False,
    )
```

```python
import functools
import math

import jax
import jax.numpy as jnp
import numpy as np
from jax import lax
from jax.experimental import pallas as pl
from jax.experimental.pallas import tpu as pltpu
from jax.sharding import PartitionSpec as P

HEADS = 32
DV = 128
DK = 16
WINDOW = 64
NORM_EPS = 1e-06

ROWS = 160
TOTAL_ROW = 33
WIDE = 40
HALF_WIDE = 2 * DK
SENT = ROWS + HALF_WIDE
GROUP = 4

F32 = jnp.float32
BF16 = jnp.bfloat16
NN = (((1,), (0,)), ((), ()))
NT = (((1,), (1,)), ((), ()))


def pair_tables(heads):
    first = np.zeros((DK, ROWS), np.float32)
    second = np.zeros((DK, ROWS), np.float32)
    add = np.zeros((8, ROWS), np.float32)
    for i in range(DK):
        first[i, i] = 1.0 / 32.0
        second[i, i] = 1.0
        first[i, DK + i] = 0.25
        add[1, DK + i] = 1.0
        for d in range(1, 8):
            row = WIDE + DK * (d - 1) + i
            first[i, row] = 1.0 / 16.0
            second[(i + d) % DK, row] = 1.0
    for i in range(8):
        first[i, 152 + i] = 1.0 / 16.0
        second[i + 8, 152 + i] = 1.0
    add[0, 2 * DK] = 1.0
    add[1, 2 * DK] = 1.0
    both = []
    for one in (first, second):
        table = np.zeros((heads, heads * DK, ROWS), np.float32)
        for j in range(heads):
            table[j, j * DK : (j + 1) * DK] = one
        both.append(jnp.asarray(table, BF16))
    return both[0], both[1], jnp.asarray(add, F32)


def dot(a, b, dims=NN):
    return lax.dot_general(a, b, dims, preferred_element_type=F32)


def split(x):
    high = x.astype(BF16)
    return high, (x - high.astype(F32)).astype(BF16)


def full(pairs, count):
    sources = [i for i in range(count) if i not in {a for a, _ in pairs}]
    targets = [i for i in range(count) if i not in {b for _, b in pairs}]
    stay = sorted(set(sources) & set(targets))
    moved = zip([i for i in sources if i not in stay], [i for i in targets if i not in stay])
    return list(pairs) + [(i, i) for i in stay] + list(moved)


def plane_index():
    return lax.axis_index("ctx") >> 2


def arrived(got_refs, limits, j):
    total = None
    for ref, (least, most) in zip(got_refs, limits):
        here = plane_index()
        meant = (here >= least) & (here <= most)
        got = jnp.where(meant, unpack(ref[j]), 0.0)
        total = got if total is None else total + got
    return total


def core_bit():
    return lax.axis_index("ctx") & 1


def pair_bit():
    return (lax.axis_index("ctx") >> 1) & 1


def each(count, body):
    group = math.gcd(GROUP, count)

    def step(i, carry):
        for j in range(group):
            body(i * group + j)
        return carry

    if group == count:
        step(0, 0)
    else:
        lax.fori_loop(0, count // group, step, 0)


def pack(ref, x):
    high = x.astype(BF16).astype(F32)
    low = x[:WIDE] - high[:WIDE]
    mid = high[HALF_WIDE:WIDE] + pltpu.roll(low[HALF_WIDE:], 3, 0).astype(BF16).astype(F32)
    ref[...] = jnp.concatenate(
        [high[:HALF_WIDE], mid, high[WIDE:], low[:HALF_WIDE]], axis=0
    ).astype(BF16)


def unpack(got):
    got = got.astype(F32)
    mid = got[HALF_WIDE:WIDE]
    row = lax.broadcasted_iota(jnp.int32, mid.shape, 0)
    mid = jnp.where(row < 3, mid + pltpu.roll(mid, 5, 0), 0.0)
    return jnp.concatenate([got[:HALF_WIDE] + got[ROWS:], mid, got[WIDE:ROWS]], axis=0)


VMEM_SPEC = pl.BlockSpec(memory_space=pltpu.VMEM)
VMEM_LIMIT = 12 << 20
FLOPS_PER_US = 1_150_000_000
EXPECTED_US = {"phi": 1.8, "intra": 2.8, "window": 3.5, "chip": 0.1, "plane": 0.1, "open": 12.0, "pick": 60.0, "turn": 60.0}


def call(body, name, outs, *operands, scratch=(), raw=False, aliases=None):
    held = [
        pltpu.with_memory_space_constraint(x, pltpu.HBM if raw else pltpu.VMEM)
        for x in operands
    ]
    many = isinstance(outs, tuple)
    spec = pl.BlockSpec(memory_space=pltpu.HBM) if raw else VMEM_SPEC
    return pl.pallas_call(
        body,
        out_shape=outs,
        in_specs=[spec] * len(operands),
        out_specs=tuple(VMEM_SPEC for _ in outs) if many else VMEM_SPEC,
        scratch_shapes=list(scratch),
        input_output_aliases=aliases or {},
        cost_estimate=pl.CostEstimate(
            flops=int(EXPECTED_US.get(name, 1.0) * FLOPS_PER_US), bytes_accessed=0, transcendentals=0
        ),
        compiler_params=pltpu.CompilerParams(vmem_limit_bytes=VMEM_LIMIT),
        name=name,
    )(*held)


def one_state(x, v):
    toks = x.shape[1]
    ones = jnp.where(lax.broadcasted_iota(jnp.int32, (8, toks), 0) == 0, 1.0, 0.0).astype(F32)
    parts = [x * x, x, ones]
    for d in range(1, 8):
        parts.append(x * pltpu.roll(x, DK - d, 0))
    parts.append(x[:8] * x[8:])
    high, low = split(jnp.concatenate(parts, axis=0))
    full = jnp.ones((8, toks), BF16)
    total = dot(full, high, NT) + dot(full, low, NT)
    return dot(high, v) + dot(low, v), total


def put_states(out_ref, far, other, kt_ref, vh_ref):
    part = out_ref.shape[0]
    base = first_head(far, other, part)

    def one(j):
        x = kt_ref[pl.ds(pl.multiple_of((base + j) * DK, DK), DK), :]
        state, total = one_state(x, vh_ref[base + j])
        out_ref[j] = state
        out_ref[j, TOTAL_ROW : TOTAL_ROW + 1, :] = total[:1, :128]
        out_ref[j, TOTAL_ROW + 1 : TOTAL_ROW + 2, : ROWS - 128] = total[:1, 128:]

    each(part, one)


def rim_kernel(wk_ref, v_ref, rim_ref, sems):
    rows = pl.ds(wk_ref.shape[0] - WINDOW, WINDOW)
    copies = [
        pltpu.make_async_copy(ref.at[rows], rim_ref.at[i], sems.at[i])
        for i, ref in enumerate((wk_ref, v_ref))
    ]
    for copy in copies:
        copy.start()
    for copy in copies:
        copy.wait()


def first_states_kernel(keys_ref, v_ref, after_ref, out_ref, vh_ref, kt_ref):
    vh_ref[...] = jnp.swapaxes(v_ref[...], 0, 1)
    kt_ref[...] = jnp.transpose(keys_ref[...].astype(F32), (1, 0))
    put_states(out_ref, 1, 1, kt_ref, vh_ref)


def states_kernel(far, other, kt_ref, vh_ref, after_ref, out_ref):
    put_states(out_ref, far, other, kt_ref, vh_ref)


def chip_kernel(own_ref, other_ref, msg_ref):
    def one(j):
        pack(msg_ref.at[j], own_ref[j] + other_ref[j])

    each(own_ref.shape[0], one)


def open_kernel(got_ref, *rest):
    out_ref = rest[-1]

    def one(j):
        out_ref[j] = unpack(got_ref[j])

    each(got_ref.shape[0], one)


def plane_kernel(own_ref, other_ref, got_ref, *rest):
    total_ref, msg_ref = rest[-2:]

    def one(j):
        total = own_ref[j] + other_ref[j] + got_ref[j]
        total_ref[j] = total
        pack(msg_ref.at[j], total)

    each(own_ref.shape[0], one)


def round_kernel(limits, total_ref, *rest):
    gots, (next_ref, msg_ref) = rest[: len(limits)], rest[-2:]

    def one(j):
        total = total_ref[j] + arrived(gots, limits, j)
        next_ref[j] = total
        pack(msg_ref.at[j], total)

    each(total_ref.shape[0], one)


def before_kernel(limits, own_ref, other_ref, pair_ref, *rest):
    gots, (mine_ref, msg_ref) = rest[: len(limits)], rest[-2:]
    mid = pair_bit()

    def one(j):
        before = arrived(gots, limits, j)
        mine_ref[j] = before + jnp.where(mid == 1, pair_ref[j], 0.0)
        pack(msg_ref.at[j], before + jnp.where(mid == 0, own_ref[j] + other_ref[j], 0.0))

    each(own_ref.shape[0], one)


def pick_kernel(rim_ref, got_ref, msg_ref, out_ref, again_ref):
    last = lax.axis_index("ctx") % 4 == 3
    again_ref[...] = msg_ref[...]

    @pl.when(last)
    def _():
        out_ref[...] = got_ref[...]

    @pl.when(jnp.logical_not(last))
    def _():
        out_ref[...] = rim_ref[...]


def phi_kernel(q_ref, e1_ref, e2_ref, add_ref, gain_ref, after_ref,
               high_ref, low_ref, gain_out_ref, q4_ref):
    for h in range(gain_ref.shape[0]):
        gain_out_ref[h] = gain_ref[h : h + 1].astype(F32)
    part = e1_ref.shape[0]
    width = part * DK
    for r in range(4):
        q4_ref[r] = q_ref[:, r * width : (r + 1) * width]

    def one(r, carry):
        q = q4_ref[r]
        for j in range(part):
            a = dot(q, e1_ref[j]) + add_ref[0:1]
            b = dot(q, e2_ref[j]) + add_ref[1:2]
            high, low = split(a * b)
            high_ref[r * part + j] = high
            low_ref[r * part + j] = low
        return carry

    lax.fori_loop(0, 4, one, 0)


def intra_kernel(q_ref, k_ref, vh_ref, rim_ref, after_ref,
                 num_ref, den_ref, token_ref, q4_ref, k4_ref):
    token_ref[...] = jnp.zeros_like(token_ref)
    heads, toks, dim = vh_ref.shape
    part = heads // 4
    width = part * DK
    half = toks // 2
    for r in range(4):
        q4_ref[r] = q_ref[:, r * width : (r + 1) * width]
        k4_ref[r] = k_ref[:, r * width : (r + 1) * width]
    row = lax.broadcasted_iota(jnp.int32, (half, half), 0)
    col = lax.broadcasted_iota(jnp.int32, (half, half), 1)
    tri = col <= row
    lane = lax.broadcasted_iota(jnp.int32, (toks, width), 1) // DK
    ones = jnp.ones((toks, dim), BF16)

    def poly(s):
        return 1.0 + s * 0.25 + s * s * (1.0 / 32.0)

    def one(r, carry):
        q, k = q4_ref[r], k4_ref[r]
        tops, lows, rights = [], [], []
        for j in range(part):
            own = jnp.where(lane == j, q, jnp.zeros_like(q))
            tops.append(dot(own[:half], k[:half], NT))
            lows.append(dot(own[half:], k, NT))
        for j in range(part):
            head = r * part + j
            v = jnp.concatenate([vh_ref[head], ones], axis=1)
            top = jnp.where(tri, poly(tops[j]), 0.0)
            left = poly(lows[j][:, :half])
            right = jnp.where(tri, poly(lows[j][:, half:]), 0.0)
            high, low = split(top)
            both = dot(high, v[:half]) + dot(low, v[:half])
            num_ref[head, :half] = both[:, :dim]
            den_ref[head, :half] = both[:, dim:]
            high, low = split(jnp.concatenate([left, right], axis=1))
            both = dot(high, v) + dot(low, v)
            num_ref[head, half:] = both[:, :dim]
            den_ref[head, half:] = both[:, dim:]
        return carry

    lax.fori_loop(0, 4, one, 0)


def softmax_blocks(scores):
    sc = jnp.concatenate(scores, axis=0)
    expo = jnp.exp(sc - jnp.max(sc, axis=1, keepdims=True))
    return (expo / jnp.sum(expo, axis=1, keepdims=True)).astype(BF16)


def band_mask():
    row = lax.broadcasted_iota(jnp.int32, (WINDOW, 2 * WINDOW), 0)
    col = lax.broadcasted_iota(jnp.int32, (WINDOW, 2 * WINDOW), 1)
    return (col > row) & (col <= row + WINDOW), col


def by_head_kernel(wq_ref, wk_ref, after_ref, qh_ref, kh_ref, token_ref):
    token_ref[...] = jnp.zeros_like(token_ref)
    qh_ref[...] = jnp.swapaxes(wq_ref[...], 0, 1)
    kh_ref[...] = jnp.swapaxes(wk_ref[...], 0, 1)


def turn_kernel(rim_ref, after_ref, k_ref, v_ref):
    k_ref[...] = jnp.swapaxes(rim_ref[0], 0, 1)
    v_ref[...] = jnp.swapaxes(rim_ref[1], 0, 1)


def window_kernel(qh_ref, kh_ref, vh_ref, near0_ref, near1_ref, after_ref,
                  win_ref, nears_ref, token_ref):
    heads, toks, dim = vh_ref.shape
    part = heads // 4
    token_ref[...] = jnp.zeros_like(token_ref)
    nears_ref[0] = near0_ref[...]
    nears_ref[1] = near1_ref[...]
    band, _ = band_mask()
    blocks = toks // WINDOW - 1

    def one(r, carry):
        scores = []
        for j in range(part):
            head = r * part + j
            for b in range(blocks):
                lo = b * WINDOW
                q = qh_ref[head, lo + WINDOW : lo + 2 * WINDOW]
                sc = dot(q, kh_ref[head, lo : lo + 2 * WINDOW], NT)
                scores.append(jnp.where(band, sc / math.sqrt(dim), -1e30))
        weights = softmax_blocks(scores)
        for j in range(part):
            head = r * part + j
            for b in range(blocks):
                lo = b * WINDOW
                at = (j * blocks + b) * WINDOW
                win_ref[head, lo : lo + WINDOW] = dot(
                    weights[at : at + WINDOW], vh_ref[head, lo : lo + 2 * WINDOW]
                )
        return carry

    lax.fori_loop(0, 4, one, 0)


def edge_kernel(qh_ref, kh_ref, vh_ref, rk_ref, rv_ref, after_ref, out_ref):
    heads, _, dim = vh_ref.shape
    part = heads // 4
    band, col = band_mask()
    valid = band & ((col >= WINDOW) | (lax.axis_index("ctx") > 0))

    def one(r, carry):
        scores = []
        for j in range(part):
            head = r * part + j
            k = jnp.concatenate([rk_ref[head], kh_ref[head, :WINDOW]], axis=0)
            sc = dot(qh_ref[head, :WINDOW], k, NT)
            scores.append(jnp.where(valid, sc / math.sqrt(dim), -1e30))
        weights = softmax_blocks(scores)
        for j in range(part):
            head = r * part + j
            v = jnp.concatenate([rv_ref[head], vh_ref[head, :WINDOW]], axis=0)
            out_ref[head] = dot(weights[j * WINDOW : (j + 1) * WINDOW], v)
        return carry

    lax.fori_loop(0, 4, one, 0)


def first_head(far, other, part):
    half = core_bit() if far == 0 else 1 - core_bit()
    mid = pair_bit() if other == 0 else 1 - pair_bit()
    return (half * 2 + mid) * part


def mix(first, base_ref, extra_ref, high_ref, low_ref, num_ref, den_ref, edge_ref, win_ref,
        gain_ref, mixed_ref, squares):
    part, dim = base_ref.shape[0], num_ref.shape[2]
    for j in range(part):
        head = first + j
        base = unpack(base_ref[j]) if base_ref.shape[1] == SENT else base_ref[j]
        prior = base + jnp.where(core_bit() == 1, extra_ref[j], 0.0)
        phi_high, phi_low = high_ref[head], low_ref[head]
        high, low = split(prior)
        both = dot(phi_high, jnp.concatenate([high, low], axis=1))
        numer = num_ref[head] + ((both[:, dim:] + dot(phi_low, high)) + both[:, :dim])
        total = jnp.concatenate(
            [prior[TOTAL_ROW : TOTAL_ROW + 1], prior[TOTAL_ROW + 1 : TOTAL_ROW + 2, : ROWS - 128]],
            axis=1,
        )
        t_high, t_low = split(jnp.broadcast_to(total, (dim, ROWS)))
        both = dot(phi_high, jnp.concatenate([t_high, t_low], axis=0), NT)
        denom = den_ref[head] + ((both[:, dim:] + dot(phi_low, t_high, NT)) + both[:, :dim])
        window = jnp.concatenate([edge_ref[head], win_ref[head]], axis=0)
        mixed = numer / denom + window
        mixed_ref[head] = mixed * gain_ref[head]
        squares = squares + mixed * mixed
    return squares


def first_final_kernel(mine_ref, other_ref, far_ref, extra_ref, *rest):
    held, (mixed_ref, sq_ref) = rest[:-2], rest[-2:]
    part = mine_ref.shape[0]
    squares = jnp.zeros(sq_ref.shape, F32)
    squares = mix(first_head(0, 0, part), mine_ref, other_ref, *held, mixed_ref, squares)
    squares = mix(first_head(1, 0, part), far_ref, extra_ref.at[0], *held, mixed_ref, squares)
    sq_ref[...] = squares


def next_final_kernel(far, base_ref, extra_ref, *rest):
    held, (squares_ref, mixed_ref, sq_ref) = rest[:7], rest[-3:]
    first = first_head(far, 1, base_ref.shape[0])
    if far == 1:
        extra_ref = extra_ref.at[1]
    squares = mix(first, base_ref, extra_ref, *held, mixed_ref, squares_ref[...])
    if far == 0:
        sq_ref[...] = squares
    else:
        sq_ref[...] = lax.dot_general(
            jnp.ones((8, squares.shape[1]), F32), squares, NT,
            precision=lax.Precision.HIGHEST, preferred_element_type=F32,
        )


def norm_kernel(peers, mixed_ref, sq_ref, *rest):
    out_ref = rest[-1]
    total = sq_ref[...]
    for got in rest[:peers]:
        total = total + got[...]
    scale = lax.rsqrt(total / (HEADS * DV) + NORM_EPS)
    column = jnp.transpose(scale, (1, 0))[:, :1]
    wide = jnp.broadcast_to(column, mixed_ref.shape[1:])
    out_ref[...] = jnp.swapaxes((mixed_ref[...] * wide[None]).astype(BF16), 0, 1)


def on_device(queries, keys, values, win_q, win_k, gain):
    toks, heads, dim = values.shape
    count = lax.axis_size("ctx")
    peers = lax.axis_size("head") - 1
    part = heads // 4
    core_swap = [(i, i ^ 1) for i in range(count)]
    pair_swap = [(i, i ^ 2) for i in range(count)]
    state_shape = pltpu.VMEM((part, ROWS, dim), F32)
    msg_shape = pltpu.VMEM((part, SENT, dim), BF16)
    head_wide = pltpu.VMEM((heads, toks, dim), F32)
    token_shape = pltpu.VMEM((8, 128), F32)

    def permute(x, pairs):
        return lax.ppermute(x, "ctx", pairs)

    rim = call(
        rim_kernel, "rim", pltpu.VMEM((2, WINDOW, heads, dim), BF16), win_k, values,
        raw=True, scratch=[pltpu.SemaphoreType.DMA((2,))],
    )
    rim_up = permute(rim, full([(i, i + 4) for i in range(3, count - 4, 4)], count))
    far1, values_h, keys_t = call(
        first_states_kernel, "far1",
        (state_shape, pltpu.VMEM((heads, toks, dim), BF16), pltpu.VMEM((heads * DK, toks), F32)),
        keys, values, rim,
    )
    other1 = permute(far1, core_swap)

    def states(name, far, other, after):
        return call(functools.partial(states_kernel, far, other), name, state_shape,
                    keys_t, values_h, after)

    near1 = states("near1", 0, 1, far1)
    msg = call(chip_kernel, "chip", msg_shape, near1, other1)
    pair = call(open_kernel, "open", state_shape, permute(msg, pair_swap))
    far0 = states("far0", 1, 0, msg)
    other0 = permute(far0, core_swap)
    near0 = states("near0", 0, 0, far0)
    first_table, second_table, add_table = pair_tables(part)
    phi_high, phi_low, gain = call(
        phi_kernel, "phi",
        (pltpu.VMEM((heads, toks, ROWS), BF16),) * 2 + (pltpu.VMEM((heads, 1, dim), F32),),
        queries, first_table, second_table, add_table, gain, near0,
        scratch=[pltpu.VMEM((4, toks, part * DK), BF16)],
    )
    wq_h, wk_h, token = call(
        by_head_kernel, "by_head",
        (pltpu.VMEM((heads, toks, dim), BF16),) * 2 + (token_shape,), win_q, win_k, gain,
    )
    total, msg = call(plane_kernel, "plane", (state_shape, msg_shape), near0, other0, pair, token)
    rim, again = call(
        pick_kernel, "pick", (pltpu.VMEM(rim.shape, BF16), msg_shape), rim, rim_up, msg
    )
    rim_prev = permute(rim, [(i, i - i % 4 + (i + 1) % 4) for i in range(count)])
    groups = count // 4
    gots, limits, early = [], [], {}
    step = 1
    while step < groups:
        if step == 1:
            got = [permute(msg, full([(i, i + 4) for i in range(count - 4)], count))]
            limit = [(1, groups)]
            num, den, token = call(
                intra_kernel, "intra", (head_wide, head_wide, token_shape),
                queries, keys, values_h, rim, msg,
                scratch=[pltpu.VMEM((4, toks, part * DK), BF16)] * 2,
            )
            while 2 * step < groups:
                step *= 2
                early[step] = permute(
                    again, full([(i, i + 4 * step) for i in range(4)], count)
                )
            step = 1
        else:
            pairs = [(i, i + 4 * step) for i in range(4, count - 4 * step)]
            got = [permute(msg, full(pairs, count)), early[step]]
            limit = [(step + 1, groups), (step, step)]
        if step == 2:
            win, nears, token = call(
                window_kernel, "window",
                (pltpu.VMEM((heads, toks - WINDOW, dim), F32),
                 pltpu.VMEM((2, part, ROWS, dim), F32), token_shape),
                wq_h, wk_h, values_h, near0, near1, msg,
            )
            rim_k, rim_v = call(
                turn_kernel, "turn", (pltpu.VMEM((heads, WINDOW, dim), BF16),) * 2, rim_prev, token
            )
        gots.extend(got)
        limits.extend(limit)
        step *= 2
        if step < groups:
            total, msg = call(
                functools.partial(round_kernel, limit), "round", (state_shape, msg_shape),
                total, *got, token,
            )
    mine, msg = call(
        functools.partial(before_kernel, limits), "before", (state_shape, msg_shape),
        near0, other0, pair, *gots, token,
    )
    got = permute(msg, pair_swap)
    far_mine = permute(mine, core_swap)
    far_nears = permute(nears, core_swap)
    edge = call(edge_kernel, "edge", pltpu.VMEM((heads, WINDOW, dim), F32),
                wq_h, wk_h, values_h, rim_k, rim_v, msg)

    held = (phi_high, phi_low, num, den, edge, win, gain)
    square_shape = pltpu.VMEM((toks, dim), F32)
    mixed, squares = call(
        first_final_kernel, "final0", (head_wide, square_shape),
        mine, other0, far_mine, far_nears, *held,
    )
    mine = call(open_kernel, "open", state_shape, got, squares)
    got, mine, squares = lax.optimization_barrier((got, mine, squares))
    far_got = permute(got, core_swap)
    mixed, squares = call(
        functools.partial(next_final_kernel, 0), "final1", (head_wide, square_shape),
        mine, other1, *held, mixed, squares, aliases={9: 0},
    )
    mixed, squares = call(
        functools.partial(next_final_kernel, 1), "final2",
        (head_wide, pltpu.VMEM((8, toks), F32)),
        far_got, far_nears, *held, mixed, squares, aliases={9: 0},
    )
    others = [
        lax.ppermute(squares, "head", [(i, (i + k) % (peers + 1)) for i in range(peers + 1)])
        for k in range(1, peers + 1)
    ]
    return call(
        functools.partial(norm_kernel, peers), "norm",
        jax.ShapeDtypeStruct((toks, heads, dim), BF16),
        mixed, squares, *others,
    )


def solution(mesh):
    return jax.shard_map(
        on_device,
        mesh=mesh,
        in_specs=(
            P("ctx", "head"),
            P("ctx", "head"),
            P("ctx", "head", None),
            P("ctx", "head", None),
            P("ctx", "head", None),
            P("head", None),
        ),
        out_specs=P("ctx", "head", None),
        check_vma=False,
    )
```

```python
import functools
import math

import jax
import jax.numpy as jnp
import numpy as np
from jax import lax
from jax.experimental import pallas as pl
from jax.experimental.pallas import tpu as pltpu
from jax.sharding import PartitionSpec as P

HEADS = 32
DV = 128
DK = 16
WINDOW = 64
NORM_EPS = 1e-06

ROWS = 160
TOTAL_ROW = 33
WIDE = 40
HALF_WIDE = 2 * DK
SENT = ROWS + HALF_WIDE
GROUP = 4

F32 = jnp.float32
BF16 = jnp.bfloat16
NN = (((1,), (0,)), ((), ()))
NT = (((1,), (1,)), ((), ()))


def pair_tables(heads):
    first = np.zeros((DK, ROWS), np.float32)
    second = np.zeros((DK, ROWS), np.float32)
    add = np.zeros((8, ROWS), np.float32)
    for i in range(DK):
        first[i, i] = 1.0 / 32.0
        second[i, i] = 1.0
        first[i, DK + i] = 0.25
        add[1, DK + i] = 1.0
        for d in range(1, 8):
            row = WIDE + DK * (d - 1) + i
            first[i, row] = 1.0 / 16.0
            second[(i + d) % DK, row] = 1.0
    for i in range(8):
        first[i, 152 + i] = 1.0 / 16.0
        second[i + 8, 152 + i] = 1.0
    add[0, 2 * DK] = 1.0
    add[1, 2 * DK] = 1.0
    both = []
    for one in (first, second):
        table = np.zeros((heads, heads * DK, ROWS), np.float32)
        for j in range(heads):
            table[j, j * DK : (j + 1) * DK] = one
        both.append(jnp.asarray(table, BF16))
    return both[0], both[1], jnp.asarray(add, F32)


def dot(a, b, dims=NN):
    return lax.dot_general(a, b, dims, preferred_element_type=F32)


def split(x):
    high = x.astype(BF16)
    return high, (x - high.astype(F32)).astype(BF16)


def full(pairs, count):
    sources = [i for i in range(count) if i not in {a for a, _ in pairs}]
    targets = [i for i in range(count) if i not in {b for _, b in pairs}]
    stay = sorted(set(sources) & set(targets))
    moved = zip([i for i in sources if i not in stay], [i for i in targets if i not in stay])
    return list(pairs) + [(i, i) for i in stay] + list(moved)


def plane_index():
    return lax.axis_index("ctx") >> 2


def arrived(got_refs, limits, j):
    total = None
    for ref, (least, most) in zip(got_refs, limits):
        here = plane_index()
        meant = (here >= least) & (here <= most)
        got = jnp.where(meant, unpack(ref[j]), 0.0)
        total = got if total is None else total + got
    return total


def core_bit():
    return lax.axis_index("ctx") & 1


def pair_bit():
    return (lax.axis_index("ctx") >> 1) & 1


def each(count, body):
    group = math.gcd(GROUP, count)

    def step(i, carry):
        for j in range(group):
            body(i * group + j)
        return carry

    if group == count:
        step(0, 0)
    else:
        lax.fori_loop(0, count // group, step, 0)


def pack(ref, x):
    high = x.astype(BF16).astype(F32)
    low = x[:WIDE] - high[:WIDE]
    mid = high[HALF_WIDE:WIDE] + pltpu.roll(low[HALF_WIDE:], 3, 0).astype(BF16).astype(F32)
    ref[...] = jnp.concatenate(
        [high[:HALF_WIDE], mid, high[WIDE:], low[:HALF_WIDE]], axis=0
    ).astype(BF16)


def unpack(got):
    got = got.astype(F32)
    mid = got[HALF_WIDE:WIDE]
    row = lax.broadcasted_iota(jnp.int32, mid.shape, 0)
    mid = jnp.where(row < 3, mid + pltpu.roll(mid, 5, 0), 0.0)
    return jnp.concatenate([got[:HALF_WIDE] + got[ROWS:], mid, got[WIDE:ROWS]], axis=0)


VMEM_SPEC = pl.BlockSpec(memory_space=pltpu.VMEM)
HBM_SPEC = pl.BlockSpec(memory_space=pltpu.HBM)
VMEM_LIMIT = 12 << 20
FLOPS_PER_US = 1_150_000_000
EXPECTED_US = {"phi": 1.8, "intra": 2.8, "window": 3.5, "chip": 0.1, "plane": 0.1, "open": 12.0, "pick": 60.0, "turn": 60.0}


def call(body, name, outs, *operands, scratch=(), raw=False, aliases=None):
    held = [
        pltpu.with_memory_space_constraint(x, pltpu.HBM if raw else pltpu.VMEM)
        for x in operands
    ]
    many = isinstance(outs, tuple)
    spec = HBM_SPEC if raw else VMEM_SPEC
    return pl.pallas_call(
        body,
        out_shape=outs,
        in_specs=[spec] * len(operands),
        out_specs=tuple(VMEM_SPEC for _ in outs) if many else VMEM_SPEC,
        scratch_shapes=list(scratch),
        input_output_aliases=aliases or {},
        cost_estimate=pl.CostEstimate(
            flops=int(EXPECTED_US.get(name, 1.0) * FLOPS_PER_US), bytes_accessed=0, transcendentals=0
        ),
        compiler_params=pltpu.CompilerParams(vmem_limit_bytes=VMEM_LIMIT),
        name=name,
    )(*held)


def one_state(x, v):
    toks = x.shape[1]
    ones = jnp.where(lax.broadcasted_iota(jnp.int32, (8, toks), 0) == 0, 1.0, 0.0).astype(F32)
    parts = [x * x, x, ones]
    for d in range(1, 8):
        parts.append(x * pltpu.roll(x, DK - d, 0))
    parts.append(x[:8] * x[8:])
    high, low = split(jnp.concatenate(parts, axis=0))
    full = jnp.ones((8, toks), BF16)
    total = dot(full, high, NT) + dot(full, low, NT)
    return dot(high, v) + dot(low, v), total


def put_states(out_ref, far, other, kt_ref, vh_ref):
    part = out_ref.shape[0]
    base = first_head(far, other, part)

    def one(j):
        x = kt_ref[pl.ds(pl.multiple_of((base + j) * DK, DK), DK), :]
        state, total = one_state(x, vh_ref[base + j])
        out_ref[j] = state
        out_ref[j, TOTAL_ROW : TOTAL_ROW + 1, :] = total[:1, :128]
        out_ref[j, TOTAL_ROW + 1 : TOTAL_ROW + 2, : ROWS - 128] = total[:1, 128:]

    each(part, one)


def first_states_kernel(keys_hbm, v_hbm, wk_hbm, out_ref, vh_ref, kt_ref, rim_ref,
                        keys_ref, v_ref, sems):
    toks, heads = v_hbm.shape[:2]
    pieces = v_ref.shape[0]
    size = heads // pieces
    tail = pl.ds(toks - WINDOW, WINDOW)
    firsts = [pl.multiple_of((1 - core_bit()) * size, size), pl.multiple_of(core_bit() * size, size)]
    if pieces == 1:
        firsts = [0]
    copies = [pltpu.make_async_copy(keys_hbm, keys_ref, sems.at[0])]
    for i, first in enumerate(firsts):
        copies.append(
            pltpu.make_async_copy(v_hbm.at[:, pl.ds(first, size)], v_ref.at[i], sems.at[1 + i])
        )
    copies.append(pltpu.make_async_copy(wk_hbm.at[tail], rim_ref.at[0], sems.at[3]))
    copies.append(pltpu.make_async_copy(v_hbm.at[tail], rim_ref.at[1], sems.at[4]))
    for copy in copies:
        copy.start()
    copies[0].wait()
    kt_ref[...] = jnp.transpose(keys_ref[...].astype(F32), (1, 0))
    for i, first in enumerate(firsts):
        copies[1 + i].wait()
        vh_ref[pl.ds(first, size)] = jnp.swapaxes(v_ref[i], 0, 1)
        if i == 0:
            put_states(out_ref, 1, 1, kt_ref, vh_ref)
    copies[-2].wait()
    copies[-1].wait()


def states_kernel(far, other, kt_ref, vh_ref, after_ref, out_ref):
    put_states(out_ref, far, other, kt_ref, vh_ref)


def chip_kernel(own_ref, other_ref, msg_ref):
    def one(j):
        pack(msg_ref.at[j], own_ref[j] + other_ref[j])

    each(own_ref.shape[0], one)


def open_kernel(got_ref, *rest):
    out_ref = rest[-1]

    def one(j):
        out_ref[j] = unpack(got_ref[j])

    each(got_ref.shape[0], one)


def plane_kernel(own_ref, other_ref, got_ref, *rest):
    total_ref, msg_ref = rest[-2:]

    def one(j):
        total = own_ref[j] + other_ref[j] + got_ref[j]
        total_ref[j] = total
        pack(msg_ref.at[j], total)

    each(own_ref.shape[0], one)


def round_kernel(limits, keep, total_ref, *rest):
    gots, outs = rest[: len(limits)], rest[len(limits) + 1 :]

    def one(j):
        total = total_ref[j] + arrived(gots, limits, j)
        pack(outs[0].at[j], total)
        if keep:
            outs[1][j] = total

    each(total_ref.shape[0], one)


def before_kernel(limits, own_ref, other_ref, pair_ref, *rest):
    gots, (mine_ref, msg_ref) = rest[: len(limits)], rest[-2:]
    mid = pair_bit()

    def one(j):
        before = arrived(gots, limits, j)
        mine_ref[j] = before + jnp.where(mid == 1, pair_ref[j], 0.0)
        pack(msg_ref.at[j], before + jnp.where(mid == 0, own_ref[j] + other_ref[j], 0.0))

    each(own_ref.shape[0], one)


def pick_kernel(rim_ref, got_ref, msg_ref, out_ref, again_ref):
    last = lax.axis_index("ctx") % 4 == 3
    again_ref[...] = msg_ref[...]

    @pl.when(last)
    def _():
        out_ref[...] = got_ref[...]

    @pl.when(jnp.logical_not(last))
    def _():
        out_ref[...] = rim_ref[...]


def phi_kernel(q_ref, e1_ref, e2_ref, add_ref, gain_ref, after_ref,
               high_ref, low_ref, gain_out_ref, q4_ref):
    for h in range(gain_ref.shape[0]):
        gain_out_ref[h] = gain_ref[h : h + 1].astype(F32)
    part = e1_ref.shape[0]
    width = part * DK
    for r in range(4):
        q4_ref[r] = q_ref[:, r * width : (r + 1) * width]

    def one(r, carry):
        q = q4_ref[r]
        for j in range(part):
            a = dot(q, e1_ref[j]) + add_ref[0:1]
            b = dot(q, e2_ref[j]) + add_ref[1:2]
            high, low = split(a * b)
            high_ref[r * part + j] = high
            low_ref[r * part + j] = low
        return carry

    lax.fori_loop(0, 4, one, 0)


def intra_kernel(q_ref, k_ref, vh_ref, rim_ref, after_ref,
                 num_ref, den_ref, token_ref, q4_ref, k4_ref):
    token_ref[...] = jnp.zeros_like(token_ref)
    heads, toks, dim = vh_ref.shape
    part = heads // 4
    width = part * DK
    half = toks // 2
    for r in range(4):
        q4_ref[r] = q_ref[:, r * width : (r + 1) * width]
        k4_ref[r] = k_ref[:, r * width : (r + 1) * width]
    row = lax.broadcasted_iota(jnp.int32, (half, half), 0)
    col = lax.broadcasted_iota(jnp.int32, (half, half), 1)
    tri = col <= row
    lane = lax.broadcasted_iota(jnp.int32, (toks, width), 1) // DK
    ones = jnp.ones((toks, dim), BF16)

    def poly(s):
        return 1.0 + s * 0.25 + s * s * (1.0 / 32.0)

    def one(r, carry):
        q, k = q4_ref[r], k4_ref[r]
        tops, lows, rights = [], [], []
        for j in range(part):
            own = jnp.where(lane == j, q, jnp.zeros_like(q))
            tops.append(dot(own[:half], k[:half], NT))
            lows.append(dot(own[half:], k, NT))
        for j in range(part):
            head = r * part + j
            v = jnp.concatenate([vh_ref[head], ones], axis=1)
            top = jnp.where(tri, poly(tops[j]), 0.0)
            left = poly(lows[j][:, :half])
            right = jnp.where(tri, poly(lows[j][:, half:]), 0.0)
            high, low = split(top)
            both = dot(high, v[:half]) + dot(low, v[:half])
            num_ref[head, :half] = both[:, :dim]
            den_ref[head, :half] = both[:, dim:]
            high, low = split(jnp.concatenate([left, right], axis=1))
            both = dot(high, v) + dot(low, v)
            num_ref[head, half:] = both[:, :dim]
            den_ref[head, half:] = both[:, dim:]
        return carry

    lax.fori_loop(0, 4, one, 0)


def softmax_blocks(scores):
    sc = jnp.concatenate(scores, axis=0)
    expo = jnp.exp(sc - jnp.max(sc, axis=1, keepdims=True))
    return (expo / jnp.sum(expo, axis=1, keepdims=True)).astype(BF16)


def band_mask():
    row = lax.broadcasted_iota(jnp.int32, (WINDOW, 2 * WINDOW), 0)
    col = lax.broadcasted_iota(jnp.int32, (WINDOW, 2 * WINDOW), 1)
    return (col > row) & (col <= row + WINDOW), col


def by_head_kernel(wq_ref, wk_ref, after_ref, qh_ref, kh_ref, token_ref):
    token_ref[...] = jnp.zeros_like(token_ref)
    qh_ref[...] = jnp.swapaxes(wq_ref[...], 0, 1)
    kh_ref[...] = jnp.swapaxes(wk_ref[...], 0, 1)


def turn_kernel(rim_ref, other1_ref, after_ref, k_ref, v_ref, keep_ref):
    keep_ref[...] = other1_ref[...]
    k_ref[...] = jnp.swapaxes(rim_ref[0], 0, 1)
    v_ref[...] = jnp.swapaxes(rim_ref[1], 0, 1)


def window_kernel(qh_ref, kh_ref, vh_ref, near0_ref, near1_ref, after_ref,
                  win_ref, nears_ref, token_ref):
    heads, toks, dim = vh_ref.shape
    part = heads // 4
    token_ref[...] = jnp.zeros_like(token_ref)
    nears_ref[0] = near0_ref[...]
    nears_ref[1] = near1_ref[...]
    band, _ = band_mask()
    blocks = toks // WINDOW - 1

    def one(r, carry):
        scores = []
        for j in range(part):
            head = r * part + j
            for b in range(blocks):
                lo = b * WINDOW
                q = qh_ref[head, lo + WINDOW : lo + 2 * WINDOW]
                sc = dot(q, kh_ref[head, lo : lo + 2 * WINDOW], NT)
                scores.append(jnp.where(band, sc / math.sqrt(dim), -1e30))
        weights = softmax_blocks(scores)
        for j in range(part):
            head = r * part + j
            for b in range(blocks):
                lo = b * WINDOW
                at = (j * blocks + b) * WINDOW
                win_ref[head, lo : lo + WINDOW] = dot(
                    weights[at : at + WINDOW], vh_ref[head, lo : lo + 2 * WINDOW]
                )
        return carry

    lax.fori_loop(0, 4, one, 0)


def edge_kernel(qh_ref, kh_ref, vh_ref, rk_ref, rv_ref, after_ref, out_ref):
    heads, _, dim = vh_ref.shape
    band, col = band_mask()
    valid = band & ((col >= WINDOW) | (lax.axis_index("ctx") > 0))

    scores = []
    for head in range(heads):
        k = jnp.concatenate([rk_ref[head], kh_ref[head, :WINDOW]], axis=0)
        sc = dot(qh_ref[head, :WINDOW], k, NT)
        scores.append(jnp.where(valid, sc / math.sqrt(dim), -1e30))
    weights = softmax_blocks(scores)
    for head in range(heads):
        v = jnp.concatenate([rv_ref[head], vh_ref[head, :WINDOW]], axis=0)
        out_ref[head] = dot(weights[head * WINDOW : (head + 1) * WINDOW], v)


def first_head(far, other, part):
    half = core_bit() if far == 0 else 1 - core_bit()
    mid = pair_bit() if other == 0 else 1 - pair_bit()
    return (half * 2 + mid) * part


def mix(first, base_ref, extra_ref, high_ref, low_ref, num_ref, den_ref, edge_ref, win_ref,
        gain_ref, mixed_ref, squares):
    part, dim = base_ref.shape[0], num_ref.shape[2]
    for j in range(part):
        head = first + j
        base = unpack(base_ref[j]) if base_ref.shape[1] == SENT else base_ref[j]
        prior = base + jnp.where(core_bit() == 1, extra_ref[j], 0.0)
        phi_high, phi_low = high_ref[head], low_ref[head]
        high, low = split(prior)
        both = dot(phi_high, jnp.concatenate([high, low], axis=1))
        numer = num_ref[head] + ((both[:, dim:] + dot(phi_low, high)) + both[:, :dim])
        total = jnp.concatenate(
            [prior[TOTAL_ROW : TOTAL_ROW + 1], prior[TOTAL_ROW + 1 : TOTAL_ROW + 2, : ROWS - 128]],
            axis=1,
        )
        t_high, t_low = split(jnp.broadcast_to(total, (dim, ROWS)))
        both = dot(phi_high, jnp.concatenate([t_high, t_low], axis=0), NT)
        denom = den_ref[head] + ((both[:, dim:] + dot(phi_low, t_high, NT)) + both[:, :dim])
        window = jnp.concatenate([edge_ref[head], win_ref[head]], axis=0)
        mixed = numer / denom + window
        mixed_ref[head] = mixed * gain_ref[head]
        squares = squares + mixed * mixed
    return squares


def first_final_kernel(mine_ref, other_ref, far_ref, extra_ref, *rest):
    held, (mixed_ref, sq_ref) = rest[:-2], rest[-2:]
    part = mine_ref.shape[0]
    squares = jnp.zeros(sq_ref.shape, F32)
    squares = mix(first_head(0, 0, part), mine_ref, other_ref, *held, mixed_ref, squares)
    squares = mix(first_head(1, 0, part), far_ref, extra_ref.at[0], *held, mixed_ref, squares)
    sq_ref[...] = squares


def next_final_kernel(far, base_ref, extra_ref, *rest):
    held, (squares_ref, mixed_ref, sq_ref) = rest[:7], rest[-3:]
    first = first_head(far, 1, base_ref.shape[0])
    if far == 1:
        extra_ref = extra_ref.at[1]
    squares = mix(first, base_ref, extra_ref, *held, mixed_ref, squares_ref[...])
    if far == 0:
        sq_ref[...] = squares
    else:
        ones = jnp.ones((8, squares.shape[1]), BF16)
        high, low = split(squares)
        rest = squares - high.astype(F32) - low.astype(F32)
        sq_ref[...] = dot(ones, high, NT) + (dot(ones, low, NT) + dot(ones, rest.astype(BF16), NT))


def norm_kernel(peers, mixed_ref, sq_ref, *rest):
    out_ref = rest[-1]
    total = sq_ref[...]
    for got in rest[:peers]:
        total = total + got[...]
    scale = lax.rsqrt(total / (HEADS * DV) + NORM_EPS)
    column = jnp.transpose(scale, (1, 0))[:, :1]
    wide = jnp.broadcast_to(column, mixed_ref.shape[1:])
    out_ref[...] = jnp.swapaxes((mixed_ref[...] * wide[None]).astype(BF16), 0, 1)


def on_device(queries, keys, values, win_q, win_k, gain):
    toks, heads, dim = values.shape
    count = lax.axis_size("ctx")
    peers = lax.axis_size("head") - 1
    part = heads // 4
    core_swap = [(i, i ^ 1) for i in range(count)]
    pair_swap = [(i, i ^ 2) for i in range(count)]
    state_shape = pltpu.VMEM((part, ROWS, dim), F32)
    msg_shape = pltpu.VMEM((part, SENT, dim), BF16)
    head_wide = pltpu.VMEM((heads, toks, dim), F32)
    token_shape = pltpu.VMEM((8, 128), F32)

    def permute(x, pairs):
        return lax.ppermute(x, "ctx", pairs)

    pieces = 2 if heads % 16 == 0 else 1
    far1, values_h, keys_t, rim = call(
        first_states_kernel, "far1",
        (state_shape, pltpu.VMEM((heads, toks, dim), BF16), pltpu.VMEM((heads * DK, toks), F32),
         pltpu.VMEM((2, WINDOW, heads, dim), BF16)),
        keys, values, win_k, raw=True,
        scratch=[
            pltpu.VMEM(keys.shape, BF16),
            pltpu.VMEM((pieces, toks, heads // pieces, dim), BF16),
            pltpu.SemaphoreType.DMA((5,)),
        ],
    )
    other1 = permute(far1, core_swap)
    rim_up = permute(rim, full([(i, i + 4) for i in range(3, count - 4, 4)], count))

    def states(name, far, other, after):
        return call(functools.partial(states_kernel, far, other), name, state_shape,
                    keys_t, values_h, after)

    near1 = states("near1", 0, 1, far1)
    msg = call(chip_kernel, "chip", msg_shape, near1, other1)
    pair = call(open_kernel, "open", state_shape, permute(msg, pair_swap))
    far0 = states("far0", 1, 0, msg)
    other0 = permute(far0, core_swap)
    near0 = states("near0", 0, 0, far0)
    first_table, second_table, add_table = pair_tables(part)
    phi_high, phi_low, gain = call(
        phi_kernel, "phi",
        (pltpu.VMEM((heads, toks, ROWS), BF16),) * 2 + (pltpu.VMEM((heads, 1, dim), F32),),
        queries, first_table, second_table, add_table, gain, near0,
        scratch=[pltpu.VMEM((4, toks, part * DK), BF16)],
    )
    wq_h, wk_h, token = call(
        by_head_kernel, "by_head",
        (pltpu.VMEM((heads, toks, dim), BF16),) * 2 + (token_shape,), win_q, win_k, gain,
    )
    total, msg = call(plane_kernel, "plane", (state_shape, msg_shape), near0, other0, pair, token)
    rim, again = call(
        pick_kernel, "pick", (pltpu.VMEM(rim.shape, BF16), msg_shape), rim, rim_up, msg
    )
    rim_prev = permute(rim, [(i, i - i % 4 + (i + 1) % 4) for i in range(count)])
    groups = count // 4
    gots, limits, early = [], [], {}
    step = 1
    while step < groups:
        if step == 1:
            got = [permute(msg, full([(i, i + 4) for i in range(count - 4)], count))]
            limit = [(1, groups)]
            num, den, token = call(
                intra_kernel, "intra", (head_wide, head_wide, token_shape),
                queries, keys, values_h, rim, msg,
                scratch=[pltpu.VMEM((4, toks, part * DK), BF16)] * 2,
            )
            while 2 * step < groups:
                step *= 2
                early[step] = permute(
                    again, full([(i, i + 4 * step) for i in range(4)], count)
                )
            step = 1
        else:
            pairs = [(i, i + 4 * step) for i in range(4, count - 4 * step)]
            got = [permute(msg, full(pairs, count)), early[step]]
            limit = [(step + 1, groups), (step, step)]
        if step == 2:
            win, nears, token = call(
                window_kernel, "window",
                (pltpu.VMEM((heads, toks - WINDOW, dim), F32),
                 pltpu.VMEM((2, part, ROWS, dim), F32), token_shape),
                wq_h, wk_h, values_h, near0, near1, msg,
            )
            rim_k, rim_v, other1 = call(
                turn_kernel, "turn",
                (pltpu.VMEM((heads, WINDOW, dim), BF16),) * 2 + (state_shape,),
                rim_prev, other1, token,
            )
        gots.extend(got)
        limits.extend(limit)
        step *= 2
        if step < groups:
            keep = 2 * step < groups
            sums = call(
                functools.partial(round_kernel, limit, keep), "round",
                (msg_shape, state_shape) if keep else msg_shape, total, *got, token,
            )
            msg, total = sums if keep else (sums, None)
    mine, msg = call(
        functools.partial(before_kernel, limits), "before", (state_shape, msg_shape),
        near0, other0, pair, *gots, token,
    )
    got = permute(msg, pair_swap)
    far_mine = permute(mine, core_swap)
    far_nears = permute(nears, core_swap)
    edge = call(edge_kernel, "edge", pltpu.VMEM((heads, WINDOW, dim), F32),
                wq_h, wk_h, values_h, rim_k, rim_v, msg)

    held = (phi_high, phi_low, num, den, edge, win, gain)
    square_shape = pltpu.VMEM((toks, dim), F32)
    mixed, squares = call(
        first_final_kernel, "final0", (head_wide, square_shape),
        mine, other0, far_mine, far_nears, *held,
    )
    mine = call(open_kernel, "open", state_shape, got, squares)
    got, mine, squares = lax.optimization_barrier((got, mine, squares))
    far_got = permute(got, core_swap)
    mixed, squares = call(
        functools.partial(next_final_kernel, 0), "final1", (head_wide, square_shape),
        mine, other1, *held, mixed, squares, aliases={9: 0},
    )
    mixed, squares = call(
        functools.partial(next_final_kernel, 1), "final2",
        (head_wide, pltpu.VMEM((8, toks), F32)),
        far_got, far_nears, *held, mixed, squares, aliases={9: 0},
    )
    others = [
        lax.ppermute(squares, "head", [(i, (i + k) % (peers + 1)) for i in range(peers + 1)])
        for k in range(1, peers + 1)
    ]
    return call(
        functools.partial(norm_kernel, peers), "norm",
        jax.ShapeDtypeStruct((toks, heads, dim), BF16),
        mixed, squares, *others,
    )


def solution(mesh):
    return jax.shard_map(
        on_device,
        mesh=mesh,
        in_specs=(
            P("ctx", "head"),
            P("ctx", "head"),
            P("ctx", "head", None),
            P("ctx", "head", None),
            P("ctx", "head", None),
            P("head", None),
        ),
        out_specs=P("ctx", "head", None),
        check_vma=False,
    )
```

```python
import functools
import math

import jax
import jax.numpy as jnp
import numpy as np
from jax import lax
from jax.experimental import pallas as pl
from jax.experimental.pallas import tpu as pltpu
from jax.sharding import PartitionSpec as P

HEADS = 32
DV = 128
DK = 16
WINDOW = 64
NORM_EPS = 1e-06

ROWS = 160
TOTAL_ROW = 33
WIDE = 40
HALF_WIDE = 2 * DK
SENT = ROWS + HALF_WIDE
GROUP = 4

F32 = jnp.float32
BF16 = jnp.bfloat16
NN = (((1,), (0,)), ((), ()))
NT = (((1,), (1,)), ((), ()))


def pair_tables(heads):
    first = np.zeros((DK, ROWS), np.float32)
    second = np.zeros((DK, ROWS), np.float32)
    add = np.zeros((8, ROWS), np.float32)
    for i in range(DK):
        first[i, i] = 1.0 / 32.0
        second[i, i] = 1.0
        first[i, DK + i] = 0.25
        add[1, DK + i] = 1.0
        for d in range(1, 8):
            row = WIDE + DK * (d - 1) + i
            first[i, row] = 1.0 / 16.0
            second[(i + d) % DK, row] = 1.0
    for i in range(8):
        first[i, 152 + i] = 1.0 / 16.0
        second[i + 8, 152 + i] = 1.0
    add[0, 2 * DK] = 1.0
    add[1, 2 * DK] = 1.0
    both = []
    for one in (first, second):
        table = np.zeros((heads, heads * DK, ROWS), np.float32)
        for j in range(heads):
            table[j, j * DK : (j + 1) * DK] = one
        both.append(jnp.asarray(table, BF16))
    return both[0], both[1], jnp.asarray(add, F32)


def dot(a, b, dims=NN):
    return lax.dot_general(a, b, dims, preferred_element_type=F32)


def split(x):
    high = x.astype(BF16)
    return high, (x - high.astype(F32)).astype(BF16)


def full(pairs, count):
    sources = [i for i in range(count) if i not in {a for a, _ in pairs}]
    targets = [i for i in range(count) if i not in {b for _, b in pairs}]
    stay = sorted(set(sources) & set(targets))
    moved = zip([i for i in sources if i not in stay], [i for i in targets if i not in stay])
    return list(pairs) + [(i, i) for i in stay] + list(moved)


def plane_index():
    return lax.axis_index("ctx") >> 2


def arrived(got_refs, limits, j):
    total = None
    for ref, (least, most) in zip(got_refs, limits):
        here = plane_index()
        meant = (here >= least) & (here <= most)
        got = jnp.where(meant, unpack(ref[j]), 0.0)
        total = got if total is None else total + got
    return total


def core_bit():
    return lax.axis_index("ctx") & 1


def pair_bit():
    return (lax.axis_index("ctx") >> 1) & 1


def each(count, body):
    group = math.gcd(GROUP, count)

    def step(i, carry):
        for j in range(group):
            body(i * group + j)
        return carry

    if group == count:
        step(0, 0)
    else:
        lax.fori_loop(0, count // group, step, 0)


def pack(ref, x):
    high = x.astype(BF16).astype(F32)
    low = x[:WIDE] - high[:WIDE]
    mid = high[HALF_WIDE:WIDE] + pltpu.roll(low[HALF_WIDE:], 3, 0).astype(BF16).astype(F32)
    ref[...] = jnp.concatenate(
        [high[:HALF_WIDE], mid, high[WIDE:], low[:HALF_WIDE]], axis=0
    ).astype(BF16)


def unpack(got):
    got = got.astype(F32)
    mid = got[HALF_WIDE:WIDE]
    row = lax.broadcasted_iota(jnp.int32, mid.shape, 0)
    mid = jnp.where(row < 3, mid + pltpu.roll(mid, 5, 0), 0.0)
    return jnp.concatenate([got[:HALF_WIDE] + got[ROWS:], mid, got[WIDE:ROWS]], axis=0)


VMEM_SPEC = pl.BlockSpec(memory_space=pltpu.VMEM)
HBM_SPEC = pl.BlockSpec(memory_space=pltpu.HBM)
VMEM_LIMIT = 12 << 20
FLOPS_PER_US = 1_150_000_000
EXPECTED_US = {"phi": 1.8, "intra": 2.8, "window": 3.5, "chip": 0.1, "plane": 0.1, "open": 12.0, "pick": 60.0, "turn": 60.0}


def call(body, name, outs, *operands, scratch=(), raw=False, aliases=None):
    held = [
        pltpu.with_memory_space_constraint(x, pltpu.HBM if raw else pltpu.VMEM)
        for x in operands
    ]
    many = isinstance(outs, tuple)
    spec = HBM_SPEC if raw else VMEM_SPEC
    return pl.pallas_call(
        body,
        out_shape=outs,
        in_specs=[spec] * len(operands),
        out_specs=tuple(VMEM_SPEC for _ in outs) if many else VMEM_SPEC,
        scratch_shapes=list(scratch),
        input_output_aliases=aliases or {},
        cost_estimate=pl.CostEstimate(
            flops=int(EXPECTED_US.get(name, 1.0) * FLOPS_PER_US), bytes_accessed=0, transcendentals=0
        ),
        compiler_params=pltpu.CompilerParams(vmem_limit_bytes=VMEM_LIMIT),
        name=name,
    )(*held)


def one_state(x, v):
    toks = x.shape[1]
    ones = jnp.where(lax.broadcasted_iota(jnp.int32, (8, toks), 0) == 0, 1.0, 0.0).astype(F32)
    parts = [x * x, x, ones]
    for d in range(1, 8):
        parts.append(x * pltpu.roll(x, DK - d, 0))
    parts.append(x[:8] * x[8:])
    high, low = split(jnp.concatenate(parts, axis=0))
    full = jnp.ones((8, toks), BF16)
    total = dot(full, high, NT) + dot(full, low, NT)
    return dot(high, v) + dot(low, v), total


def put_states(out_ref, far, other, kt_ref, vh_ref):
    part = out_ref.shape[0]
    base = first_head(far, other, part)

    def one(j):
        x = kt_ref[pl.ds(pl.multiple_of((base + j) * DK, DK), DK), :]
        state, total = one_state(x, vh_ref[base + j])
        out_ref[j] = state
        out_ref[j, TOTAL_ROW : TOTAL_ROW + 1, :] = total[:1, :128]
        out_ref[j, TOTAL_ROW + 1 : TOTAL_ROW + 2, : ROWS - 128] = total[:1, 128:]

    each(part, one)


def first_states_kernel(keys_hbm, v_hbm, wk_hbm, out_ref, vh_ref, kt_ref, rim_ref,
                        keys_ref, v_ref, sems):
    toks, heads = v_hbm.shape[:2]
    pieces = v_ref.shape[0]
    size = heads // pieces
    tail = pl.ds(toks - WINDOW, WINDOW)
    firsts = [pl.multiple_of((1 - core_bit()) * size, size), pl.multiple_of(core_bit() * size, size)]
    if pieces == 1:
        firsts = [0]
    copies = [pltpu.make_async_copy(keys_hbm, keys_ref, sems.at[0])]
    for i, first in enumerate(firsts):
        copies.append(
            pltpu.make_async_copy(v_hbm.at[:, pl.ds(first, size)], v_ref.at[i], sems.at[1 + i])
        )
    copies.append(pltpu.make_async_copy(wk_hbm.at[tail], rim_ref.at[0], sems.at[3]))
    copies.append(pltpu.make_async_copy(v_hbm.at[tail], rim_ref.at[1], sems.at[4]))
    for copy in copies:
        copy.start()
    copies[0].wait()
    kt_ref[...] = jnp.transpose(keys_ref[...].astype(F32), (1, 0))
    for i, first in enumerate(firsts):
        copies[1 + i].wait()
        vh_ref[pl.ds(first, size)] = jnp.swapaxes(v_ref[i], 0, 1)
        if i == 0:
            put_states(out_ref, 1, 1, kt_ref, vh_ref)
    copies[-2].wait()
    copies[-1].wait()


def states_kernel(far, other, kt_ref, vh_ref, after_ref, out_ref):
    put_states(out_ref, far, other, kt_ref, vh_ref)


def chip_kernel(own_ref, other_ref, msg_ref):
    def one(j):
        pack(msg_ref.at[j], own_ref[j] + other_ref[j])

    each(own_ref.shape[0], one)


def open_kernel(got_ref, *rest):
    out_ref = rest[-1]

    def one(j):
        out_ref[j] = unpack(got_ref[j])

    each(got_ref.shape[0], one)


def plane_kernel(own_ref, other_ref, got_ref, *rest):
    total_ref, msg_ref = rest[-2:]

    def one(j):
        total = own_ref[j] + other_ref[j] + got_ref[j]
        total_ref[j] = total
        pack(msg_ref.at[j], total)

    each(own_ref.shape[0], one)


def round_kernel(limits, keep, total_ref, *rest):
    gots, outs = rest[: len(limits)], rest[len(limits) + 1 :]

    def one(j):
        total = total_ref[j] + arrived(gots, limits, j)
        pack(outs[0].at[j], total)
        if keep:
            outs[1][j] = total

    each(total_ref.shape[0], one)


def before_kernel(limits, own_ref, other_ref, pair_ref, *rest):
    gots, (mine_ref, msg_ref) = rest[: len(limits)], rest[-2:]
    mid = pair_bit()

    def one(j):
        before = arrived(gots, limits, j)
        mine_ref[j] = before + jnp.where(mid == 1, pair_ref[j], 0.0)
        pack(msg_ref.at[j], before + jnp.where(mid == 0, own_ref[j] + other_ref[j], 0.0))

    each(own_ref.shape[0], one)


def again_kernel(msg_ref, after_ref, again_ref):
    again_ref[...] = msg_ref[...]


def pick_kernel(rim_ref, got_ref, msg_ref, out_ref):
    last = lax.axis_index("ctx") % 4 == 3

    @pl.when(last)
    def _():
        out_ref[...] = got_ref[...]

    @pl.when(jnp.logical_not(last))
    def _():
        out_ref[...] = rim_ref[...]


def phi_kernel(q_ref, e1_ref, e2_ref, add_ref, gain_ref, after_ref,
               high_ref, low_ref, gain_out_ref, q4_ref):
    for h in range(gain_ref.shape[0]):
        gain_out_ref[h] = gain_ref[h : h + 1].astype(F32)
    part = e1_ref.shape[0]
    width = part * DK
    for r in range(4):
        q4_ref[r] = q_ref[:, r * width : (r + 1) * width]

    def one(r, carry):
        q = q4_ref[r]
        for j in range(part):
            a = dot(q, e1_ref[j]) + add_ref[0:1]
            b = dot(q, e2_ref[j]) + add_ref[1:2]
            high, low = split(a * b)
            high_ref[r * part + j] = high
            low_ref[r * part + j] = low
        return carry

    lax.fori_loop(0, 4, one, 0)


def intra_kernel(q_ref, k_ref, vh_ref, rim_ref, after_ref,
                 num_ref, den_ref, token_ref, q4_ref, k4_ref):
    token_ref[...] = jnp.zeros_like(token_ref)
    heads, toks, dim = vh_ref.shape
    part = heads // 4
    width = part * DK
    half = toks // 2
    for r in range(4):
        q4_ref[r] = q_ref[:, r * width : (r + 1) * width]
        k4_ref[r] = k_ref[:, r * width : (r + 1) * width]
    row = lax.broadcasted_iota(jnp.int32, (half, half), 0)
    col = lax.broadcasted_iota(jnp.int32, (half, half), 1)
    tri = col <= row
    lane = lax.broadcasted_iota(jnp.int32, (toks, width), 1) // DK
    ones = jnp.ones((toks, dim), BF16)

    def poly(s):
        return 1.0 + s * 0.25 + s * s * (1.0 / 32.0)

    def one(r, carry):
        q, k = q4_ref[r], k4_ref[r]
        tops, lows, rights = [], [], []
        for j in range(part):
            own = jnp.where(lane == j, q, jnp.zeros_like(q))
            tops.append(dot(own[:half], k[:half], NT))
            lows.append(dot(own[half:], k, NT))
        for j in range(part):
            head = r * part + j
            v = jnp.concatenate([vh_ref[head], ones], axis=1)
            top = jnp.where(tri, poly(tops[j]), 0.0)
            left = poly(lows[j][:, :half])
            right = jnp.where(tri, poly(lows[j][:, half:]), 0.0)
            high, low = split(top)
            both = dot(high, v[:half]) + dot(low, v[:half])
            num_ref[head, :half] = both[:, :dim]
            den_ref[head, :half] = both[:, dim:]
            high, low = split(jnp.concatenate([left, right], axis=1))
            both = dot(high, v) + dot(low, v)
            num_ref[head, half:] = both[:, :dim]
            den_ref[head, half:] = both[:, dim:]
        return carry

    lax.fori_loop(0, 4, one, 0)


def softmax_blocks(scores):
    sc = jnp.concatenate(scores, axis=0)
    expo = jnp.exp(sc - jnp.max(sc, axis=1, keepdims=True))
    return (expo / jnp.sum(expo, axis=1, keepdims=True)).astype(BF16)


def band_mask():
    row = lax.broadcasted_iota(jnp.int32, (WINDOW, 2 * WINDOW), 0)
    col = lax.broadcasted_iota(jnp.int32, (WINDOW, 2 * WINDOW), 1)
    return (col > row) & (col <= row + WINDOW), col


def by_head_kernel(wq_ref, wk_ref, after_ref, qh_ref, kh_ref, token_ref):
    token_ref[...] = jnp.zeros_like(token_ref)
    qh_ref[...] = jnp.swapaxes(wq_ref[...], 0, 1)
    kh_ref[...] = jnp.swapaxes(wk_ref[...], 0, 1)


def turn_kernel(rim_ref, other1_ref, near0_ref, near1_ref, after_ref,
                k_ref, v_ref, keep_ref, nears_ref):
    keep_ref[...] = other1_ref[...]
    nears_ref[0] = near0_ref[...]
    nears_ref[1] = near1_ref[...]
    k_ref[...] = jnp.swapaxes(rim_ref[0], 0, 1)
    v_ref[...] = jnp.swapaxes(rim_ref[1], 0, 1)


def window_kernel(qh_ref, kh_ref, vh_ref, after_ref, win_ref, token_ref):
    heads, toks, dim = vh_ref.shape
    part = heads // 4
    token_ref[...] = jnp.zeros_like(token_ref)
    band, _ = band_mask()
    blocks = toks // WINDOW - 1

    def one(r, carry):
        scores = []
        for j in range(part):
            head = r * part + j
            for b in range(blocks):
                lo = b * WINDOW
                q = qh_ref[head, lo + WINDOW : lo + 2 * WINDOW]
                sc = dot(q, kh_ref[head, lo : lo + 2 * WINDOW], NT)
                scores.append(jnp.where(band, sc / math.sqrt(dim), -1e30))
        weights = softmax_blocks(scores)
        for j in range(part):
            head = r * part + j
            for b in range(blocks):
                lo = b * WINDOW
                at = (j * blocks + b) * WINDOW
                win_ref[head, lo : lo + WINDOW] = dot(
                    weights[at : at + WINDOW], vh_ref[head, lo : lo + 2 * WINDOW]
                )
        return carry

    lax.fori_loop(0, 4, one, 0)


def edge_kernel(qh_ref, kh_ref, vh_ref, rk_ref, rv_ref, after_ref, out_ref):
    heads, _, dim = vh_ref.shape
    band, col = band_mask()
    valid = band & ((col >= WINDOW) | (lax.axis_index("ctx") > 0))

    scores = []
    for head in range(heads):
        k = jnp.concatenate([rk_ref[head], kh_ref[head, :WINDOW]], axis=0)
        sc = dot(qh_ref[head, :WINDOW], k, NT)
        scores.append(jnp.where(valid, sc / math.sqrt(dim), -1e30))
    weights = softmax_blocks(scores)
    for head in range(heads):
        v = jnp.concatenate([rv_ref[head], vh_ref[head, :WINDOW]], axis=0)
        out_ref[head] = dot(weights[head * WINDOW : (head + 1) * WINDOW], v)


def first_head(far, other, part):
    half = core_bit() if far == 0 else 1 - core_bit()
    mid = pair_bit() if other == 0 else 1 - pair_bit()
    return (half * 2 + mid) * part


def mix(first, base_ref, extra_ref, high_ref, low_ref, num_ref, den_ref, edge_ref, win_ref,
        gain_ref, mixed_ref, squares):
    part, dim = base_ref.shape[0], num_ref.shape[2]
    for j in range(part):
        head = first + j
        base = unpack(base_ref[j]) if base_ref.shape[1] == SENT else base_ref[j]
        prior = base + jnp.where(core_bit() == 1, extra_ref[j], 0.0)
        phi_high, phi_low = high_ref[head], low_ref[head]
        high, low = split(prior)
        both = dot(phi_high, jnp.concatenate([high, low], axis=1))
        numer = num_ref[head] + ((both[:, dim:] + dot(phi_low, high)) + both[:, :dim])
        total = jnp.concatenate(
            [prior[TOTAL_ROW : TOTAL_ROW + 1], prior[TOTAL_ROW + 1 : TOTAL_ROW + 2, : ROWS - 128]],
            axis=1,
        )
        t_high, t_low = split(jnp.broadcast_to(total, (dim, ROWS)))
        both = dot(phi_high, jnp.concatenate([t_high, t_low], axis=0), NT)
        denom = den_ref[head] + ((both[:, dim:] + dot(phi_low, t_high, NT)) + both[:, :dim])
        window = jnp.concatenate([edge_ref[head], win_ref[head]], axis=0)
        mixed = numer / denom + window
        mixed_ref[head] = mixed * gain_ref[head]
        squares = squares + mixed * mixed
    return squares


def first_final_kernel(mine_ref, other_ref, far_ref, extra_ref, *rest):
    held, (mixed_ref, sq_ref) = rest[:-2], rest[-2:]
    part = mine_ref.shape[0]
    squares = jnp.zeros(sq_ref.shape, F32)
    squares = mix(first_head(0, 0, part), mine_ref, other_ref, *held, mixed_ref, squares)
    squares = mix(first_head(1, 0, part), far_ref, extra_ref.at[0], *held, mixed_ref, squares)
    sq_ref[...] = squares


def next_final_kernel(far, base_ref, extra_ref, *rest):
    held, (squares_ref, mixed_ref, sq_ref) = rest[:7], rest[-3:]
    first = first_head(far, 1, base_ref.shape[0])
    if far == 1:
        extra_ref = extra_ref.at[1]
    squares = mix(first, base_ref, extra_ref, *held, mixed_ref, squares_ref[...])
    if far == 0:
        sq_ref[...] = squares
    else:
        ones = jnp.ones((8, squares.shape[1]), BF16)
        high, low = split(squares)
        rest = squares - high.astype(F32) - low.astype(F32)
        sq_ref[...] = dot(ones, high, NT) + (dot(ones, low, NT) + dot(ones, rest.astype(BF16), NT))


def norm_kernel(peers, mixed_ref, sq_ref, *rest):
    out_ref = rest[-1]
    total = sq_ref[...]
    for got in rest[:peers]:
        total = total + got[...]
    scale = lax.rsqrt(total / (HEADS * DV) + NORM_EPS)
    column = jnp.transpose(scale, (1, 0))[:, :1]
    wide = jnp.broadcast_to(column, mixed_ref.shape[1:])
    out_ref[...] = jnp.swapaxes((mixed_ref[...] * wide[None]).astype(BF16), 0, 1)


def on_device(queries, keys, values, win_q, win_k, gain):
    toks, heads, dim = values.shape
    count = lax.axis_size("ctx")
    peers = lax.axis_size("head") - 1
    part = heads // 4
    core_swap = [(i, i ^ 1) for i in range(count)]
    pair_swap = [(i, i ^ 2) for i in range(count)]
    state_shape = pltpu.VMEM((part, ROWS, dim), F32)
    msg_shape = pltpu.VMEM((part, SENT, dim), BF16)
    head_wide = pltpu.VMEM((heads, toks, dim), F32)
    token_shape = pltpu.VMEM((8, 128), F32)

    def permute(x, pairs):
        return lax.ppermute(x, "ctx", pairs)

    pieces = 2 if heads % 16 == 0 else 1
    far1, values_h, keys_t, rim = call(
        first_states_kernel, "far1",
        (state_shape, pltpu.VMEM((heads, toks, dim), BF16), pltpu.VMEM((heads * DK, toks), F32),
         pltpu.VMEM((2, WINDOW, heads, dim), BF16)),
        keys, values, win_k, raw=True,
        scratch=[
            pltpu.VMEM(keys.shape, BF16),
            pltpu.VMEM((pieces, toks, heads // pieces, dim), BF16),
            pltpu.SemaphoreType.DMA((5,)),
        ],
    )
    other1 = permute(far1, core_swap)
    rim_up = permute(rim, full([(i, i + 4) for i in range(3, count - 4, 4)], count))

    def states(name, far, other, after):
        return call(functools.partial(states_kernel, far, other), name, state_shape,
                    keys_t, values_h, after)

    near1 = states("near1", 0, 1, far1)
    msg = call(chip_kernel, "chip", msg_shape, near1, other1)
    pair = call(open_kernel, "open", state_shape, permute(msg, pair_swap))
    far0 = states("far0", 1, 0, msg)
    other0 = permute(far0, core_swap)
    near0 = states("near0", 0, 0, far0)
    far_near0, far_near1 = permute(near0, core_swap), permute(near1, core_swap)
    first_table, second_table, add_table = pair_tables(part)
    phi_high, phi_low, gain = call(
        phi_kernel, "phi",
        (pltpu.VMEM((heads, toks, ROWS), BF16),) * 2 + (pltpu.VMEM((heads, 1, dim), F32),),
        queries, first_table, second_table, add_table, gain, near0,
        scratch=[pltpu.VMEM((4, toks, part * DK), BF16)],
    )
    wq_h, wk_h, token = call(
        by_head_kernel, "by_head",
        (pltpu.VMEM((heads, toks, dim), BF16),) * 2 + (token_shape,), win_q, win_k, gain,
    )
    total, msg = call(plane_kernel, "plane", (state_shape, msg_shape), near0, other0, pair, token)
    rim = call(pick_kernel, "pick", pltpu.VMEM(rim.shape, BF16), rim, rim_up, msg)
    again = call(again_kernel, "again", msg_shape, msg, rim)
    rim_prev = permute(rim, [(i, i - i % 4 + (i + 1) % 4) for i in range(count)])
    groups = count // 4
    gots, limits, early = [], [], {}
    step = 1
    while step < groups:
        if step == 1:
            got = [permute(msg, full([(i, i + 4) for i in range(count - 4)], count))]
            limit = [(1, groups)]
            num, den, token = call(
                intra_kernel, "intra", (head_wide, head_wide, token_shape),
                queries, keys, values_h, rim, msg,
                scratch=[pltpu.VMEM((4, toks, part * DK), BF16)] * 2,
            )
            while 2 * step < groups:
                step *= 2
                early[step] = permute(
                    again, full([(i, i + 4 * step) for i in range(4)], count)
                )
            step = 1
        else:
            pairs = [(i, i + 4 * step) for i in range(4, count - 4 * step)]
            got = [permute(msg, full(pairs, count)), early[step]]
            limit = [(step + 1, groups), (step, step)]
        if step == 2:
            win, token = call(
                window_kernel, "window",
                (pltpu.VMEM((heads, toks - WINDOW, dim), F32),
                 token_shape),
                wq_h, wk_h, values_h, msg,
            )
            rim_k, rim_v, other1, far_nears = call(
                turn_kernel, "turn",
                (pltpu.VMEM((heads, WINDOW, dim), BF16),) * 2
                + (state_shape, pltpu.VMEM((2, part, ROWS, dim), F32)),
                rim_prev, other1, far_near0, far_near1, token,
            )
        gots.extend(got)
        limits.extend(limit)
        step *= 2
        if step < groups:
            keep = 2 * step < groups
            sums = call(
                functools.partial(round_kernel, limit, keep), "round",
                (msg_shape, state_shape) if keep else msg_shape, total, *got, token,
            )
            msg, total = sums if keep else (sums, None)
    mine, msg = call(
        functools.partial(before_kernel, limits), "before", (state_shape, msg_shape),
        near0, other0, pair, *gots, token,
    )
    got = permute(msg, pair_swap)
    far_mine = permute(mine, core_swap)
    edge = call(edge_kernel, "edge", pltpu.VMEM((heads, WINDOW, dim), F32),
                wq_h, wk_h, values_h, rim_k, rim_v, msg)

    held = (phi_high, phi_low, num, den, edge, win, gain)
    square_shape = pltpu.VMEM((toks, dim), F32)
    mixed, squares = call(
        first_final_kernel, "final0", (head_wide, square_shape),
        mine, other0, far_mine, far_nears, *held,
    )
    mine = call(open_kernel, "open", state_shape, got, squares)
    got, mine, squares = lax.optimization_barrier((got, mine, squares))
    far_got = permute(got, core_swap)
    mixed, squares = call(
        functools.partial(next_final_kernel, 0), "final1", (head_wide, square_shape),
        mine, other1, *held, mixed, squares, aliases={9: 0},
    )
    mixed, squares = call(
        functools.partial(next_final_kernel, 1), "final2",
        (head_wide, pltpu.VMEM((8, toks), F32)),
        far_got, far_nears, *held, mixed, squares, aliases={9: 0},
    )
    others = [
        lax.ppermute(squares, "head", [(i, (i + k) % (peers + 1)) for i in range(peers + 1)])
        for k in range(1, peers + 1)
    ]
    return call(
        functools.partial(norm_kernel, peers), "norm",
        jax.ShapeDtypeStruct((toks, heads, dim), BF16),
        mixed, squares, *others,
    )


def solution(mesh):
    return jax.shard_map(
        on_device,
        mesh=mesh,
        in_specs=(
            P("ctx", "head"),
            P("ctx", "head"),
            P("ctx", "head", None),
            P("ctx", "head", None),
            P("ctx", "head", None),
            P("head", None),
        ),
        out_specs=P("ctx", "head", None),
        check_vma=False,
    )
```

```python
import functools
import math

import jax
import jax.numpy as jnp
import numpy as np
from jax import lax
from jax.experimental import pallas as pl
from jax.experimental.pallas import tpu as pltpu
from jax.sharding import PartitionSpec as P

HEADS = 32
DV = 128
DK = 16
WINDOW = 64
NORM_EPS = 1e-06

ROWS = 160
TOTAL_ROW = 33
WIDE = 40
HALF_WIDE = 2 * DK
SENT = ROWS + HALF_WIDE
GROUP = 4

F32 = jnp.float32
BF16 = jnp.bfloat16
NN = (((1,), (0,)), ((), ()))
NT = (((1,), (1,)), ((), ()))


def pair_tables(heads):
    first = np.zeros((DK, ROWS), np.float32)
    second = np.zeros((DK, ROWS), np.float32)
    add = np.zeros((8, ROWS), np.float32)
    for i in range(DK):
        first[i, i] = 1.0 / 32.0
        second[i, i] = 1.0
        first[i, DK + i] = 0.25
        add[1, DK + i] = 1.0
        for d in range(1, 8):
            row = WIDE + DK * (d - 1) + i
            first[i, row] = 1.0 / 16.0
            second[(i + d) % DK, row] = 1.0
    for i in range(8):
        first[i, 152 + i] = 1.0 / 16.0
        second[i + 8, 152 + i] = 1.0
    add[0, 2 * DK] = 1.0
    add[1, 2 * DK] = 1.0
    both = []
    for one in (first, second):
        table = np.zeros((heads, heads * DK, ROWS), np.float32)
        for j in range(heads):
            table[j, j * DK : (j + 1) * DK] = one
        both.append(jnp.asarray(table, BF16))
    return both[0], both[1], jnp.asarray(add, F32)


def dot(a, b, dims=NN):
    return lax.dot_general(a, b, dims, preferred_element_type=F32)


def split(x):
    high = x.astype(BF16)
    return high, (x - high.astype(F32)).astype(BF16)


def full(pairs, count):
    sources = [i for i in range(count) if i not in {a for a, _ in pairs}]
    targets = [i for i in range(count) if i not in {b for _, b in pairs}]
    stay = sorted(set(sources) & set(targets))
    moved = zip([i for i in sources if i not in stay], [i for i in targets if i not in stay])
    return list(pairs) + [(i, i) for i in stay] + list(moved)


def plane_index():
    return lax.axis_index("ctx") >> 2


def arrived(got_refs, limits, j):
    total = None
    for ref, (least, most) in zip(got_refs, limits):
        here = plane_index()
        meant = (here >= least) & (here <= most)
        got = jnp.where(meant, unpack(ref[j]), 0.0)
        total = got if total is None else total + got
    return total


def core_bit():
    return lax.axis_index("ctx") & 1


def pair_bit():
    return (lax.axis_index("ctx") >> 1) & 1


def each(count, body):
    group = math.gcd(GROUP, count)

    def step(i, carry):
        for j in range(group):
            body(i * group + j)
        return carry

    if group == count:
        step(0, 0)
    else:
        lax.fori_loop(0, count // group, step, 0)


def pack(ref, x):
    high = x.astype(BF16).astype(F32)
    low = x[:WIDE] - high[:WIDE]
    mid = high[HALF_WIDE:WIDE] + pltpu.roll(low[HALF_WIDE:], 3, 0).astype(BF16).astype(F32)
    ref[...] = jnp.concatenate(
        [high[:HALF_WIDE], mid, high[WIDE:], low[:HALF_WIDE]], axis=0
    ).astype(BF16)


def unpack(got):
    got = got.astype(F32)
    mid = got[HALF_WIDE:WIDE]
    row = lax.broadcasted_iota(jnp.int32, mid.shape, 0)
    mid = jnp.where(row < 3, mid + pltpu.roll(mid, 5, 0), 0.0)
    return jnp.concatenate([got[:HALF_WIDE] + got[ROWS:], mid, got[WIDE:ROWS]], axis=0)


VMEM_SPEC = pl.BlockSpec(memory_space=pltpu.VMEM)
HBM_SPEC = pl.BlockSpec(memory_space=pltpu.HBM)
VMEM_LIMIT = 12 << 20
FLOPS_PER_US = 1_150_000_000
EXPECTED_US = {"phi": 1.8, "intra": 2.8, "window": 3.5, "chip": 0.1, "plane": 0.1, "open": 12.0, "pick": 60.0, "turn": 60.0}


def call(body, name, outs, *operands, scratch=(), raw=False, aliases=None):
    held = [
        pltpu.with_memory_space_constraint(x, pltpu.HBM if raw else pltpu.VMEM)
        for x in operands
    ]
    many = isinstance(outs, tuple)
    spec = HBM_SPEC if raw else VMEM_SPEC
    return pl.pallas_call(
        body,
        out_shape=outs,
        in_specs=[spec] * len(operands),
        out_specs=tuple(VMEM_SPEC for _ in outs) if many else VMEM_SPEC,
        scratch_shapes=list(scratch),
        input_output_aliases=aliases or {},
        cost_estimate=pl.CostEstimate(
            flops=int(EXPECTED_US.get(name, 1.0) * FLOPS_PER_US), bytes_accessed=0, transcendentals=0
        ),
        compiler_params=pltpu.CompilerParams(vmem_limit_bytes=VMEM_LIMIT),
        name=name,
    )(*held)


def one_state(x, v):
    toks = x.shape[1]
    ones = jnp.where(lax.broadcasted_iota(jnp.int32, (8, toks), 0) == 0, 1.0, 0.0).astype(F32)
    parts = [x * x, x, ones]
    for d in range(1, 8):
        parts.append(x * pltpu.roll(x, DK - d, 0))
    parts.append(x[:8] * x[8:])
    high, low = split(jnp.concatenate(parts, axis=0))
    full = jnp.ones((8, toks), BF16)
    total = dot(full, high, NT) + dot(full, low, NT)
    return dot(high, v) + dot(low, v), total


def put_states(out_ref, far, other, kt_ref, vh_ref):
    part = out_ref.shape[0]
    base = first_head(far, other, part)

    def one(j):
        x = kt_ref[pl.ds(pl.multiple_of((base + j) * DK, DK), DK), :]
        state, total = one_state(x, vh_ref[base + j])
        out_ref[j] = state
        out_ref[j, TOTAL_ROW : TOTAL_ROW + 1, :] = total[:1, :128]
        out_ref[j, TOTAL_ROW + 1 : TOTAL_ROW + 2, : ROWS - 128] = total[:1, 128:]

    each(part, one)


def first_states_kernel(keys_hbm, v_hbm, wk_hbm, out_ref, vh_ref, kt_ref, rim_ref,
                        keys_ref, v_ref, sems):
    toks, heads = v_hbm.shape[:2]
    pieces = v_ref.shape[0]
    size = heads // pieces
    tail = pl.ds(toks - WINDOW, WINDOW)
    firsts = [pl.multiple_of((1 - core_bit()) * size, size), pl.multiple_of(core_bit() * size, size)]
    if pieces == 1:
        firsts = [0]
    copies = [pltpu.make_async_copy(keys_hbm, keys_ref, sems.at[0])]
    for i, first in enumerate(firsts):
        copies.append(
            pltpu.make_async_copy(v_hbm.at[:, pl.ds(first, size)], v_ref.at[i], sems.at[1 + i])
        )
    copies.append(pltpu.make_async_copy(wk_hbm.at[tail], rim_ref.at[0], sems.at[3]))
    copies.append(pltpu.make_async_copy(v_hbm.at[tail], rim_ref.at[1], sems.at[4]))
    for copy in copies:
        copy.start()
    copies[0].wait()
    kt_ref[...] = jnp.transpose(keys_ref[...].astype(F32), (1, 0))
    for i, first in enumerate(firsts):
        copies[1 + i].wait()
        vh_ref[pl.ds(first, size)] = jnp.swapaxes(v_ref[i], 0, 1)
        if i == 0:
            put_states(out_ref, 1, 1, kt_ref, vh_ref)
    copies[-2].wait()
    copies[-1].wait()


def states_kernel(far, other, kt_ref, vh_ref, after_ref, out_ref):
    put_states(out_ref, far, other, kt_ref, vh_ref)


def chip_kernel(own_ref, other_ref, msg_ref):
    def one(j):
        pack(msg_ref.at[j], own_ref[j] + other_ref[j])

    each(own_ref.shape[0], one)


def open_kernel(got_ref, *rest):
    out_ref = rest[-1]

    def one(j):
        out_ref[j] = unpack(got_ref[j])

    each(got_ref.shape[0], one)


def plane_kernel(own_ref, other_ref, got_ref, *rest):
    total_ref, msg_ref = rest[-2:]

    def one(j):
        total = own_ref[j] + other_ref[j] + got_ref[j]
        total_ref[j] = total
        pack(msg_ref.at[j], total)

    each(own_ref.shape[0], one)


def round_kernel(limits, keep, total_ref, *rest):
    gots, outs = rest[: len(limits)], rest[len(limits) + 1 :]

    def one(j):
        total = total_ref[j] + arrived(gots, limits, j)
        pack(outs[0].at[j], total)
        if keep:
            outs[1][j] = total

    each(total_ref.shape[0], one)


def before_kernel(limits, own_ref, other_ref, pair_ref, *rest):
    gots, (mine_ref, msg_ref) = rest[: len(limits)], rest[-2:]
    mid = pair_bit()

    def one(j):
        before = arrived(gots, limits, j)
        mine_ref[j] = before + jnp.where(mid == 1, pair_ref[j], 0.0)
        pack(msg_ref.at[j], before + jnp.where(mid == 0, own_ref[j] + other_ref[j], 0.0))

    each(own_ref.shape[0], one)


def again_kernel(msg_ref, after_ref, again_ref):
    again_ref[...] = msg_ref[...]


def pick_kernel(rim_ref, got_ref, msg_ref, out_ref):
    last = lax.axis_index("ctx") % 4 == 3

    @pl.when(last)
    def _():
        out_ref[...] = got_ref[...]

    @pl.when(jnp.logical_not(last))
    def _():
        out_ref[...] = rim_ref[...]


def phi_kernel(q_ref, e1_ref, e2_ref, add_ref, gain_ref, after_ref,
               high_ref, low_ref, gain_out_ref, q4_ref):
    for h in range(gain_ref.shape[0]):
        gain_out_ref[h] = gain_ref[h : h + 1].astype(F32)
    part = e1_ref.shape[0]
    width = part * DK
    for r in range(4):
        q4_ref[r] = q_ref[:, r * width : (r + 1) * width]

    def one(r, carry):
        q = q4_ref[r]
        for j in range(part):
            a = dot(q, e1_ref[j]) + add_ref[0:1]
            b = dot(q, e2_ref[j]) + add_ref[1:2]
            high, low = split(a * b)
            high_ref[r * part + j] = high
            low_ref[r * part + j] = low
        return carry

    lax.fori_loop(0, 4, one, 0)


def intra_kernel(q_ref, k_ref, vh_ref, rim_ref, after_ref,
                 num_ref, den_ref, token_ref, q4_ref, k4_ref):
    token_ref[...] = jnp.zeros_like(token_ref)
    heads, toks, dim = vh_ref.shape
    part = heads // 4
    width = part * DK
    half = toks // 2
    for r in range(4):
        q4_ref[r] = q_ref[:, r * width : (r + 1) * width]
        k4_ref[r] = k_ref[:, r * width : (r + 1) * width]
    row = lax.broadcasted_iota(jnp.int32, (half, half), 0)
    col = lax.broadcasted_iota(jnp.int32, (half, half), 1)
    tri = col <= row
    lane = lax.broadcasted_iota(jnp.int32, (toks, width), 1) // DK
    ones = jnp.ones((toks, dim), BF16)

    def poly(s):
        return 1.0 + s * 0.25 + s * s * (1.0 / 32.0)

    def one(r, carry):
        q, k = q4_ref[r], k4_ref[r]
        tops, lows, rights = [], [], []
        for j in range(part):
            own = jnp.where(lane == j, q, jnp.zeros_like(q))
            tops.append(dot(own[:half], k[:half], NT))
            lows.append(dot(own[half:], k, NT))
        for j in range(part):
            head = r * part + j
            v = jnp.concatenate([vh_ref[head], ones], axis=1)
            top = jnp.where(tri, poly(tops[j]), 0.0)
            left = poly(lows[j][:, :half])
            right = jnp.where(tri, poly(lows[j][:, half:]), 0.0)
            high, low = split(top)
            both = dot(high, v[:half]) + dot(low, v[:half])
            num_ref[head, :half] = both[:, :dim]
            den_ref[head, :half] = both[:, dim:]
            high, low = split(jnp.concatenate([left, right], axis=1))
            both = dot(high, v) + dot(low, v)
            num_ref[head, half:] = both[:, :dim]
            den_ref[head, half:] = both[:, dim:]
        return carry

    lax.fori_loop(0, 4, one, 0)


def softmax_blocks(scores, dim):
    sc = jnp.concatenate(scores, axis=0)
    expo = jnp.exp2((sc - jnp.max(sc, axis=1, keepdims=True)) * (math.log2(math.e) / math.sqrt(dim)))
    return (expo * pl.reciprocal(jnp.sum(expo, axis=1, keepdims=True))).astype(BF16)


def band_mask():
    row = lax.broadcasted_iota(jnp.int32, (WINDOW, 2 * WINDOW), 0)
    col = lax.broadcasted_iota(jnp.int32, (WINDOW, 2 * WINDOW), 1)
    return (col > row) & (col <= row + WINDOW), col


def by_head_kernel(wq_ref, wk_ref, after_ref, qh_ref, kh_ref, token_ref):
    token_ref[...] = jnp.zeros_like(token_ref)
    qh_ref[...] = jnp.swapaxes(wq_ref[...], 0, 1)
    kh_ref[...] = jnp.swapaxes(wk_ref[...], 0, 1)


def turn_kernel(rim_ref, other1_ref, near0_ref, near1_ref, after_ref,
                k_ref, v_ref, keep_ref, nears_ref):
    keep_ref[...] = other1_ref[...]
    nears_ref[0] = near0_ref[...]
    nears_ref[1] = near1_ref[...]
    k_ref[...] = jnp.swapaxes(rim_ref[0], 0, 1)
    v_ref[...] = jnp.swapaxes(rim_ref[1], 0, 1)


def window_kernel(qh_ref, kh_ref, vh_ref, after_ref, win_ref, token_ref):
    heads, toks, dim = vh_ref.shape
    part = heads // 4
    token_ref[...] = jnp.zeros_like(token_ref)
    band, _ = band_mask()
    blocks = toks // WINDOW - 1

    def one(r, carry):
        scores = []
        for j in range(part):
            head = r * part + j
            for b in range(blocks):
                lo = b * WINDOW
                q = qh_ref[head, lo + WINDOW : lo + 2 * WINDOW]
                sc = dot(q, kh_ref[head, lo : lo + 2 * WINDOW], NT)
                scores.append(jnp.where(band, sc, -1e30))
        weights = softmax_blocks(scores, dim)
        for j in range(part):
            head = r * part + j
            for b in range(blocks):
                lo = b * WINDOW
                at = (j * blocks + b) * WINDOW
                win_ref[head, lo : lo + WINDOW] = dot(
                    weights[at : at + WINDOW], vh_ref[head, lo : lo + 2 * WINDOW]
                )
        return carry

    lax.fori_loop(0, 4, one, 0)


def edge_kernel(qh_ref, kh_ref, vh_ref, rk_ref, rv_ref, after_ref, out_ref):
    heads, _, dim = vh_ref.shape
    band, col = band_mask()
    valid = band & ((col >= WINDOW) | (lax.axis_index("ctx") > 0))

    scores = []
    for head in range(heads):
        k = jnp.concatenate([rk_ref[head], kh_ref[head, :WINDOW]], axis=0)
        sc = dot(qh_ref[head, :WINDOW], k, NT)
        scores.append(jnp.where(valid, sc, -1e30))
    weights = softmax_blocks(scores, dim)
    for head in range(heads):
        v = jnp.concatenate([rv_ref[head], vh_ref[head, :WINDOW]], axis=0)
        out_ref[head] = dot(weights[head * WINDOW : (head + 1) * WINDOW], v)


def first_head(far, other, part):
    half = core_bit() if far == 0 else 1 - core_bit()
    mid = pair_bit() if other == 0 else 1 - pair_bit()
    return (half * 2 + mid) * part


def mix(first, base_ref, extra_ref, high_ref, low_ref, num_ref, den_ref, edge_ref, win_ref,
        gain_ref, mixed_ref, squares):
    part, dim = base_ref.shape[0], num_ref.shape[2]
    for j in range(part):
        head = first + j
        base = unpack(base_ref[j]) if base_ref.shape[1] == SENT else base_ref[j]
        prior = base + jnp.where(core_bit() == 1, extra_ref[j], 0.0)
        phi_high, phi_low = high_ref[head], low_ref[head]
        high, low = split(prior)
        both = dot(phi_high, jnp.concatenate([high, low], axis=1))
        numer = num_ref[head] + ((both[:, dim:] + dot(phi_low, high)) + both[:, :dim])
        total = jnp.concatenate(
            [prior[TOTAL_ROW : TOTAL_ROW + 1], prior[TOTAL_ROW + 1 : TOTAL_ROW + 2, : ROWS - 128]],
            axis=1,
        )
        t_high, t_low = split(jnp.broadcast_to(total, (dim, ROWS)))
        both = dot(phi_high, jnp.concatenate([t_high, t_low], axis=0), NT)
        denom = den_ref[head] + ((both[:, dim:] + dot(phi_low, t_high, NT)) + both[:, :dim])
        window = jnp.concatenate([edge_ref[head], win_ref[head]], axis=0)
        mixed = numer / denom + window
        mixed_ref[head] = mixed * gain_ref[head]
        squares = squares + mixed * mixed
    return squares


def first_final_kernel(mine_ref, other_ref, far_ref, extra_ref, *rest):
    held, (mixed_ref, sq_ref) = rest[:-2], rest[-2:]
    part = mine_ref.shape[0]
    squares = jnp.zeros(sq_ref.shape, F32)
    squares = mix(first_head(0, 0, part), mine_ref, other_ref, *held, mixed_ref, squares)
    squares = mix(first_head(1, 0, part), far_ref, extra_ref.at[0], *held, mixed_ref, squares)
    sq_ref[...] = squares


def next_final_kernel(far, base_ref, extra_ref, *rest):
    held, (squares_ref, mixed_ref, sq_ref) = rest[:7], rest[-3:]
    first = first_head(far, 1, base_ref.shape[0])
    if far == 1:
        extra_ref = extra_ref.at[1]
    squares = mix(first, base_ref, extra_ref, *held, mixed_ref, squares_ref[...])
    if far == 0:
        sq_ref[...] = squares
    else:
        ones = jnp.ones((8, squares.shape[1]), BF16)
        high, low = split(squares)
        rest = squares - high.astype(F32) - low.astype(F32)
        sq_ref[...] = dot(ones, high, NT) + (dot(ones, low, NT) + dot(ones, rest.astype(BF16), NT))


def norm_kernel(peers, mixed_ref, sq_ref, *rest):
    out_ref = rest[-1]
    total = sq_ref[...]
    for got in rest[:peers]:
        total = total + got[...]
    scale = lax.rsqrt(total / (HEADS * DV) + NORM_EPS)
    column = jnp.transpose(scale, (1, 0))[:, :1]
    wide = jnp.broadcast_to(column, mixed_ref.shape[1:])
    out_ref[...] = jnp.swapaxes((mixed_ref[...] * wide[None]).astype(BF16), 0, 1)


def on_device(queries, keys, values, win_q, win_k, gain):
    toks, heads, dim = values.shape
    count = lax.axis_size("ctx")
    peers = lax.axis_size("head") - 1
    part = heads // 4
    core_swap = [(i, i ^ 1) for i in range(count)]
    pair_swap = [(i, i ^ 2) for i in range(count)]
    state_shape = pltpu.VMEM((part, ROWS, dim), F32)
    msg_shape = pltpu.VMEM((part, SENT, dim), BF16)
    head_wide = pltpu.VMEM((heads, toks, dim), F32)
    token_shape = pltpu.VMEM((8, 128), F32)

    def permute(x, pairs):
        return lax.ppermute(x, "ctx", pairs)

    pieces = 2 if heads % 16 == 0 else 1
    far1, values_h, keys_t, rim = call(
        first_states_kernel, "far1",
        (state_shape, pltpu.VMEM((heads, toks, dim), BF16), pltpu.VMEM((heads * DK, toks), F32),
         pltpu.VMEM((2, WINDOW, heads, dim), BF16)),
        keys, values, win_k, raw=True,
        scratch=[
            pltpu.VMEM(keys.shape, BF16),
            pltpu.VMEM((pieces, toks, heads // pieces, dim), BF16),
            pltpu.SemaphoreType.DMA((5,)),
        ],
    )
    other1 = permute(far1, core_swap)
    rim_up = permute(rim, full([(i, i + 4) for i in range(3, count - 4, 4)], count))

    def states(name, far, other, after):
        return call(functools.partial(states_kernel, far, other), name, state_shape,
                    keys_t, values_h, after)

    near1 = states("near1", 0, 1, far1)
    msg = call(chip_kernel, "chip", msg_shape, near1, other1)
    pair = call(open_kernel, "open", state_shape, permute(msg, pair_swap))
    far0 = states("far0", 1, 0, msg)
    other0 = permute(far0, core_swap)
    near0 = states("near0", 0, 0, far0)
    far_near0, far_near1 = permute(near0, core_swap), permute(near1, core_swap)
    first_table, second_table, add_table = pair_tables(part)
    phi_high, phi_low, gain = call(
        phi_kernel, "phi",
        (pltpu.VMEM((heads, toks, ROWS), BF16),) * 2 + (pltpu.VMEM((heads, 1, dim), F32),),
        queries, first_table, second_table, add_table, gain, near0,
        scratch=[pltpu.VMEM((4, toks, part * DK), BF16)],
    )
    wq_h, wk_h, token = call(
        by_head_kernel, "by_head",
        (pltpu.VMEM((heads, toks, dim), BF16),) * 2 + (token_shape,), win_q, win_k, gain,
    )
    total, msg = call(plane_kernel, "plane", (state_shape, msg_shape), near0, other0, pair, token)
    rim = call(pick_kernel, "pick", pltpu.VMEM(rim.shape, BF16), rim, rim_up, msg)
    again = call(again_kernel, "again", msg_shape, msg, rim)
    rim_prev = permute(rim, [(i, i - i % 4 + (i + 1) % 4) for i in range(count)])
    groups = count // 4
    gots, limits, early = [], [], {}
    step = 1
    while step < groups:
        if step == 1:
            got = [permute(msg, full([(i, i + 4) for i in range(count - 4)], count))]
            limit = [(1, groups)]
            num, den, token = call(
                intra_kernel, "intra", (head_wide, head_wide, token_shape),
                queries, keys, values_h, rim, msg,
                scratch=[pltpu.VMEM((4, toks, part * DK), BF16)] * 2,
            )
            while 2 * step < groups:
                step *= 2
                early[step] = permute(
                    again, full([(i, i + 4 * step) for i in range(4)], count)
                )
            step = 1
        else:
            pairs = [(i, i + 4 * step) for i in range(4, count - 4 * step)]
            got = [permute(msg, full(pairs, count)), early[step]]
            limit = [(step + 1, groups), (step, step)]
        if step == 2:
            win, token = call(
                window_kernel, "window",
                (pltpu.VMEM((heads, toks - WINDOW, dim), F32),
                 token_shape),
                wq_h, wk_h, values_h, msg,
            )
            rim_k, rim_v, other1, far_nears = call(
                turn_kernel, "turn",
                (pltpu.VMEM((heads, WINDOW, dim), BF16),) * 2
                + (state_shape, pltpu.VMEM((2, part, ROWS, dim), F32)),
                rim_prev, other1, far_near0, far_near1, token,
            )
        gots.extend(got)
        limits.extend(limit)
        step *= 2
        if step < groups:
            keep = 2 * step < groups
            sums = call(
                functools.partial(round_kernel, limit, keep), "round",
                (msg_shape, state_shape) if keep else msg_shape, total, *got, token,
            )
            msg, total = sums if keep else (sums, None)
    mine, msg = call(
        functools.partial(before_kernel, limits), "before", (state_shape, msg_shape),
        near0, other0, pair, *gots, token,
    )
    got = permute(msg, pair_swap)
    far_mine = permute(mine, core_swap)
    edge = call(edge_kernel, "edge", pltpu.VMEM((heads, WINDOW, dim), F32),
                wq_h, wk_h, values_h, rim_k, rim_v, msg)

    held = (phi_high, phi_low, num, den, edge, win, gain)
    square_shape = pltpu.VMEM((toks, dim), F32)
    mixed, squares = call(
        first_final_kernel, "final0", (head_wide, square_shape),
        mine, other0, far_mine, far_nears, *held,
    )
    mine = call(open_kernel, "open", state_shape, got, squares)
    got, mine, squares = lax.optimization_barrier((got, mine, squares))
    far_got = permute(got, core_swap)
    mixed, squares = call(
        functools.partial(next_final_kernel, 0), "final1", (head_wide, square_shape),
        mine, other1, *held, mixed, squares, aliases={9: 0},
    )
    mixed, squares = call(
        functools.partial(next_final_kernel, 1), "final2",
        (head_wide, pltpu.VMEM((8, toks), F32)),
        far_got, far_nears, *held, mixed, squares, aliases={9: 0},
    )
    others = [
        lax.ppermute(squares, "head", [(i, (i + k) % (peers + 1)) for i in range(peers + 1)])
        for k in range(1, peers + 1)
    ]
    return call(
        functools.partial(norm_kernel, peers), "norm",
        jax.ShapeDtypeStruct((toks, heads, dim), BF16),
        mixed, squares, *others,
    )


def solution(mesh):
    return jax.shard_map(
        on_device,
        mesh=mesh,
        in_specs=(
            P("ctx", "head"),
            P("ctx", "head"),
            P("ctx", "head", None),
            P("ctx", "head", None),
            P("ctx", "head", None),
            P("head", None),
        ),
        out_specs=P("ctx", "head", None),
        check_vma=False,
    )
```

```python
import functools
import math

import jax
import jax.numpy as jnp
import numpy as np
from jax import lax
from jax.experimental import pallas as pl
from jax.experimental.pallas import tpu as pltpu
from jax.sharding import PartitionSpec as P

HEADS = 32
DV = 128
DK = 16
WINDOW = 64
NORM_EPS = 1e-06

ROWS = 160
TOTAL_ROW = 33
WIDE = 40
HALF_WIDE = 2 * DK
SENT = ROWS + HALF_WIDE
GROUP = 4

F32 = jnp.float32
BF16 = jnp.bfloat16
NN = (((1,), (0,)), ((), ()))
NT = (((1,), (1,)), ((), ()))


def pair_tables(heads):
    first = np.zeros((DK, ROWS), np.float32)
    second = np.zeros((DK, ROWS), np.float32)
    add = np.zeros((8, ROWS), np.float32)
    for i in range(DK):
        first[i, i] = 1.0 / 32.0
        second[i, i] = 1.0
        first[i, DK + i] = 0.25
        add[1, DK + i] = 1.0
        for d in range(1, 8):
            row = WIDE + DK * (d - 1) + i
            first[i, row] = 1.0 / 16.0
            second[(i + d) % DK, row] = 1.0
    for i in range(8):
        first[i, 152 + i] = 1.0 / 16.0
        second[i + 8, 152 + i] = 1.0
    add[0, 2 * DK] = 1.0
    add[1, 2 * DK] = 1.0
    both = []
    for one in (first, second):
        table = np.zeros((heads, heads * DK, ROWS), np.float32)
        for j in range(heads):
            table[j, j * DK : (j + 1) * DK] = one
        both.append(jnp.asarray(table, BF16))
    return both[0], both[1], jnp.asarray(add, F32)


def dot(a, b, dims=NN):
    return lax.dot_general(a, b, dims, preferred_element_type=F32)


def split(x):
    high = x.astype(BF16)
    return high, (x - high.astype(F32)).astype(BF16)


def full(pairs, count):
    sources = [i for i in range(count) if i not in {a for a, _ in pairs}]
    targets = [i for i in range(count) if i not in {b for _, b in pairs}]
    stay = sorted(set(sources) & set(targets))
    moved = zip([i for i in sources if i not in stay], [i for i in targets if i not in stay])
    return list(pairs) + [(i, i) for i in stay] + list(moved)


def plane_index():
    return lax.axis_index("ctx") >> 2


def arrived(got_refs, limits, j):
    total = None
    for ref, (least, most) in zip(got_refs, limits):
        here = plane_index()
        meant = (here >= least) & (here <= most)
        got = jnp.where(meant, unpack(ref[j]), 0.0)
        total = got if total is None else total + got
    return total


def core_bit():
    return lax.axis_index("ctx") & 1


def pair_bit():
    return (lax.axis_index("ctx") >> 1) & 1


def each(count, body):
    group = math.gcd(GROUP, count)

    def step(i, carry):
        for j in range(group):
            body(i * group + j)
        return carry

    if group == count:
        step(0, 0)
    else:
        lax.fori_loop(0, count // group, step, 0)


def pack(ref, x):
    high = x.astype(BF16).astype(F32)
    low = x[:WIDE] - high[:WIDE]
    mid = high[HALF_WIDE:WIDE] + pltpu.roll(low[HALF_WIDE:], 3, 0).astype(BF16).astype(F32)
    ref[...] = jnp.concatenate(
        [high[:HALF_WIDE], mid, high[WIDE:], low[:HALF_WIDE]], axis=0
    ).astype(BF16)


def unpack(got):
    got = got.astype(F32)
    mid = got[HALF_WIDE:WIDE]
    row = lax.broadcasted_iota(jnp.int32, mid.shape, 0)
    mid = jnp.where(row < 3, mid + pltpu.roll(mid, 5, 0), 0.0)
    return jnp.concatenate([got[:HALF_WIDE] + got[ROWS:], mid, got[WIDE:ROWS]], axis=0)


VMEM_SPEC = pl.BlockSpec(memory_space=pltpu.VMEM)
HBM_SPEC = pl.BlockSpec(memory_space=pltpu.HBM)
VMEM_LIMIT = 12 << 20
FLOPS_PER_US = 1_150_000_000
EXPECTED_US = {"phi": 1.8, "intra": 2.8, "window": 3.5, "chip": 0.1, "plane": 0.1, "open": 12.0, "pick": 60.0, "turn": 60.0}


def call(body, name, outs, *operands, scratch=(), raw=False, aliases=None):
    held = [
        pltpu.with_memory_space_constraint(x, pltpu.HBM if raw else pltpu.VMEM)
        for x in operands
    ]
    many = isinstance(outs, tuple)
    spec = HBM_SPEC if raw else VMEM_SPEC
    return pl.pallas_call(
        body,
        out_shape=outs,
        in_specs=[spec] * len(operands),
        out_specs=tuple(VMEM_SPEC for _ in outs) if many else VMEM_SPEC,
        scratch_shapes=list(scratch),
        input_output_aliases=aliases or {},
        cost_estimate=pl.CostEstimate(
            flops=int(EXPECTED_US.get(name, 1.0) * FLOPS_PER_US), bytes_accessed=0, transcendentals=0
        ),
        compiler_params=pltpu.CompilerParams(vmem_limit_bytes=VMEM_LIMIT),
        name=name,
    )(*held)


def one_state(x, v):
    toks = x.shape[1]
    ones = jnp.where(lax.broadcasted_iota(jnp.int32, (8, toks), 0) == 0, 1.0, 0.0).astype(F32)
    parts = [x * x, x, ones]
    for d in range(1, 8):
        parts.append(x * pltpu.roll(x, DK - d, 0))
    parts.append(x[:8] * x[8:])
    high, low = split(jnp.concatenate(parts, axis=0))
    full = jnp.ones((8, toks), BF16)
    total = dot(full, high, NT) + dot(full, low, NT)
    return dot(high, v) + dot(low, v), total


def put_states(out_ref, far, other, kt_ref, vh_ref):
    part = out_ref.shape[0]
    base = first_head(far, other, part)

    def one(j):
        x = kt_ref[pl.ds(pl.multiple_of((base + j) * DK, DK), DK), :]
        state, total = one_state(x, vh_ref[base + j])
        out_ref[j] = state
        out_ref[j, TOTAL_ROW : TOTAL_ROW + 1, :] = total[:1, :128]
        out_ref[j, TOTAL_ROW + 1 : TOTAL_ROW + 2, : ROWS - 128] = total[:1, 128:]

    each(part, one)


def first_states_kernel(keys_hbm, v_hbm, wk_hbm, out_ref, vh_ref, kt_ref, rim_ref,
                        keys_ref, v_ref, sems):
    toks, heads = v_hbm.shape[:2]
    pieces = v_ref.shape[0]
    size = heads // pieces
    tail = pl.ds(toks - WINDOW, WINDOW)
    firsts = [pl.multiple_of((1 - core_bit()) * size, size), pl.multiple_of(core_bit() * size, size)]
    if pieces == 1:
        firsts = [0]
    copies = [pltpu.make_async_copy(keys_hbm, keys_ref, sems.at[0])]
    for i, first in enumerate(firsts):
        copies.append(
            pltpu.make_async_copy(v_hbm.at[:, pl.ds(first, size)], v_ref.at[i], sems.at[1 + i])
        )
    copies.append(pltpu.make_async_copy(wk_hbm.at[tail], rim_ref.at[0], sems.at[3]))
    copies.append(pltpu.make_async_copy(v_hbm.at[tail], rim_ref.at[1], sems.at[4]))
    for copy in copies:
        copy.start()
    copies[0].wait()
    kt_ref[...] = jnp.transpose(keys_ref[...].astype(F32), (1, 0))
    for i, first in enumerate(firsts):
        copies[1 + i].wait()
        vh_ref[pl.ds(first, size)] = jnp.swapaxes(v_ref[i], 0, 1)
        if i == 0:
            put_states(out_ref, 1, 1, kt_ref, vh_ref)
    copies[-2].wait()
    copies[-1].wait()


def states_kernel(far, other, kt_ref, vh_ref, after_ref, out_ref):
    put_states(out_ref, far, other, kt_ref, vh_ref)


def chip_kernel(own_ref, other_ref, msg_ref):
    def one(j):
        pack(msg_ref.at[j], own_ref[j] + other_ref[j])

    each(own_ref.shape[0], one)


def open_kernel(got_ref, *rest):
    out_ref = rest[-1]

    def one(j):
        out_ref[j] = unpack(got_ref[j])

    each(got_ref.shape[0], one)


def plane_kernel(own_ref, other_ref, got_ref, *rest):
    total_ref, msg_ref = rest[-2:]

    def one(j):
        total = own_ref[j] + other_ref[j] + got_ref[j]
        total_ref[j] = total
        pack(msg_ref.at[j], total)

    each(own_ref.shape[0], one)


def round_kernel(limits, keep, total_ref, *rest):
    gots, outs = rest[: len(limits)], rest[len(limits) + 1 :]

    def one(j):
        total = total_ref[j] + arrived(gots, limits, j)
        pack(outs[0].at[j], total)
        if keep:
            outs[1][j] = total

    each(total_ref.shape[0], one)


def before_kernel(limits, own_ref, other_ref, pair_ref, *rest):
    gots, (mine_ref, msg_ref) = rest[: len(limits)], rest[-2:]
    mid = pair_bit()

    def one(j):
        before = arrived(gots, limits, j)
        mine_ref[j] = before + jnp.where(mid == 1, pair_ref[j], 0.0)
        pack(msg_ref.at[j], before + jnp.where(mid == 0, own_ref[j] + other_ref[j], 0.0))

    each(own_ref.shape[0], one)


def again_kernel(msg_ref, after_ref, again_ref):
    again_ref[...] = msg_ref[...]


def pick_kernel(rim_ref, got_ref, msg_ref, out_ref):
    last = lax.axis_index("ctx") % 4 == 3

    @pl.when(last)
    def _():
        out_ref[...] = got_ref[...]

    @pl.when(jnp.logical_not(last))
    def _():
        out_ref[...] = rim_ref[...]


def phi_kernel(q_ref, e1_ref, e2_ref, add_ref, gain_ref, after_ref,
               high_ref, low_ref, gain_out_ref, q4_ref):
    for h in range(gain_ref.shape[0]):
        gain_out_ref[h] = gain_ref[h : h + 1].astype(F32)
    part = e1_ref.shape[0]
    width = part * DK
    for r in range(4):
        q4_ref[r] = q_ref[:, r * width : (r + 1) * width]

    def one(r, carry):
        q = q4_ref[r]
        for j in range(part):
            a = dot(q, e1_ref[j]) + add_ref[0:1]
            b = dot(q, e2_ref[j]) + add_ref[1:2]
            high, low = split(a * b)
            high_ref[r * part + j] = high
            low_ref[r * part + j] = low
        return carry

    lax.fori_loop(0, 4, one, 0)


def intra_kernel(q_ref, k_ref, vh_ref, rim_ref, after_ref,
                 num_ref, den_ref, token_ref, q4_ref, k4_ref):
    token_ref[...] = jnp.zeros_like(token_ref)
    heads, toks, dim = vh_ref.shape
    part = heads // 4
    width = part * DK
    half = toks // 2
    for r in range(4):
        q4_ref[r] = q_ref[:, r * width : (r + 1) * width]
        k4_ref[r] = k_ref[:, r * width : (r + 1) * width]
    row = lax.broadcasted_iota(jnp.int32, (half, half), 0)
    col = lax.broadcasted_iota(jnp.int32, (half, half), 1)
    tri = col <= row
    lane = lax.broadcasted_iota(jnp.int32, (toks, width), 1) // DK
    ones = jnp.ones((toks, dim), BF16)

    def poly(s):
        return 1.0 + s * 0.25 + s * s * (1.0 / 32.0)

    def one(r, carry):
        q, k = q4_ref[r], k4_ref[r]
        tops, lows, rights = [], [], []
        for j in range(part):
            own = jnp.where(lane == j, q, jnp.zeros_like(q))
            tops.append(dot(own[:half], k[:half], NT))
            lows.append(dot(own[half:], k, NT))
        for j in range(part):
            head = r * part + j
            v = jnp.concatenate([vh_ref[head], ones], axis=1)
            top = jnp.where(tri, poly(tops[j]), 0.0)
            left = poly(lows[j][:, :half])
            right = jnp.where(tri, poly(lows[j][:, half:]), 0.0)
            high, low = split(top)
            both = dot(high, v[:half]) + dot(low, v[:half])
            num_ref[head, :half] = both[:, :dim]
            den_ref[head, :half] = both[:, dim:]
            high, low = split(jnp.concatenate([left, right], axis=1))
            both = dot(high, v) + dot(low, v)
            num_ref[head, half:] = both[:, :dim]
            den_ref[head, half:] = both[:, dim:]
        return carry

    lax.fori_loop(0, 4, one, 0)


def softmax_blocks(scores, dim):
    sc = jnp.concatenate(scores, axis=0)
    expo = jnp.exp2((sc - jnp.max(sc, axis=1, keepdims=True)) * (math.log2(math.e) / math.sqrt(dim)))
    return (expo * pl.reciprocal(jnp.sum(expo, axis=1, keepdims=True))).astype(BF16)


def band_mask():
    row = lax.broadcasted_iota(jnp.int32, (WINDOW, 2 * WINDOW), 0)
    col = lax.broadcasted_iota(jnp.int32, (WINDOW, 2 * WINDOW), 1)
    return (col > row) & (col <= row + WINDOW), col


def by_head_kernel(wq_ref, wk_ref, after_ref, qh_ref, kh_ref, token_ref):
    token_ref[...] = jnp.zeros_like(token_ref)
    qh_ref[...] = jnp.swapaxes(wq_ref[...], 0, 1)
    kh_ref[...] = jnp.swapaxes(wk_ref[...], 0, 1)


def turn_kernel(rim_ref, other1_ref, near0_ref, near1_ref, after_ref,
                k_ref, v_ref, keep_ref, nears_ref):
    keep_ref[...] = other1_ref[...]
    nears_ref[0] = near0_ref[...]
    nears_ref[1] = near1_ref[...]
    k_ref[...] = jnp.swapaxes(rim_ref[0], 0, 1)
    v_ref[...] = jnp.swapaxes(rim_ref[1], 0, 1)


def window_kernel(qh_ref, kh_ref, vh_ref, after_ref, win_ref, token_ref):
    heads, toks, dim = vh_ref.shape
    part = heads // 4
    token_ref[...] = jnp.zeros_like(token_ref)
    band, _ = band_mask()
    blocks = toks // WINDOW - 1

    def one(r, carry):
        scores = []
        for j in range(part):
            head = r * part + j
            for b in range(blocks):
                lo = b * WINDOW
                q = qh_ref[head, lo + WINDOW : lo + 2 * WINDOW]
                sc = dot(q, kh_ref[head, lo : lo + 2 * WINDOW], NT)
                scores.append(jnp.where(band, sc, -1e30))
        weights = softmax_blocks(scores, dim)
        for j in range(part):
            head = r * part + j
            for b in range(blocks):
                lo = b * WINDOW
                at = (j * blocks + b) * WINDOW
                win_ref[head, lo : lo + WINDOW] = dot(
                    weights[at : at + WINDOW], vh_ref[head, lo : lo + 2 * WINDOW]
                )
        return carry

    lax.fori_loop(0, 4, one, 0)


def edge_kernel(qh_ref, kh_ref, vh_ref, rk_ref, rv_ref, after_ref, out_ref):
    heads, _, dim = vh_ref.shape
    band, col = band_mask()
    valid = band & ((col >= WINDOW) | (lax.axis_index("ctx") > 0))

    scores = []
    for head in range(heads):
        k = jnp.concatenate([rk_ref[head], kh_ref[head, :WINDOW]], axis=0)
        sc = dot(qh_ref[head, :WINDOW], k, NT)
        scores.append(jnp.where(valid, sc, -1e30))
    weights = softmax_blocks(scores, dim)
    for head in range(heads):
        v = jnp.concatenate([rv_ref[head], vh_ref[head, :WINDOW]], axis=0)
        out_ref[head] = dot(weights[head * WINDOW : (head + 1) * WINDOW], v)


def first_head(far, other, part):
    half = core_bit() if far == 0 else 1 - core_bit()
    mid = pair_bit() if other == 0 else 1 - pair_bit()
    return (half * 2 + mid) * part


def mix(first, base_ref, extra_ref, high_ref, low_ref, num_ref, den_ref, edge_ref, win_ref,
        gain_ref, mixed_ref, squares):
    part, dim = base_ref.shape[0], num_ref.shape[2]
    for j in range(part):
        head = first + j
        base = unpack(base_ref[j]) if base_ref.shape[1] == SENT else base_ref[j]
        prior = base + jnp.where(core_bit() == 1, extra_ref[j], 0.0)
        phi_high, phi_low = high_ref[head], low_ref[head]
        high, low = split(prior)
        both = dot(phi_high, jnp.concatenate([high, low], axis=1))
        numer = num_ref[head] + ((both[:, dim:] + dot(phi_low, high)) + both[:, :dim])
        total = jnp.concatenate(
            [prior[TOTAL_ROW : TOTAL_ROW + 1], prior[TOTAL_ROW + 1 : TOTAL_ROW + 2, : ROWS - 128]],
            axis=1,
        )
        t_high, t_low = split(jnp.broadcast_to(total, (dim, ROWS)))
        both = dot(phi_high, jnp.concatenate([t_high, t_low], axis=0), NT)
        denom = den_ref[head] + ((both[:, dim:] + dot(phi_low, t_high, NT)) + both[:, :dim])
        window = jnp.concatenate([edge_ref[head], win_ref[head]], axis=0)
        mixed = numer / denom + window
        mixed_ref[head] = mixed * gain_ref[head]
        squares = squares + mixed * mixed
    return squares


def first_final_kernel(mine_ref, other_ref, far_ref, extra_ref, *rest):
    held, (mixed_ref, sq_ref) = rest[:-2], rest[-2:]
    part = mine_ref.shape[0]
    squares = jnp.zeros(sq_ref.shape, F32)
    squares = mix(first_head(0, 0, part), mine_ref, other_ref, *held, mixed_ref, squares)
    squares = mix(first_head(1, 0, part), far_ref, extra_ref.at[0], *held, mixed_ref, squares)
    sq_ref[...] = squares


def next_final_kernel(far, base_ref, extra_ref, *rest):
    held, (squares_ref, mixed_ref, sq_ref) = rest[:7], rest[-3:]
    first = first_head(far, 1, base_ref.shape[0])
    if far == 1:
        extra_ref = extra_ref.at[1]
    squares = mix(first, base_ref, extra_ref, *held, mixed_ref, squares_ref[...])
    if far == 0:
        sq_ref[...] = squares
    else:
        ones = jnp.ones((8, squares.shape[1]), BF16)
        high, low = split(squares)
        rest = squares - high.astype(F32) - low.astype(F32)
        sq_ref[...] = dot(ones, high, NT) + (dot(ones, low, NT) + dot(ones, rest.astype(BF16), NT))


def norm_kernel(peers, mixed_ref, sq_ref, *rest):
    out_ref = rest[-1]
    total = sq_ref[...]
    for got in rest[:peers]:
        total = total + got[...]
    scale = lax.rsqrt(total / (HEADS * DV) + NORM_EPS)
    column = jnp.transpose(scale, (1, 0))[:, :1]
    wide = jnp.broadcast_to(column, mixed_ref.shape[1:])
    out_ref[...] = jnp.swapaxes((mixed_ref[...] * wide[None]).astype(BF16), 0, 1)


def on_device(queries, keys, values, win_q, win_k, gain):
    toks, heads, dim = values.shape
    count = lax.axis_size("ctx")
    peers = lax.axis_size("head") - 1
    part = heads // 4
    core_swap = [(i, i ^ 1) for i in range(count)]
    pair_swap = [(i, i ^ 2) for i in range(count)]
    state_shape = pltpu.VMEM((part, ROWS, dim), F32)
    msg_shape = pltpu.VMEM((part, SENT, dim), BF16)
    head_wide = pltpu.VMEM((heads, toks, dim), F32)
    token_shape = pltpu.VMEM((8, 128), F32)

    def permute(x, pairs):
        return lax.ppermute(x, "ctx", pairs)

    pieces = 2 if heads % 16 == 0 else 1
    far1, values_h, keys_t, rim = call(
        first_states_kernel, "far1",
        (state_shape, pltpu.VMEM((heads, toks, dim), BF16), pltpu.VMEM((heads * DK, toks), F32),
         pltpu.VMEM((2, WINDOW, heads, dim), BF16)),
        keys, values, win_k, raw=True,
        scratch=[
            pltpu.VMEM(keys.shape, BF16),
            pltpu.VMEM((pieces, toks, heads // pieces, dim), BF16),
            pltpu.SemaphoreType.DMA((5,)),
        ],
    )
    other1 = permute(far1, core_swap)
    rim_up = permute(rim, full([(i, i + 4) for i in range(3, count - 4, 4)], count))

    def states(name, far, other, after):
        return call(functools.partial(states_kernel, far, other), name, state_shape,
                    keys_t, values_h, after)

    near1 = states("near1", 0, 1, far1)
    msg = call(chip_kernel, "chip", msg_shape, near1, other1)
    pair = call(open_kernel, "open", state_shape, permute(msg, pair_swap))
    far0 = states("far0", 1, 0, msg)
    other0 = permute(far0, core_swap)
    near0 = states("near0", 0, 0, far0)
    far_near0, far_near1 = permute(near0, core_swap), permute(near1, core_swap)
    first_table, second_table, add_table = pair_tables(part)
    phi_high, phi_low, gain = call(
        phi_kernel, "phi",
        (pltpu.VMEM((heads, toks, ROWS), BF16),) * 2 + (pltpu.VMEM((heads, 1, dim), F32),),
        queries, first_table, second_table, add_table, gain, near0,
        scratch=[pltpu.VMEM((4, toks, part * DK), BF16)],
    )
    wq_h, wk_h, token = call(
        by_head_kernel, "by_head",
        (pltpu.VMEM((heads, toks, dim), BF16),) * 2 + (token_shape,), win_q, win_k, gain,
    )
    total, msg = call(plane_kernel, "plane", (state_shape, msg_shape), near0, other0, pair, token)
    rim = call(pick_kernel, "pick", pltpu.VMEM(rim.shape, BF16), rim, rim_up, msg)
    again = call(again_kernel, "again", msg_shape, msg, rim)
    rim_prev = permute(rim, [(i, i - i % 4 + (i + 1) % 4) for i in range(count)])
    groups = count // 4
    gots, limits, early = [], [], {}
    step = 1
    while step < groups:
        if step == 1:
            got = [permute(msg, full([(i, i + 4) for i in range(count - 4)], count))]
            limit = [(1, groups)]
            num, den, token = call(
                intra_kernel, "intra", (head_wide, head_wide, token_shape),
                queries, keys, values_h, rim, msg,
                scratch=[pltpu.VMEM((4, toks, part * DK), BF16)] * 2,
            )
            while 2 * step < groups:
                step *= 2
                early[step] = permute(again, [(i, i + 4 * step) for i in range(4)])
            step = 1
        else:
            pairs = [(i, i + 4 * step) for i in range(4, count - 4 * step)]
            got = [permute(msg, pairs), early[step]]
            limit = [(step + 1, groups), (step, step)]
        if step == 2:
            win, token = call(
                window_kernel, "window",
                (pltpu.VMEM((heads, toks - WINDOW, dim), F32),
                 token_shape),
                wq_h, wk_h, values_h, msg,
            )
            rim_k, rim_v, other1, far_nears = call(
                turn_kernel, "turn",
                (pltpu.VMEM((heads, WINDOW, dim), BF16),) * 2
                + (state_shape, pltpu.VMEM((2, part, ROWS, dim), F32)),
                rim_prev, other1, far_near0, far_near1, token,
            )
        gots.extend(got)
        limits.extend(limit)
        step *= 2
        if step < groups:
            keep = 2 * step < groups
            sums = call(
                functools.partial(round_kernel, limit, keep), "round",
                (msg_shape, state_shape) if keep else msg_shape, total, *got, token,
            )
            msg, total = sums if keep else (sums, None)
    mine, msg = call(
        functools.partial(before_kernel, limits), "before", (state_shape, msg_shape),
        near0, other0, pair, *gots, token,
    )
    got = permute(msg, pair_swap)
    far_mine = permute(mine, core_swap)
    edge = call(edge_kernel, "edge", pltpu.VMEM((heads, WINDOW, dim), F32),
                wq_h, wk_h, values_h, rim_k, rim_v, msg)

    held = (phi_high, phi_low, num, den, edge, win, gain)
    square_shape = pltpu.VMEM((toks, dim), F32)
    mixed, squares = call(
        first_final_kernel, "final0", (head_wide, square_shape),
        mine, other0, far_mine, far_nears, *held,
    )
    mine = call(open_kernel, "open", state_shape, got, squares)
    got, mine, squares = lax.optimization_barrier((got, mine, squares))
    far_got = permute(got, core_swap)
    mixed, squares = call(
        functools.partial(next_final_kernel, 0), "final1", (head_wide, square_shape),
        mine, other1, *held, mixed, squares, aliases={9: 0},
    )
    mixed, squares = call(
        functools.partial(next_final_kernel, 1), "final2",
        (head_wide, pltpu.VMEM((8, toks), F32)),
        far_got, far_nears, *held, mixed, squares, aliases={9: 0},
    )
    others = [
        lax.ppermute(squares, "head", [(i, (i + k) % (peers + 1)) for i in range(peers + 1)])
        for k in range(1, peers + 1)
    ]
    return call(
        functools.partial(norm_kernel, peers), "norm",
        jax.ShapeDtypeStruct((toks, heads, dim), BF16),
        mixed, squares, *others,
    )


def solution(mesh):
    return jax.shard_map(
        on_device,
        mesh=mesh,
        in_specs=(
            P("ctx", "head"),
            P("ctx", "head"),
            P("ctx", "head", None),
            P("ctx", "head", None),
            P("ctx", "head", None),
            P("head", None),
        ),
        out_specs=P("ctx", "head", None),
        check_vma=False,
    )
```
